32 devices in a mesh: wide: 8 (over y, x, core), narrow: 4 (over z).
Axes of the slice: x: 2, y: 2, z: 4, core: 2. Of those that a mesh axis runs over, the one named last changes fastest.
Arguments:
- tokens: bfloat16 [16, 1024, 768], P('wide', 'narrow'), may hold values from -6 to 6
- step_ids: int32 [16], P('wide'), may hold values from 0 to 999
- prefix: int32 [16], P('wide'), may hold values from 1 to 1024, as said below
- keep_bits: int32 [16, 1024], P('wide'), may hold values 0 or 1
- ada_weight: bfloat16 [4608, 128], replicated, may hold values from -0.5 to 0.5
- ada_bias: float32 [4608], replicated, may hold values from -3 to 3
- norm1_gain: float32 [768], replicated, may hold values from 0.5 to 1.5
- qkv_weight: bfloat16 [768, 2304], replicated, may hold values from -0.21875 to 0.21875
- out_weight: bfloat16 [768, 768], replicated, may hold values from -6 to 6
- norm2_gain: float32 [768], replicated, may hold values from 0.5 to 1.5
- up_weight: bfloat16 [768, 3072], replicated, may hold values from -0.21875 to 0.21875
- up_bias: float32 [3072], replicated, may hold values from -3 to 3
- down_weight: bfloat16 [3072, 768], replicated, may hold values from -0.21875 to 0.21875
- down_bias: float32 [768], replicated, may hold values from -3 to 3
- cotangent: bfloat16 [16, 1024, 768], P('wide', 'narrow'), may hold values from -6 to 6
Outputs:
- out_tokens: bfloat16 [16, 1024, 768], P('wide', 'narrow')
- input_grad: bfloat16 [16, 1024, 768], P('wide', 'narrow')
- ada_weight_grad: float32 [4608, 128], replicated
- ada_bias_grad: float32 [4608], replicated
- norm1_gain_grad: float32 [768], replicated
- qkv_weight_grad: float32 [768, 2304], replicated
- out_weight_grad: float32 [768, 768], replicated
- norm2_gain_grad: float32 [768], replicated
- up_weight_grad: float32 [768, 3072], replicated
- up_bias_grad: float32 [3072], replicated
- down_weight_grad: float32 [3072, 768], replicated
- down_bias_grad: float32 [768], replicated
The draws below stay inside these ranges and needn't reach their ends.
Inputs may be any that keep to these rules, and one draw needn't show every extreme that they name: Every prefix keeps at least the first position visible; of the 2 consecutive sequences of each index of wide, one has the whole length 1024 as prefix.
All inputs are finite; a program needn't handle non-finite values. No bound on the sum of `keep_bits` on one device may be relied on, other than what follows from the above.
Results may differ from the reference program's by a relative error of at most 0.015.
Values may be sent and summed in bfloat16 or wider, within the bound.
A program may use at most 192 MiB of HBM per device.

```python
import math
import jax
import jax.numpy as jnp
from jax import lax

D = 768
HEADS = 12
HEAD = 64
FF = 3072
TEMB = 128
LEN = 1024
GROUP_SEQ = 2
SEQS = 16


def draw_prefix(key, part):
    first_key, second_key = jax.random.split(jax.random.fold_in(key, 17))
    lengths = jax.random.randint(first_key, (SEQS,), 1, LEN + 1)
    chosen = jax.random.randint(second_key, (SEQS // GROUP_SEQ,), 0, GROUP_SEQ)
    placed = jnp.arange(SEQS, dtype=jnp.int32) % GROUP_SEQ
    marked = placed == jnp.repeat(chosen, GROUP_SEQ, total_repeat_length=SEQS)
    return jnp.where(marked, LEN, lengths).astype(jnp.int32)


def touch_ends(drawn, rng, least, largest):
    dims = drawn.shape
    place = [jax.random.randint(jax.random.fold_in(rng, axis), (), 0, dims[axis]) for axis in range(len(dims))]
    drawn = drawn.at[tuple(place)].set(least)
    longest = dims.index(max(dims))
    place[longest] = (place[longest] + 1) % dims[longest]
    return drawn.at[tuple(place)].set(largest)


def block_scale(key, dims, shards, smallest, top_value):
    gain = 1.0
    for axis_at, shards_of in shards:
        heights = jax.random.uniform(jax.random.fold_in(jax.random.fold_in(key, 6), axis_at), (shards_of,), jnp.float32, smallest / len(shards), top_value / len(shards))
        gain = gain * jnp.repeat(jnp.exp(heights), dims[axis_at] // shards_of).reshape((-1,) + (1,) * (len(dims) - 1 - axis_at))
    return gain


def noise(own_key, shape, scale, bound, cuts=(), held_as=jnp.bfloat16):
    drawn = jax.random.normal(own_key, shape, jnp.float32) * scale
    if len(cuts) > 0:
        drawn = block_scale(own_key, shape, cuts, -0.22, 0.18) * drawn
    return jnp.clip(drawn, min=-bound, max=bound).astype(held_as)


def setup_inputs(seed: int = 0) -> dict:
    splits = jax.random.split(jax.random.key(seed), 16)
    tokens = noise(splits[0], (SEQS, LEN, D), 1.0, 6.0, ((0, 8), (1, 4)))
    step_ids = touch_ends(jax.random.randint(splits[1], (SEQS,), 0, 1000), jax.random.fold_in(splits[1], 1), 0, 999).astype(jnp.int32)
    prefix = draw_prefix(jax.random.fold_in(splits[15], 71), 0)
    keep_bits = touch_ends((jax.random.randint(splits[3], (SEQS, LEN), 0, 2) < 1).astype(jnp.int32), jax.random.fold_in(splits[3], 1), 0, 1)
    ada_weight = noise(splits[4], (6 * D, TEMB), TEMB ** -0.5, 0.5)
    ada_bias = noise(splits[5], (6 * D,), 0.5, 3.0, (), jnp.float32)
    norm1_gain = jnp.clip(1.0 + 0.1 * jax.random.normal(splits[6], (D,), jnp.float32), 0.5, 1.5)
    qkv_weight = noise(splits[7], (D, 3 * D), D ** -0.5, 0.21875)
    out_weight = noise(splits[8], (D, D), (max(1, 2 * D // LEN)) ** -0.5, 6.0)
    norm2_gain = jnp.clip(1.0 + 0.1 * jax.random.normal(splits[9], (D,), jnp.float32), 0.5, 1.5)
    up_weight = noise(splits[10], (D, FF), D ** -0.5, 0.21875)
    up_bias = noise(splits[11], (FF,), 0.5, 3.0, (), jnp.float32)
    down_weight = noise(splits[12], (FF, D), (FF // 4) ** -0.5, 0.21875)
    down_bias = noise(splits[13], (D,), 0.5, 3.0, (), jnp.float32)
    cotangent = noise(splits[14], (SEQS, LEN, D), 1.0, 6.0, ((0, 8), (1, 4)))
    return {"tokens": tokens, "step_ids": step_ids, "prefix": prefix, "keep_bits": keep_bits, "ada_weight": ada_weight, "ada_bias": ada_bias, "norm1_gain": norm1_gain, "qkv_weight": qkv_weight, "out_weight": out_weight, "norm2_gain": norm2_gain, "up_weight": up_weight, "up_bias": up_bias, "down_weight": down_weight, "down_bias": down_bias, "cotangent": cotangent}


@jax.custom_vjp
def low(v):
    return lax.optimization_barrier(v.astype(jnp.bfloat16)).astype(jnp.float32)

@jax.custom_vjp
def low_back(v):
    return v

def low_keep(v):
    return (low(v), None)

def low_pass(kept, grad):
    return (grad,)

def back_keep(v):
    return (v, None)

def back_low(kept, grad):
    return (low(grad),)
low.defvjp(low_keep, low_pass)
low_back.defvjp(back_keep, back_low)
norm_epsilon = 1e-05
gelu_coeff = 0.7978845608028654
masked_score = -1e+30

def matmul(former, latter):
    return jnp.dot(former, latter, precision=lax.Precision.HIGHEST, preferred_element_type=jnp.float32)

def time_embed(step_ids):
    halfway = TEMB // 2
    frequency = jnp.exp(jnp.arange(halfway, dtype=jnp.float32) * (-math.log(10000.0) / halfway))
    angles = step_ids.astype(jnp.float32)[:, None] * frequency[None, :]
    return jnp.concatenate([jnp.cos(angles), jnp.sin(angles)], axis=-1)

def rope_tables(positions):
    halfway = HEAD // 2
    inverse = jnp.exp(jnp.arange(halfway, dtype=jnp.float32) * (-2.0 * math.log(10000.0) / HEAD))
    angles = positions[:, None] * inverse[None, :]
    return (jnp.cos(angles), jnp.sin(angles))

def rotate(values, cosine_rows, sine_rows):
    halfway = values.shape[-1] // 2
    former = values[..., :halfway]
    latter = values[..., halfway:]
    cos_wide = cosine_rows[:, None, :]
    sin_wide = sine_rows[:, None, :]
    return jnp.concatenate([former * cos_wide - latter * sin_wide, latter * cos_wide + former * sin_wide], axis=-1)

def layer_norm(values, scaling):
    center = values - lax.optimization_barrier(jnp.mean(values, axis=-1, keepdims=True))
    spread = lax.optimization_barrier(jnp.mean(center * center, axis=-1, keepdims=True))
    return center * lax.rsqrt(spread + norm_epsilon) * scaling

def gelu_tanh(values):
    inner_arg = gelu_coeff * (values + 0.044715 * values * values * values)
    return 0.5 * values * (1.0 + jnp.tanh(inner_arg))

def attend_one(carried):
    queries, key_rows, value_rows, visible = carried
    scores = jnp.einsum('qhe,khe->hqk', queries, key_rows, precision=lax.Precision.HIGHEST, preferred_element_type=jnp.float32) * HEAD ** (-0.5)
    scores = low_back(scores)
    allowed = visible[None, None, :]
    masked = jnp.where(allowed, scores, masked_score)
    highest = lax.optimization_barrier(jnp.max(masked, axis=-1, keepdims=True))
    log_total = highest + jnp.log(lax.optimization_barrier(jnp.sum(jnp.exp(masked - highest), axis=-1, keepdims=True)))
    weights = low(jnp.where(allowed, jnp.exp(masked - log_total), 0.0))
    return jnp.einsum('hqk,khe->qhe', weights, value_rows, precision=lax.Precision.HIGHEST, preferred_element_type=jnp.float32)

def reference(tokens, step_ids, prefix, keep_bits, ada_weight, ada_bias, norm1_gain, qkv_weight, out_weight, norm2_gain, up_weight, up_bias, down_weight, down_bias, cotangent):
    cosine_rows, sine_rows = rope_tables(jnp.arange(LEN).astype(jnp.float32))
    visible = (jnp.arange(LEN, dtype=jnp.int32)[None, :] < prefix[:, None]) | (keep_bits == 1)
    condition = jax.nn.silu(time_embed(step_ids))
    params = (ada_weight.astype(jnp.float32), ada_bias.astype(jnp.float32), norm1_gain.astype(jnp.float32), qkv_weight.astype(jnp.float32), out_weight.astype(jnp.float32), norm2_gain.astype(jnp.float32), up_weight.astype(jnp.float32), up_bias.astype(jnp.float32), down_weight.astype(jnp.float32), down_bias.astype(jnp.float32))

    def forward(weights, inputs):
        ada_matrix, ada_offset, first_gain, qkv_matrix, out_matrix, second_gain, up_matrix, up_offset, down_matrix, down_offset = weights
        modulation = matmul(condition, ada_matrix.T) + ada_offset

        def group_step(carried):
            group_tokens, group_mod, group_visible = carried
            shift_one, scale_one, gate_one, shift_two, scale_two, gate_two = jnp.split(group_mod[:, None, :], 6, axis=-1)
            normed = low(layer_norm(group_tokens, first_gain) * (1.0 + scale_one) + shift_one)
            projected = low_back(matmul(normed, qkv_matrix))
            shaped = projected.reshape(GROUP_SEQ, LEN, 3, HEADS, HEAD)
            queries = low(rotate(shaped[:, :, 0], cosine_rows, sine_rows))
            key_rows = low(rotate(shaped[:, :, 1], cosine_rows, sine_rows))
            value_rows = low(shaped[:, :, 2])
            attended = lax.map(jax.checkpoint(attend_one), (queries, key_rows, value_rows, group_visible))
            attended = low(low_back(attended.reshape(GROUP_SEQ, LEN, D)))
            branch_one = low_back(matmul(attended, out_matrix))
            middle = group_tokens + gate_one * branch_one
            normed_two = low(layer_norm(middle, second_gain) * (1.0 + scale_two) + shift_two)
            hidden = low_back(matmul(normed_two, up_matrix) + up_offset)
            active = low(gelu_tanh(hidden))
            branch_two = low_back(matmul(active, down_matrix) + down_offset)
            return middle + gate_two * branch_two
        grouped_tokens = inputs.reshape(SEQS // GROUP_SEQ, GROUP_SEQ, LEN, D)
        grouped_mod = modulation.reshape(SEQS // GROUP_SEQ, GROUP_SEQ, 6 * D)
        grouped_visible = visible.reshape(SEQS // GROUP_SEQ, GROUP_SEQ, LEN)
        outputs = lax.map(jax.checkpoint(group_step), (grouped_tokens, grouped_mod, grouped_visible))
        return outputs.reshape(SEQS, LEN, D)
    result, pullback = jax.vjp(forward, params, tokens.astype(jnp.float32))
    param_grads, input_grad = pullback(cotangent.astype(jnp.float32))
    return (result.astype(jnp.bfloat16), input_grad.astype(jnp.bfloat16), param_grads[0], param_grads[1], param_grads[2], param_grads[3], param_grads[4], param_grads[5], param_grads[6], param_grads[7], param_grads[8], param_grads[9])
```

```python
import functools
import math

import jax
import jax.numpy as jnp
from jax import lax
from jax.experimental import pallas as pl
from jax.experimental.pallas import tpu as pltpu
from jax.sharding import PartitionSpec as P

HEAD = 64
TEMB = 128
MESH = pl.DeviceIdType.MESH
BF = jnp.bfloat16
F32 = jnp.float32

norm_epsilon = 1e-05
gelu_coeff = 0.7978845608028654
masked_score = -1e30


def time_embed(step_ids):
    halfway = TEMB // 2
    frequency = jnp.exp(jnp.arange(halfway, dtype=F32) * (-math.log(10000.0) / halfway))
    angles = step_ids.astype(F32)[:, None] * frequency[None, :]
    return jnp.concatenate([jnp.cos(angles), jnp.sin(angles)], axis=-1)


def rope_tables(positions):
    halfway = HEAD // 2
    inverse = jnp.exp(jnp.arange(halfway, dtype=F32) * (-2.0 * math.log(10000.0) / HEAD))
    angles = positions[:, None] * inverse[None, :]
    return (jnp.cos(angles), jnp.sin(angles))


def rotate(values, cosine_rows, sine_rows, sign):
    former, latter = jnp.split(values, 2, axis=-1)
    cos_wide = cosine_rows[:, None, :]
    sin_wide = sine_rows[:, None, :] * sign
    return jnp.concatenate(
        [former * cos_wide - latter * sin_wide, latter * cos_wide + former * sin_wide], axis=-1
    )


def layer_norm(values, scaling):
    center = values - jnp.mean(values, axis=-1, keepdims=True)
    spread = jnp.mean(center * center, axis=-1, keepdims=True)
    return center * lax.rsqrt(spread + norm_epsilon) * scaling


def modulate(values, scaling, shift_rows, scale_rows):
    return layer_norm(values, scaling) * (1.0 + scale_rows) + shift_rows


def gelu_tanh(values):
    inner_arg = gelu_coeff * (values + 0.044715 * values * values * values)
    return 0.5 * values * (1.0 + jnp.tanh(inner_arg))


def dot(former, latter, dims):
    return lax.dot_general(former, latter, (dims, ((), ())), preferred_element_type=F32)


def attend_kernel(q_ref, ka_ref, va_ref, kb_ref, vb_ref, ba_ref, bb_ref, o_ref, lse_ref):
    count = q_ref.shape[0]
    copies = count // 128
    lane = lax.broadcasted_iota(jnp.int32, (1, 128), 1)
    q = q_ref[...]
    va_t = va_ref[...].T
    vb_t = vb_ref[...].T
    for h in range(2):
        qm = jnp.where((lane // HEAD) == h, q, jnp.zeros_like(q))
        sa = dot(ka_ref[...], qm, ((1,), (1,))) + jnp.concatenate([ba_ref[...]] * copies, axis=1)
        sb = dot(kb_ref[...], qm, ((1,), (1,))) + jnp.concatenate([bb_ref[...]] * copies, axis=1)
        top = jnp.maximum(jnp.max(sa, axis=0, keepdims=True), jnp.max(sb, axis=0, keepdims=True))
        pa = jnp.exp(sa - top)
        pb = jnp.exp(sb - top)
        total = jnp.sum(pa, axis=0, keepdims=True) + jnp.sum(pb, axis=0, keepdims=True)
        rows = slice(h * HEAD, (h + 1) * HEAD)
        out = dot(va_t[rows], pa.astype(BF), ((1,), (0,))) + dot(
            vb_t[rows], pb.astype(BF), ((1,), (0,))
        )
        o_ref[rows, :] = (out / total).astype(BF)
        lse_ref[0, h : h + 1, :] = top + jnp.log(total)


def attend(q, ka, va, kb, vb, bias_a, bias_b):
    count, width = q.shape
    pairs = width // 128
    col = pl.BlockSpec((count, 128), lambda p: (0, p))
    fixed = pl.BlockSpec((count, 128), lambda p: (0, 0))
    return pl.pallas_call(
        attend_kernel,
        grid=(pairs,),
        in_specs=[col] * 5 + [fixed] * 2,
        out_specs=[
            pl.BlockSpec((128, count), lambda p: (p, 0)),
            pl.BlockSpec((1, 8, count), lambda p: (p, 0, 0)),
        ],
        out_shape=[
            jax.ShapeDtypeStruct((width, count), BF),
            jax.ShapeDtypeStruct((pairs, 8, count), F32),
        ],
        compiler_params=pltpu.CompilerParams(vmem_limit_bytes=48 << 20),
        name="attend",
    )(q, ka, va, kb, vb, bias_a, bias_b)


def attend_back_kernel(
    q_ref, ka_ref, va_ref, kb_ref, vb_ref, ba_ref, bb_ref, o_ref, lse_ref, do_ref,
    dq_ref, dka_ref, dva_ref, dkb_ref, dvb_ref,
):
    count = q_ref.shape[0]
    copies = count // 128
    lane = lax.broadcasted_iota(jnp.int32, (1, 128), 1)
    q = q_ref[...]
    do = do_ref[...]
    do_t = do.astype(F32).T
    prod = o_ref[...].astype(F32) * do_t
    dq_parts = []
    for h in range(2):
        rows = slice(h * HEAD, (h + 1) * HEAD)
        picked = (lane // HEAD) == h
        qm = jnp.where(picked, q, jnp.zeros_like(q))
        dom = jnp.where(picked, do, jnp.zeros_like(do))
        delta = jnp.sum(prod[rows], axis=0, keepdims=True)
        lse = lse_ref[0, h : h + 1, :]
        dq_t = None
        for k_ref, v_ref, b_ref, dk_ref, dv_ref in (
            (ka_ref, va_ref, ba_ref, dka_ref, dva_ref),
            (kb_ref, vb_ref, bb_ref, dkb_ref, dvb_ref),
        ):
            k = k_ref[...]
            s = dot(k, qm, ((1,), (1,))) + jnp.concatenate([b_ref[...]] * copies, axis=1)
            p = jnp.exp(s - lse)
            dv = dot(p.astype(BF), dom, ((1,), (0,)))
            dp = dot(v_ref[...], dom, ((1,), (1,)))
            ds = (p * (dp - delta)).astype(BF)
            dk = dot(ds, qm, ((1,), (0,)))
            part = dot(k.T[rows], ds, ((1,), (0,)))
            dq_t = part if dq_t is None else dq_t + part
            if h == 0:
                dk_ref[...] = dk.astype(dk_ref.dtype)
                dv_ref[...] = dv.astype(dv_ref.dtype)
            else:
                dk_ref[...] = dk_ref[...] + dk.astype(dk_ref.dtype)
                dv_ref[...] = dv_ref[...] + dv.astype(dv_ref.dtype)
        dq_parts.append(dq_t)
    dq_ref[...] = (jnp.concatenate(dq_parts, axis=0) * (HEAD**-0.5)).T


def attend_back(q, ka, va, kb, vb, bias_a, bias_b, o_t, lse, do):
    count, width = q.shape
    pairs = width // 128
    col = pl.BlockSpec((count, 128), lambda p: (0, p))
    fixed = pl.BlockSpec((count, 128), lambda p: (0, 0))
    full = jax.ShapeDtypeStruct((count, width), F32)
    half = jax.ShapeDtypeStruct((count, width), BF)
    return pl.pallas_call(
        attend_back_kernel,
        grid=(pairs,),
        in_specs=[col] * 5
        + [fixed] * 2
        + [
            pl.BlockSpec((128, count), lambda p: (p, 0)),
            pl.BlockSpec((1, 8, count), lambda p: (p, 0, 0)),
            col,
        ],
        out_specs=[col] * 5,
        out_shape=[full, full, full, half, half],
        compiler_params=pltpu.CompilerParams(vmem_limit_bytes=48 << 20),
        name="attend_back",
    )(q, ka, va, kb, vb, bias_a, bias_b, o_t, lse, do)


def reduce_kernel(
    wide_size, ring,
    big_ref, small_ref, out_ref, sout_ref,
    acc, sacc, core_in, score_in, bit_in, sbit_in, ring_in, sring_in,
    copy_sem, send_sem, recv_sem, ring_send, ring_recv, gather_send, gather_recv,
):
    chunks, pieces = big_ref.shape[:2]
    nbits = (wide_size // 2).bit_length() - 1
    wide = lax.axis_index("wide")
    here = lax.axis_index("narrow")
    core = lax.rem(wide, 2)
    core_peer = (wide + 1 - 2 * core, here)
    bits = [lax.rem(wide // (2 << b), 2) for b in range(nbits)]
    bit_peers = [wide + (1 - 2 * bits[b]) * (2 << b) for b in range(nbits)]
    ring_peers = [(wide, lax.rem(here + d, ring)) for d in range(1, ring)]

    barrier = pltpu.get_barrier_semaphore()
    for peer in [core_peer] + [(w, here) for w in bit_peers] + ring_peers:
        pl.semaphore_signal(barrier, inc=1, device_id=peer, device_id_type=MESH)
    pl.semaphore_wait(barrier, 1 + nbits + ring - 1)

    def plan(parity):
        low = 0
        size = pieces
        steps = []
        for i in range(nbits):
            up, down = i, nbits - 1 - i
            bit = bits[up] + parity * (bits[down] - bits[up])
            peer = bit_peers[up] + parity * (bit_peers[down] - bit_peers[up])
            size //= 2
            before = low
            low = low + bit * size
            steps.append((before + (1 - bit) * size, low, size, (peer, here)))
        return steps, low

    def stage(step, chunk, parity, sem, big, out, total, core_slot, bit_slots, ring_slot):
        cols = out.shape[-1] // 2
        mine = pl.ds(pl.multiple_of(core * cols, 128), cols)
        other = pl.ds(pl.multiple_of((1 - core) * cols, 128), cols)
        steps, low = plan(parity)
        final = low + here

        def remote(src, dst, index, peer):
            return pltpu.make_async_remote_copy(
                src_ref=src,
                dst_ref=dst,
                send_sem=send_sem.at[index, sem],
                recv_sem=recv_sem.at[index, sem],
                device_id=peer,
                device_id_type=MESH,
            )

        def core_copy():
            return remote(big.at[:, :, other], core_slot, 0, core_peer)

        def own_copy():
            return pltpu.make_async_copy(big.at[:, :, mine], total, copy_sem.at[sem])

        def bit_copy(i):
            away, _, size, peer = steps[i]
            return remote(total.at[pl.ds(away, size)], bit_slots[i], 1 + i, peer)

        def ring_copy(d):
            target = lax.rem(here + d, ring)
            return pltpu.make_async_remote_copy(
                src_ref=total.at[low + target],
                dst_ref=ring_slot.at[d - 1],
                send_sem=ring_send.at[d - 1, sem],
                recv_sem=ring_recv.at[d - 1, sem],
                device_id=(wide, target),
                device_id_type=MESH,
            )

        def spread_copy(d):
            target = lax.rem(here + d, ring)
            place = out.at[final, :, mine]
            return pltpu.make_async_remote_copy(
                src_ref=place,
                dst_ref=place,
                send_sem=gather_send.at[d - 1, sem],
                recv_sem=gather_recv.at[d - 1, sem],
                device_id=(wide, target),
                device_id_type=MESH,
            )

        def back_copy(i):
            _, keep, size, peer = steps[i]
            place = out.at[pl.ds(keep, size), :, mine]
            return remote(place, place, 1 + nbits + i, peer)

        def core_back():
            place = out.at[:, :, mine]
            return remote(place, place, 1 + 2 * nbits, core_peer)

        def add(start, size, slot):
            @pl.loop(0, size)
            def _(j):
                total[start + j] = (total[start + j].astype(F32) + slot[j].astype(F32)).astype(BF)

        if step == 0:
            core_copy().start()
            own_copy().start()
        elif step == 1:
            own_copy().wait()
            core_copy().wait()
            add(0, pieces, core_slot)
            bit_copy(0).start()
        elif step <= nbits:
            bit_copy(step - 2).wait()
            add(steps[step - 2][1], steps[step - 2][2], bit_slots[step - 2])
            bit_copy(step - 1).start()
        elif step == nbits + 1:
            bit_copy(nbits - 1).wait()
            add(steps[nbits - 1][1], steps[nbits - 1][2], bit_slots[nbits - 1])
            for d in range(1, ring):
                ring_copy(d).start()
        elif step == nbits + 2:
            for d in range(1, ring):
                ring_copy(d).wait()
            value = total[final].astype(F32)
            for d in range(1, ring):
                value = value + ring_slot[d - 1].astype(F32)
            out[final, :, mine] = value.astype(BF)
            for d in range(1, ring):
                spread_copy(d).start()
        elif step == nbits + 3:
            for d in range(1, ring):
                spread_copy(d).wait()
            back_copy(nbits - 1).start()
        elif step <= 2 * nbits + 2:
            i = nbits - 1 - (step - nbits - 3)
            back_copy(i + 1).wait()
            back_copy(i).start()
        elif step == 2 * nbits + 3:
            back_copy(0).wait()
            core_back().start()
        else:
            core_back().wait()

    last = 2 * nbits + 4

    @pl.loop(0, chunks + 1 + last)
    def _(tick):
        for step in range(last, -1, -1):
            chunk = tick - step

            @pl.when((chunk >= 0) & (chunk < chunks))
            def _():
                stage(
                    step, chunk, lax.rem(chunk, 2), chunk,
                    big_ref.at[chunk], out_ref.at[chunk], acc.at[chunk], core_in.at[chunk],
                    [ref.at[chunk] for ref in bit_in], ring_in.at[chunk],
                )

            @pl.when(chunk == chunks)
            def _():
                stage(
                    step, chunks, 0, chunks,
                    small_ref, sout_ref, sacc, score_in, sbit_in, sring_in,
                )


def reduce_all(big, small, wide_size, ring):
    chunks, pieces, rows, cols = big.shape
    srows = small.shape[1]
    half = cols // 2
    nbits = (wide_size // 2).bit_length() - 1
    sizes = [pieces >> (i + 1) for i in range(nbits)]
    any_space = pl.BlockSpec(memory_space=pl.ANY)
    vmem = pl.BlockSpec(memory_space=pltpu.VMEM)
    dma = pltpu.SemaphoreType.DMA
    return pl.pallas_call(
        functools.partial(reduce_kernel, wide_size, ring),
        in_specs=[any_space, any_space],
        out_specs=[vmem, vmem],
        out_shape=[
            jax.ShapeDtypeStruct(big.shape, BF),
            jax.ShapeDtypeStruct(small.shape, BF),
        ],
        scratch_shapes=[
            pltpu.VMEM((chunks, pieces, rows, half), BF),
            pltpu.VMEM((pieces, srows, half), BF),
            pltpu.VMEM((chunks, pieces, rows, half), BF),
            pltpu.VMEM((pieces, srows, half), BF),
            [pltpu.VMEM((chunks, n, rows, half), BF) for n in sizes],
            [pltpu.VMEM((n, srows, half), BF) for n in sizes],
            pltpu.VMEM((chunks, ring - 1, rows, half), BF),
            pltpu.VMEM((ring - 1, srows, half), BF),
            dma((chunks + 1,)),
            dma((2 + 2 * nbits, chunks + 1)),
            dma((2 + 2 * nbits, chunks + 1)),
            dma((ring - 1, chunks + 1)),
            dma((ring - 1, chunks + 1)),
            dma((ring - 1, chunks + 1)),
            dma((ring - 1, chunks + 1)),
        ],
        compiler_params=pltpu.CompilerParams(
            collective_id=0, has_side_effects=True, vmem_limit_bytes=60 << 20
        ),
        name="reduce_all",
    )(big, small)


def local(
    tokens, step_ids, prefix, keep_bits, ada_weight, ada_bias, norm1_gain, qkv_weight, out_weight,
    norm2_gain, up_weight, up_bias, down_weight, down_bias, cotangent,
):
    wide_size = lax.axis_size("wide")
    ring = lax.axis_size("narrow")
    wide = lax.axis_index("wide")
    chip = lax.axis_index("narrow")
    core = wide % 2
    groups, span, width = tokens.shape
    assert ring == 2 * groups and wide_size % 2 == 0
    count = groups * span
    length = ring * span
    hidden_width = up_weight.shape[1]
    head_count = width // HEAD
    both = ("wide", "narrow")

    routes = []
    for step in range(groups):
        route = []
        for outer in range(wide_size // 2):
            for c in range(2):
                for z in range(ring):
                    seq = c * groups + (step + z) % groups
                    source = (2 * outer + c) * ring + z
                    target = (2 * outer + z // groups) * ring + seq
                    route.append((source, target))
        routes.append(route)

    def bring(array):
        got = jnp.stack(
            [
                lax.ppermute(
                    lax.dynamic_index_in_dim(array, (step + chip) % groups, 0, keepdims=False),
                    both,
                    routes[step],
                )
                for step in range(groups)
            ]
        )
        blocks = [
            lax.dynamic_index_in_dim(got, (chip - j) % groups, 0, keepdims=False)
            for j in range(groups)
        ]
        return jnp.concatenate(blocks, axis=0)

    def give_back(rows):
        blocks = rows.reshape(groups, span, width)
        got = jnp.stack(
            [
                lax.ppermute(
                    lax.dynamic_index_in_dim(blocks, (chip - step) % groups, 0, keepdims=False),
                    both,
                    [(b, a) for a, b in routes[step]],
                )
                for step in range(groups)
            ]
        )
        return jnp.stack(
            [
                lax.dynamic_index_in_dim(got, (g - chip) % groups, 0, keepdims=False)
                for g in range(groups)
            ]
        )

    swap = [(w, w + 1 - 2 * (w % 2)) for w in range(wide_size)]

    inputs_low = bring(tokens)
    table = jnp.concatenate([prefix[:, None], step_ids[:, None], keep_bits], axis=1)
    table = jnp.where(chip // groups == core, table, lax.ppermute(table, "wide", swap))
    row = lax.dynamic_index_in_dim(table, chip % groups, 0, keepdims=False)
    inputs_low, cotangent = lax.optimization_barrier((inputs_low, cotangent))
    out_grad = bring(cotangent).astype(F32)

    bits_here = row[2:]
    allowed = (jnp.arange(length, dtype=jnp.int32) < row[0]) | (bits_here == 1)
    bias = jnp.where(allowed, 0.0, masked_score).astype(F32)
    bias_wide = jnp.broadcast_to(bias.reshape(2, count, 1), (2, count, 128))
    bias_a = lax.dynamic_index_in_dim(bias_wide, core, 0, keepdims=False)
    bias_b = lax.dynamic_index_in_dim(bias_wide, 1 - core, 0, keepdims=False)

    condition = jax.nn.silu(time_embed(row[1:2]))
    modulation = (
        jnp.dot(
            condition, ada_weight.astype(F32).T, precision=lax.Precision.HIGHEST,
            preferred_element_type=F32,
        )
        + ada_bias
    )
    shift_one, scale_one, gate_one, shift_two, scale_two, gate_two = jnp.split(
        modulation, 6, axis=-1
    )
    cosine_rows, sine_rows = rope_tables(
        (core * count + jnp.arange(count, dtype=jnp.int32)).astype(F32)
    )

    inputs = inputs_low.astype(F32)
    normed, norm_back = jax.vjp(modulate, inputs, norm1_gain, shift_one, scale_one)
    normed_low = normed.astype(BF)
    projected = dot(normed_low, qkv_weight, ((1,), (0,)))
    shaped = projected.reshape(count, 3, head_count, HEAD)
    queries = (
        (rotate(shaped[:, 0], cosine_rows, sine_rows, 1.0) * HEAD**-0.5)
        .astype(BF)
        .reshape(count, width)
    )
    keys = rotate(shaped[:, 1], cosine_rows, sine_rows, 1.0).astype(BF).reshape(count, width)
    values = shaped[:, 2].astype(BF).reshape(count, width)
    keys_b = lax.ppermute(keys, "wide", swap)
    values_b = lax.ppermute(values, "wide", swap)

    attended_t, lse = attend(queries, keys, values, keys_b, values_b, bias_a, bias_b)
    branch_one = dot(attended_t, out_weight, ((0,), (0,)))
    middle = inputs + gate_one * branch_one
    normed_two, norm_back_two = jax.vjp(modulate, middle, norm2_gain, shift_two, scale_two)
    normed_two_low = normed_two.astype(BF)
    hidden = dot(normed_two_low, up_weight, ((1,), (0,))) + up_bias
    active, gelu_back = jax.vjp(gelu_tanh, hidden)
    active_low = active.astype(BF)
    branch_two = dot(active_low, down_weight, ((1,), (0,))) + down_bias
    outputs = give_back((middle + gate_two * branch_two).astype(BF))

    gate_two_grad = jnp.sum(out_grad * branch_two, axis=0)
    branch_two_grad = (gate_two * out_grad).astype(BF)
    down_grad = dot(active_low, branch_two_grad, ((0,), (0,))).astype(BF)
    down_bias_grad = jnp.sum(branch_two_grad.astype(F32), axis=0)
    (hidden_grad,) = gelu_back(dot(branch_two_grad, down_weight, ((1,), (1,))))
    hidden_low = hidden_grad.astype(BF)
    up_grad = dot(normed_two_low, hidden_low, ((0,), (0,))).astype(BF)
    up_bias_grad = jnp.sum(hidden_low.astype(F32), axis=0)
    middle_part, gain_two_grad, shift_two_grad, scale_two_grad = norm_back_two(
        dot(hidden_low, up_weight, ((1,), (1,)))
    )
    middle_grad = out_grad + middle_part
    gate_one_grad = jnp.sum(middle_grad * branch_one, axis=0)
    branch_one_grad = (gate_one * middle_grad).astype(BF)
    out_weight_grad = dot(attended_t, branch_one_grad, ((1,), (0,))).astype(BF)
    attended_grad = dot(branch_one_grad, out_weight, ((1,), (1,))).astype(BF)

    dq, dk, dv, dk_b, dv_b = attend_back(
        queries, keys, values, keys_b, values_b, bias_a, bias_b, attended_t, lse, attended_grad
    )
    dk = dk + lax.ppermute(dk_b, "wide", swap).astype(F32)
    dv = dv + lax.ppermute(dv_b, "wide", swap).astype(F32)

    def unrotate(values):
        return rotate(
            values.reshape(count, head_count, HEAD), cosine_rows, sine_rows, -1.0
        ).reshape(count, width)

    joined = jnp.concatenate([unrotate(dq), unrotate(dk), dv], axis=-1).astype(BF)
    qkv_grad = dot(normed_low, joined, ((0,), (0,))).astype(BF)
    input_part, gain_one_grad, shift_one_grad, scale_one_grad = norm_back(
        dot(joined, qkv_weight, ((1,), (1,)))
    )
    input_grad = give_back((middle_grad + input_part).astype(BF))

    pieces = wide_size // 2 * ring
    rows = width // pieces
    folds = hidden_width // width

    def tiles(array):
        return jnp.transpose(array.reshape(width, -1, width), (1, 0, 2))

    big = jnp.concatenate(
        [
            down_grad.reshape(folds, width, width),
            tiles(up_grad),
            out_weight_grad[None],
            tiles(qkv_grad),
        ]
    ).reshape(-1, pieces, rows, width)
    mod_grad = jnp.concatenate(
        [
            shift_one_grad[0], scale_one_grad[0], gate_one_grad,
            shift_two_grad[0], scale_two_grad[0], gate_two_grad,
        ]
    )
    total_seqs = wide_size * groups
    mod_size = 6 * width
    seq = (wide // 2) * ring + chip
    mod_rows = jnp.where(jnp.arange(total_seqs)[:, None] == seq, mod_grad[None, :], 0.0)
    small = jnp.concatenate(
        [mod_rows.reshape(-1), gain_one_grad, gain_two_grad, down_bias_grad, up_bias_grad]
    )
    srows = -(-small.shape[0] // (width * pieces * 8)) * 8
    small = jnp.pad(small, (0, srows * width * pieces - small.shape[0]))
    small = small.astype(BF).reshape(pieces, srows, width)

    summed, small_sum = reduce_all(big, small, wide_size, ring)
    summed = summed.reshape(-1, width, width)
    flat = small_sum.reshape(-1)
    at = total_seqs * mod_size
    mod_all = flat[:at].reshape(total_seqs, mod_size).astype(F32)
    rest = flat[at : at + 3 * width + hidden_width].astype(F32)
    steps_all = lax.all_gather(step_ids, "wide", axis=0, tiled=True)
    condition_all = jax.nn.silu(time_embed(steps_all))
    ada_grad = jnp.dot(
        mod_all.T, condition_all, precision=lax.Precision.HIGHEST, preferred_element_type=F32
    )

    def untile(array):
        return jnp.concatenate([array[i] for i in range(array.shape[0])], axis=1).astype(F32)

    return (
        outputs,
        input_grad,
        ada_grad,
        jnp.sum(mod_all, axis=0),
        rest[:width],
        untile(summed[2 * folds + 1 :]),
        summed[2 * folds].astype(F32),
        rest[width : 2 * width],
        untile(summed[folds : 2 * folds]),
        rest[3 * width :],
        summed[:folds].reshape(hidden_width, width).astype(F32),
        rest[2 * width : 3 * width],
    )


def solution(mesh):
    split = P("wide", "narrow", None)
    in_specs = (
        (split, P("wide"), P("wide"), P("wide", None)) + (P(),) * 10 + (split,)
    )
    out_specs = (split, split) + (P(),) * 10
    return jax.shard_map(local, mesh=mesh, in_specs=in_specs, out_specs=out_specs, check_vma=False)
```

```python
import functools
import math

import jax
import jax.numpy as jnp
import numpy as np
from jax import lax
from jax.experimental import pallas as pl
from jax.experimental.pallas import tpu as pltpu
from jax.sharding import PartitionSpec as P

HEAD = 64
TEMB = 128
MESH = pl.DeviceIdType.MESH
BF = jnp.bfloat16
F32 = jnp.float32
DMA = pltpu.SemaphoreType.DMA

norm_epsilon = 1e-05
gelu_coeff = 0.7978845608028654
masked_score = -1e30


def time_embed(step_ids):
    halfway = TEMB // 2
    frequency = jnp.exp(jnp.arange(halfway, dtype=F32) * (-math.log(10000.0) / halfway))
    angles = step_ids.astype(F32)[:, None] * frequency[None, :]
    return jnp.concatenate([jnp.cos(angles), jnp.sin(angles)], axis=-1)


def rope_tables(length):
    halfway = HEAD // 2
    inverse = 10000.0 ** (-2.0 * np.arange(halfway) / HEAD)
    angles = np.arange(length)[:, None] * inverse[None, :]
    sines = np.sin(angles)
    return (
        np.tile(np.cos(angles), (1, 4)).astype(np.float32),
        np.concatenate([-sines, sines, -sines, sines], axis=1).astype(np.float32),
    )


def dot(former, latter, dims):
    return lax.dot_general(former, latter, (dims, ((), ())), preferred_element_type=F32)


def rotate(values, cosines, sines, sign):
    lane = lax.broadcasted_iota(jnp.int32, (1, 128), 1)
    first = (lane % HEAD) < HEAD // 2
    parts = []
    for n in range(values.shape[1] // 128):
        part = values[:, n * 128 : (n + 1) * 128]
        partner = jnp.where(first, pltpu.roll(part, 128 - HEAD // 2, 1), pltpu.roll(part, HEAD // 2, 1))
        turned = partner * sines
        parts.append(part * cosines + (turned if sign > 0 else -turned))
    return parts[0] if len(parts) == 1 else jnp.concatenate(parts, axis=1)


def normed_rows(values):
    center = values - jnp.mean(values, axis=-1, keepdims=True)
    spread = jnp.mean(center * center, axis=-1, keepdims=True)
    scale = lax.rsqrt(spread + norm_epsilon)
    return center * scale, scale


def part_of(mod_ref, index, width):
    return mod_ref[:, index * width : (index + 1) * width]


def wide_of(block, copies):
    return jnp.concatenate([block] * copies, axis=1)
LAG = 2


def front_kernel(
    groups, ring,
    tok_ref, cot_ref, wqkv_ref, ada_ref, info_ref, ada_bias_ref, gain_ref, cos_ref, sin_ref,
    x_ref, dy_ref, h_ref, q_ref, ka_ref, va_ref, kb_ref, vb_ref, o_ref, ot_ref, lse_ref,
    mod_ref, ba_ref, bb_ref, misc_ref,
    wqkv, ada, table,
    load_sem, self_sem, info_send, info_recv, send_sem, recv_sem, kv_send, kv_recv,
):
    span, width = tok_ref.shape[1:]
    count = groups * span
    wide = lax.axis_index("wide")
    chip = lax.axis_index("narrow")
    core = lax.rem(wide, 2)
    base = wide - core
    peer = (base + 1 - core, chip)

    load_w = pltpu.make_async_copy(wqkv_ref, wqkv, load_sem.at[0])
    load_a = pltpu.make_async_copy(ada_ref, ada, load_sem.at[1])
    load_a.start()
    load_w.start()

    barrier = pltpu.get_barrier_semaphore()
    for c in range(2):
        for d in range(ring):
            if c or d:
                other = (base + lax.rem(core + c, 2), lax.rem(chip + d, ring))
                pl.semaphore_signal(barrier, inc=1, device_id=other, device_id_type=MESH)
    pl.semaphore_wait(barrier, 2 * ring - 1)

    slot = lax.rem(chip, groups)
    to_core = chip // groups
    rows_out = pl.ds(pl.multiple_of(slot * span, span), span)

    def move(src, dst, kind, g):
        remote = pltpu.make_async_remote_copy(
            src_ref=src.at[g],
            dst_ref=dst.at[rows_out],
            send_sem=send_sem.at[kind, g],
            recv_sem=recv_sem.at[kind, slot],
            device_id=(base + to_core, core * groups + g),
            device_id_type=MESH,
        )
        here = pltpu.make_async_copy(src.at[g], dst.at[rows_out], self_sem.at[kind])
        own = (to_core == core) & (slot == g)
        return remote, here, own

    def send(src, dst, kind):
        for g in range(groups):
            remote, here, own = move(src, dst, kind, g)

            @pl.when(own)
            def _():
                here.start()

            @pl.when(jnp.logical_not(own))
            def _():
                remote.start()

    def sent(src, dst, kind):
        for g in range(groups):
            remote, here, own = move(src, dst, kind, g)

            @pl.when(jnp.logical_not(own))
            def _():
                remote.wait_send()

    def arrive(src, dst, kind, j):
        rows = pl.ds(j * span, span)
        own = (to_core == core) & (slot == j)

        @pl.when(own)
        def _():
            pltpu.make_async_copy(src.at[0], dst.at[rows], self_sem.at[kind]).wait()

        @pl.when(jnp.logical_not(own))
        def _():
            pltpu.make_async_remote_copy(
                src_ref=src.at[0],
                dst_ref=dst.at[rows],
                send_sem=send_sem.at[kind, 0],
                recv_sem=recv_sem.at[kind, j],
                device_id=peer,
                device_id_type=MESH,
            ).wait_recv()

    send(tok_ref, x_ref, 0)
    table[core] = info_ref[...]
    swap_info = pltpu.make_async_remote_copy(
        src_ref=info_ref,
        dst_ref=table.at[core],
        send_sem=info_send,
        recv_sem=info_recv,
        device_id=peer,
        device_id_type=MESH,
    )
    swap_info.start()
    swap_info.wait()
    row = table[chip // groups, lax.rem(chip, groups)]
    length = row.shape[1] - 2 * TEMB
    misc_ref[...] = row[:, TEMB + length :]
    bias = jnp.where(core == 0, row[:, TEMB : TEMB + count], row[:, TEMB + count : TEMB + length])
    ba_ref[...] = jnp.broadcast_to(bias, (128, count)).T
    bias = jnp.where(core == 1, row[:, TEMB : TEMB + count], row[:, TEMB + count : TEMB + length])
    bb_ref[...] = jnp.broadcast_to(bias, (128, count)).T

    cond = jnp.broadcast_to(row[:, :TEMB], (16, TEMB))
    high = cond.astype(BF).astype(F32)
    middle = (cond - high).astype(BF).astype(F32)
    low = cond - high - middle
    line = lax.broadcasted_iota(jnp.int32, (16, TEMB), 0)
    three = jnp.where(
        line == 0, high, jnp.where(line == 1, middle, jnp.where(line == 2, low, 0.0))
    ).astype(BF)
    load_a.wait()
    for i in range(6):
        cols = slice(i * width, (i + 1) * width)
        mod_ref[:, cols] = (
            jnp.sum(dot(three, ada[cols, :], ((1,), (1,))), axis=0, keepdims=True)
            + ada_bias_ref[:, cols]
        )
    shift = part_of(mod_ref, 0, width)
    scale = gain_ref[...] * (1.0 + part_of(mod_ref, 1, width))

    load_w.wait()
    swaps = []
    for j in range(groups):
        rows = pl.ds(j * span, span)
        arrive(tok_ref, x_ref, 0, j)
        if j == groups - 1:
            send(cot_ref, dy_ref, 1)
        normed, _ = normed_rows(x_ref[rows, :].astype(F32))
        h_ref[rows, :] = (normed * scale + shift).astype(BF)
        place = pl.ds(pl.multiple_of(core * count + j * span, span), span)
        cosines = cos_ref[place, :]
        sines = sin_ref[place, :]
        step = 256
        for n in (2, 1, 0):
            target = (q_ref, ka_ref, va_ref)[n]
            for m in range(width // step):
                cols = pl.ds(n * width + m * step, step)
                block = dot(h_ref[rows, :], wqkv[:, cols], ((1,), (0,)))
                if n < 2:
                    block = rotate(block, cosines, sines, 1)
                if n == 0:
                    block = block * HEAD**-0.5
                target[rows, m * step : (m + 1) * step] = block.astype(BF)
            if n > 0:
                swap = pltpu.make_async_remote_copy(
                    src_ref=target.at[rows],
                    dst_ref=(kb_ref, vb_ref)[n - 1].at[rows],
                    send_sem=kv_send.at[n - 1, j],
                    recv_sem=kv_recv.at[n - 1, j],
                    device_id=peer,
                    device_id_type=MESH,
                )
                swap.start()
                swaps.append(swap)
    for swap in swaps:
        swap.wait()

    copies = count // 128
    lane = lax.broadcasted_iota(jnp.int32, (1, 128), 1)

    @pl.loop(0, width // 128)
    def _(p):
        cols = pl.ds(pl.multiple_of(p * 128, 128), 128)
        q = q_ref[:, cols]
        ka = ka_ref[:, cols]
        kb = kb_ref[:, cols]
        va_t = va_ref[:, cols].T
        vb_t = vb_ref[:, cols].T
        outs = []
        for h in range(2):
            qm = jnp.where((lane // HEAD) == h, q, jnp.zeros_like(q))
            sa = dot(ka, qm, ((1,), (1,))) + wide_of(ba_ref[...], copies)
            sb = dot(kb, qm, ((1,), (1,))) + wide_of(bb_ref[...], copies)
            top = jnp.maximum(jnp.max(sa, axis=0, keepdims=True), jnp.max(sb, axis=0, keepdims=True))
            pa = jnp.exp(sa - top)
            pb = jnp.exp(sb - top)
            total = jnp.sum(pa, axis=0, keepdims=True) + jnp.sum(pb, axis=0, keepdims=True)
            part = slice(h * HEAD, (h + 1) * HEAD)
            out = dot(va_t[part], pa.astype(BF), ((1,), (0,))) + dot(
                vb_t[part], pb.astype(BF), ((1,), (0,))
            )
            outs.append(out / total)
            lse_ref[p, h : h + 1, :] = top + jnp.log(total)
        both = jnp.concatenate(outs, axis=0)
        ot_ref[cols, :] = both.astype(BF)
        o_ref[:, cols] = both.T.astype(BF)

    sent(tok_ref, x_ref, 0)
    for j in range(groups):
        arrive(cot_ref, dy_ref, 1, j)
    sent(cot_ref, dy_ref, 1)


def front(tokens, cotangent, wqkv, ada, info, ada_bias, gain, cosines, sines, ring):
    groups, span, width = tokens.shape
    count = groups * span
    any_space = pl.BlockSpec(memory_space=pl.ANY)
    vmem = pl.BlockSpec(memory_space=pltpu.VMEM)
    rows = jax.ShapeDtypeStruct((count, width), BF)
    return pl.pallas_call(
        functools.partial(front_kernel, groups, ring),
        in_specs=[any_space] * 4 + [vmem] * 5,
        out_specs=[vmem] * 15,
        out_shape=[rows] * 9
        + [
            jax.ShapeDtypeStruct((width, count), BF),
            jax.ShapeDtypeStruct((width // 128, 8, count), F32),
            jax.ShapeDtypeStruct((1, 6 * width), F32),
            jax.ShapeDtypeStruct((count, 128), F32),
            jax.ShapeDtypeStruct((count, 128), F32),
            jax.ShapeDtypeStruct((1, TEMB), F32),
        ],
        scratch_shapes=[
            pltpu.VMEM(wqkv.shape, BF),
            pltpu.VMEM(ada.shape, BF),
            pltpu.VMEM((2,) + info.shape, F32),
            DMA((2,)),
            DMA((2,)),
            DMA,
            DMA,
            DMA((2, groups)),
            DMA((2, groups)),
            DMA((2, groups)),
            DMA((2, groups)),
        ],
        compiler_params=pltpu.CompilerParams(
            collective_id=1, has_side_effects=True, vmem_limit_bytes=56 << 20
        ),
        name="front",
    )(tokens, cotangent, wqkv, ada, info, ada_bias, gain, cosines, sines)


def ffn_kernel(
    x_ref, o_ref, ot_ref, dy_ref, mod_ref, gain_ref, wout_ref, up_ref, up_bias_ref, down_ref,
    down_bias_ref,
    out_ref, do_ref, dx_ref, vec_ref, dup_bias_ref, ddown_ref, dup_ref, dout_ref,
    middle, branch, h, h_t, dm, acc, dacc,
):
    f = pl.program_id(0)
    count, width = x_ref.shape
    tile = min(256, count)
    shift, scale, gate_one, gate_two = (
        part_of(mod_ref, i, width) for i in (3, 4, 2, 5)
    )

    @pl.when(f == 0)
    def _():
        for r in range(0, count, tile):
            rows = slice(r, r + tile)
            a = dot(o_ref[rows, :], wout_ref[...], ((1,), (0,)))
            branch[rows, :] = a
            x1 = x_ref[rows, :].astype(F32) + gate_one * a
            middle[rows, :] = x1
            normed, _ = normed_rows(x1)
            h2 = (normed * (gain_ref[...] * (1.0 + scale)) + shift).astype(BF)
            h[rows, :] = h2
            h_t[:, rows] = h2.T
            dm_rows = (dy_ref[rows, :].astype(F32) * gate_two).astype(BF)
            dm[rows, :] = dm_rows
            part = jnp.sum(dm_rows.astype(F32), axis=0, keepdims=True)
            vec_ref[5:6, :] = part if r == 0 else vec_ref[5:6, :] + part

    u = dot(h[...], up_ref[...], ((1,), (0,))) + up_bias_ref[...]
    square = u * u
    tanh = jnp.tanh(gelu_coeff * (u + 0.044715 * u * square))
    g = (0.5 * u * (1.0 + tanh)).astype(BF)
    slope = 0.5 * (1.0 + tanh) + (0.5 * gelu_coeff) * u * (1.0 - tanh * tanh) * (
        1.0 + (3 * 0.044715) * square
    )
    part = dot(g, down_ref[...], ((1,), (0,)))
    ddown_ref[...] = dot(g, dm[...], ((0,), (0,))).astype(BF)
    du = (dot(dm[...], down_ref[...], ((1,), (1,))) * slope).astype(BF)
    dup_bias_ref[...] = jnp.sum(du.astype(F32), axis=0, keepdims=True)
    dup_ref[0] = dot(h_t[...], du, ((1,), (0,))).astype(BF)
    dpart = dot(du, up_ref[...], ((1,), (1,)))

    @pl.when(f == 0)
    def _():
        acc[...] = part
        dacc[...] = dpart

    @pl.when(f > 0)
    def _():
        acc[...] += part
        dacc[...] += dpart

    @pl.when(f == pl.num_programs(0) - 1)
    def _():
        sums = [0.0] * 5
        for r in range(0, count, tile):
            rows = slice(r, r + tile)
            m = acc[rows, :] + down_bias_ref[...]
            x1 = middle[rows, :]
            out_ref[rows, :] = (x1 + gate_two * m).astype(BF)
            dy = dy_ref[rows, :].astype(F32)
            dh = dacc[rows, :]
            n2, rscale = normed_rows(x1)
            dhn = dh * n2
            e = dh * ((1.0 + scale) * gain_ref[...])
            dx1 = dy + rscale * (
                e
                - jnp.mean(e, axis=-1, keepdims=True)
                - n2 * jnp.mean(e * n2, axis=-1, keepdims=True)
            )
            dx_ref[rows, :] = dx1
            da = (gate_one * dx1).astype(BF)
            h[rows, :] = da
            for i, value in enumerate((dx1 * branch[rows, :], dh, dhn, dy * m)):
                sums[i] = sums[i] + jnp.sum(value, axis=0, keepdims=True)
            do_ref[rows, :] = dot(da, wout_ref[...], ((1,), (1,))).astype(BF)
        vec_ref[0:1, :] = sums[0]
        vec_ref[1:2, :] = sums[1]
        vec_ref[2:3, :] = sums[2] * gain_ref[...]
        vec_ref[3:4, :] = sums[3]
        vec_ref[4:5, :] = sums[2] * (1.0 + scale)
        dout_ref[...] = dot(ot_ref[...], h[...], ((1,), (0,))).astype(BF)


def ffn(x, o, ot, dy, mod, gain, wout, up, up_bias, down, down_bias):
    count, width = x.shape
    hidden = up.shape[1]
    step = 256
    folds = width // step

    def full(array):
        return pl.BlockSpec(array.shape, lambda f: (0,) * array.ndim)

    rows = jax.ShapeDtypeStruct((count, width), BF)
    outs = [
        rows,
        rows,
        jax.ShapeDtypeStruct((count, width), F32),
        jax.ShapeDtypeStruct((8, width), F32),
        jax.ShapeDtypeStruct((1, hidden), F32),
        jax.ShapeDtypeStruct((hidden, width), BF),
        jax.ShapeDtypeStruct((hidden // width, width, width), BF),
        jax.ShapeDtypeStruct((width, width), BF),
    ]
    up_bias_spec = pl.BlockSpec((1, step), lambda f: (0, f))
    down_spec = pl.BlockSpec((step, width), lambda f: (f, 0))
    return pl.pallas_call(
        ffn_kernel,
        grid=(hidden // step,),
        in_specs=[
            full(x), full(o), full(ot), full(dy), full(mod), full(gain), full(wout),
            pl.BlockSpec((width, step), lambda f: (0, f)), up_bias_spec, down_spec,
            full(down_bias),
        ],
        out_specs=[full(s) for s in outs[:4]]
        + [
            up_bias_spec,
            down_spec,
            pl.BlockSpec((1, width, step), lambda f: (f // folds, 0, f % folds)),
            full(outs[7]),
        ],
        out_shape=outs,
        scratch_shapes=[
            pltpu.VMEM((count, width), F32),
            pltpu.VMEM((count, width), F32),
            pltpu.VMEM((count, width), BF),
            pltpu.VMEM((width, count), BF),
            pltpu.VMEM((count, width), BF),
            pltpu.VMEM((count, width), F32),
            pltpu.VMEM((count, width), F32),
        ],
        compiler_params=pltpu.CompilerParams(vmem_limit_bytes=56 << 20),
        name="ffn",
    )(x, o, ot, dy, mod, gain, wout, up, up_bias, down, down_bias)


def back_kernel(
    groups, wide_size, ring, lag,
    q_ref, ka_ref, va_ref, kb_ref, vb_ref, ba_ref, bb_ref, ot_ref, lse_ref, do_ref, x_ref, h_ref,
    dx_ref, mod_ref, gain_ref, cos_ref, sin_ref, misc_ref, vec_ref, dup_bias_ref,
    wqkv_ref, ddown_ref, dup_ref, dout_ref, rows_ref,
    sum_ref, ssum_ref, tokens_ref, grad_ref,
    wqkv, dqkv, dk_own, dv_own, dk_away, dv_away, dk_in, dv_in, dq_big, dsmall, drows,
    acc, sacc, core_in, score_in, bit_in, sbit_in,
    load_sem, copy_sem, send_sem, recv_sem, kv_send, kv_recv, self_sem, row_send, row_recv,
):
    chunks, pieces, piece_rows = acc.shape[:3]
    outer = (wide_size // 2).bit_length() - 1
    inner = ring.bit_length() - 1
    total_bits = outer + inner
    count, width = x_ref.shape
    span = count // groups
    pairs = width // 128
    folds = ddown_ref.shape[0]
    wide = lax.axis_index("wide")
    chip = lax.axis_index("narrow")
    core = lax.rem(wide, 2)
    base = wide - core
    core_peer = (base + 1 - core, chip)
    dims = []
    for b in range(outer):
        bit = lax.rem(wide // (2 << b), 2)
        dims.append((bit, wide + (1 - 2 * bit) * (2 << b), chip))
    for b in range(inner):
        bit = lax.rem(chip // (1 << b), 2)
        dims.append((bit, wide, chip + (1 - 2 * bit) * (1 << b)))
    up = list(range(outer))
    rest = list(range(outer, total_bits))
    orders = (up + rest, up[::-1] + rest, rest + up)

    load_w = pltpu.make_async_copy(wqkv_ref, wqkv, load_sem)
    load_w.start()
    barrier = pltpu.get_barrier_semaphore()
    for d in dims[:outer]:
        pl.semaphore_signal(barrier, inc=1, device_id=d[1:], device_id_type=MESH)
    for c in range(2):
        for d in range(ring):
            if c or d:
                other = (base + lax.rem(core + c, 2), lax.rem(chip + d, ring))
                pl.semaphore_signal(barrier, inc=1, device_id=other, device_id_type=MESH)
    pl.semaphore_wait(barrier, outer + 2 * ring - 1)

    slot = lax.rem(chip, groups)
    home = chip // groups

    def row_move(src, dst, kind, j):
        rows = pl.ds(j * span, span)
        remote = pltpu.make_async_remote_copy(
            src_ref=src.at[rows],
            dst_ref=dst.at[slot],
            send_sem=row_send.at[kind, j],
            recv_sem=row_recv.at[kind, slot],
            device_id=(base + home, core * groups + j),
            device_id_type=MESH,
        )
        here = pltpu.make_async_copy(src.at[rows], dst.at[slot], self_sem.at[kind])
        own = (home == core) & (slot == j)
        return remote, here, own

    def row_send_all(src, dst, kind):
        for j in range(groups):
            remote, here, own = row_move(src, dst, kind, j)

            @pl.when(own)
            def _():
                here.start()

            @pl.when(jnp.logical_not(own))
            def _():
                remote.start()

    def row_wait_all(src, dst, kind):
        for j in range(groups):
            remote, here, own = row_move(src, dst, kind, j)

            @pl.when(own)
            def _():
                here.wait()

            @pl.when(jnp.logical_not(own))
            def _():
                remote.wait_send()

        for g in range(groups):
            own = (home == core) & (slot == g)

            @pl.when(jnp.logical_not(own))
            def _():
                pltpu.make_async_remote_copy(
                    src_ref=src.at[pl.ds(0, span)],
                    dst_ref=dst.at[g],
                    send_sem=row_send.at[kind, 0],
                    recv_sem=row_recv.at[kind, g],
                    device_id=core_peer,
                    device_id_type=MESH,
                ).wait_recv()

    def plan(kind):
        late = kind // 4
        odd = lax.rem(kind, 2) * (1 - late)
        low = 0
        size = pieces
        steps = []
        for i in range(total_bits):
            bit, peer_wide, peer_here = (
                a + odd * (b - a) + late * (c - a)
                for a, b, c in zip(*(dims[order[i]] for order in orders))
            )
            size //= 2
            before = low
            low = low + bit * size
            steps.append((before + (1 - bit) * size, low, size, (peer_wide, peer_here)))
        return steps

    def stage(step, kind, sem, big, out, total, core_slot, bit_slots):
        cols = total.shape[-1]
        mine = pl.ds(pl.multiple_of(core * cols, 128), cols)
        other = pl.ds(pl.multiple_of((1 - core) * cols, 128), cols)
        steps = plan(kind)

        def remote(src, dst, index, peer):
            return pltpu.make_async_remote_copy(
                src_ref=src,
                dst_ref=dst,
                send_sem=send_sem.at[index, sem],
                recv_sem=recv_sem.at[index, sem],
                device_id=peer,
                device_id_type=MESH,
            )

        def core_copy():
            return remote(big.at[:, :, other], core_slot, 0, core_peer)

        def own_copy():
            return pltpu.make_async_copy(big.at[:, :, mine], total, copy_sem.at[sem])

        def bit_copy(i):
            away, _, size, peer = steps[i]
            return remote(total.at[pl.ds(away, size)], bit_slots[i], 1 + i, peer)

        def back_copy(i):
            _, keep, size, peer = steps[i]
            place = out.at[pl.ds(keep, size), :, mine]
            if i == total_bits - 1:
                return remote(total.at[pl.ds(keep, size)], place, 1 + total_bits + i, peer)
            return remote(place, place, 1 + total_bits + i, peer)

        def keep_copy():
            _, keep, size, _ = steps[-1]
            return pltpu.make_async_copy(
                total.at[pl.ds(keep, size)], out.at[pl.ds(keep, size), :, mine], copy_sem.at[sem]
            )

        def core_back():
            place = out.at[:, :, mine]
            return remote(place, place, 1 + 2 * total_bits, core_peer)

        def add(start, size, from_slot):
            @pl.loop(0, size)
            def _(j):
                total[start + j] = (total[start + j].astype(F32) + from_slot[j].astype(F32)).astype(BF)

        if step == 0:
            core_copy().start()
            own_copy().start()
        elif step == 1:
            own_copy().wait()
            core_copy().wait()
            add(0, pieces, core_slot)
            bit_copy(0).start()
        elif step <= total_bits + 1:
            i = step - 2
            bit_copy(i).wait()
            add(steps[i][1], steps[i][2], bit_slots[i])
            if step <= total_bits:
                bit_copy(i + 1).start()
            else:
                keep_copy().start()
                back_copy(i).start()
        elif step <= 2 * total_bits:
            i = 2 * total_bits + 1 - step
            if i == total_bits - 1:
                keep_copy().wait()
            back_copy(i).wait()
            back_copy(i - 1).start()
        elif step == 2 * total_bits + 1:
            back_copy(0).wait()
            core_back().start()
        else:
            core_back().wait()

    last = 2 * total_bits + 2

    def communicate(tick):
        for step in range(last, -1, -1):
            chunk = tick - lag * step

            def at_chunk(source):
                stage(
                    step, lax.rem(chunk, 5), chunk,
                    source, sum_ref.at[chunk], acc.at[chunk], core_in.at[chunk],
                    [ref.at[chunk] for ref in bit_in],
                )

            if step < 2:
                for source, first, size in (
                    (ddown_ref, 0, folds),
                    (dup_ref, folds, folds),
                    (dout_ref, 2 * folds, 1),
                    (dq_big, 2 * folds + 1, 3),
                ):

                    @pl.when((chunk >= first) & (chunk < first + size))
                    def _():
                        at_chunk(source.at[chunk - first])
            else:

                @pl.when((chunk >= 0) & (chunk < chunks))
                def _():
                    at_chunk(sum_ref.at[chunk])

            @pl.when(chunk == chunks)
            def _():
                stage(step, 0, chunks, dsmall, ssum_ref, sacc, score_in, sbit_in)

    copies = count // 128
    lane = lax.broadcasted_iota(jnp.int32, (1, 128), 1)
    place = pl.ds(pl.multiple_of(core * count, count), count)

    def kv_copies(p):
        cols = pl.ds(pl.multiple_of(p * 128, 128), 128)
        return [
            pltpu.make_async_remote_copy(
                src_ref=away.at[:, cols],
                dst_ref=landing.at[:, cols],
                send_sem=kv_send.at[i, p],
                recv_sem=kv_recv.at[i, p],
                device_id=core_peer,
                device_id_type=MESH,
            )
            for i, (away, landing) in enumerate(((dk_away, dk_in), (dv_away, dv_in)))
        ]

    def attention(p):
        cols = pl.ds(pl.multiple_of(p * 128, 128), 128)
        q = q_ref[:, cols]
        do = do_ref[:, cols]
        prod = ot_ref[cols, :].astype(F32) * do.astype(F32).T
        qs, dos, deltas, lses = [], [], [], []
        for h in range(2):
            picked = (lane // HEAD) == h
            qs.append(jnp.where(picked, q, jnp.zeros_like(q)))
            dos.append(jnp.where(picked, do, jnp.zeros_like(do)))
            deltas.append(jnp.sum(prod[h * HEAD : (h + 1) * HEAD], axis=0, keepdims=True))
            lses.append(lse_ref[p, h : h + 1, :])
        dq = [None, None]
        for k_ref, v_ref, b_ref, dk_ref, dv_ref in (
            (kb_ref, vb_ref, bb_ref, dk_away, dv_away),
            (ka_ref, va_ref, ba_ref, dk_own, dv_own),
        ):
            k = k_ref[:, cols]
            v = v_ref[:, cols]
            k_t = k.T
            dk = dv = None
            for h in range(2):
                s = dot(k, qs[h], ((1,), (1,))) + wide_of(b_ref[...], copies)
                prob = jnp.exp(s - lses[h])
                dv_h = dot(prob.astype(BF), dos[h], ((1,), (0,)))
                dprob = dot(v, dos[h], ((1,), (1,)))
                ds = (prob * (dprob - deltas[h])).astype(BF)
                dk_h = dot(ds, qs[h], ((1,), (0,)))
                part = dot(k_t[h * HEAD : (h + 1) * HEAD], ds, ((1,), (0,)))
                dq[h] = part if dq[h] is None else dq[h] + part
                dk = dk_h if dk is None else dk + dk_h
                dv = dv_h if dv is None else dv + dv_h
            dk_ref[:, cols] = dk.astype(dk_ref.dtype)
            dv_ref[:, cols] = dv.astype(dv_ref.dtype)
        dq_both = (jnp.concatenate(dq, axis=0) * (HEAD**-0.5)).T
        dqkv[:, cols] = rotate(dq_both, cos_ref[place, :], sin_ref[place, :], -1).astype(BF)
        for copy in kv_copies(p):
            copy.start()

    def join():
        @pl.loop(0, pairs)
        def _(p):
            for copy in kv_copies(p):
                copy.wait()
            cols = pl.ds(pl.multiple_of(p * 128, 128), 128)
            dk = dk_own[:, cols] + dk_in[:, cols].astype(F32)
            dv = dv_own[:, cols] + dv_in[:, cols].astype(F32)
            k_cols = pl.ds(pl.multiple_of(width + p * 128, 128), 128)
            v_cols = pl.ds(pl.multiple_of(2 * width + p * 128, 128), 128)
            dqkv[:, k_cols] = rotate(dk, cos_ref[place, :], sin_ref[place, :], -1).astype(BF)
            dqkv[:, v_cols] = dv.astype(BF)

    def weights():
        h_t = h_ref[...].T
        step = 256
        for n in range(3):
            for m in range(width // step):
                cols = pl.ds(n * width + m * step, step)
                block = dot(h_t, dqkv[:, cols], ((1,), (0,))).astype(BF)
                for i in range(pieces):
                    dq_big[n, i, :, m * step : (m + 1) * step] = block[
                        i * piece_rows : (i + 1) * piece_rows
                    ]

    def finish():
        load_w.wait()
        tile = min(256, count)
        scale = 1.0 + part_of(mod_ref, 1, width)
        sums = [0.0, 0.0]
        for r in range(0, count, tile):
            rows = slice(r, r + tile)
            dh = dot(dqkv[rows, :], wqkv[...], ((1,), (1,)))
            n1, rscale = normed_rows(x_ref[rows, :].astype(F32))
            e = dh * (scale * gain_ref[...])
            drows[rows, :] = (
                dx_ref[rows, :]
                + rscale
                * (
                    e
                    - jnp.mean(e, axis=-1, keepdims=True)
                    - n1 * jnp.mean(e * n1, axis=-1, keepdims=True)
                )
            ).astype(BF)
            sums[0] = sums[0] + jnp.sum(dh, axis=0, keepdims=True)
            sums[1] = sums[1] + jnp.sum(dh * n1, axis=0, keepdims=True)
        row_send_all(drows, grad_ref, 1)
        srows = dsmall.shape[1]
        seq = (wide // 2) * ring + chip
        seqs = wide_size * groups
        line = lax.broadcasted_iota(jnp.int32, (pieces * srows, width), 0)
        line_lane = lax.broadcasted_iota(jnp.int32, (1, width), 1)
        held = jnp.where((line_lane == seq) & (core == 0), 1.0, 0.0)
        fixed = seqs * 6
        entries = [
            (seq * 6, sums[0]),
            (seq * 6 + 1, sums[1] * gain_ref[...]),
            (seq * 6 + 2, vec_ref[0:1, :]),
            (seq * 6 + 3, vec_ref[1:2, :]),
            (seq * 6 + 4, vec_ref[2:3, :]),
            (seq * 6 + 5, vec_ref[3:4, :]),
            (fixed, sums[1] * scale),
            (fixed + 1, vec_ref[4:5, :]),
            (fixed + 2, vec_ref[5:6, :]),
            (fixed + 3, held * misc_ref[:, 0:1]),
            (fixed + 4, held * misc_ref[:, 1:2]),
        ] + [(fixed + 5 + i, dup_bias_ref[i : i + 1, :]) for i in range(folds)]
        value = jnp.zeros((pieces * srows, width), F32)
        for at, entry in entries:
            value = jnp.where(line == at, entry, value)
        dsmall[...] = value.reshape(pieces, srows, width).astype(BF)

    row_send_all(rows_ref, tokens_ref, 0)

    @pl.loop(0, chunks + 1 + lag * last)
    def _(tick):
        communicate(tick)

        @pl.when(tick < pairs)
        def _():
            attention(tick)

        @pl.when(tick == pairs)
        def _():
            join()
            weights()

        @pl.when(tick == pairs + 1)
        def _():
            finish()

    row_wait_all(rows_ref, tokens_ref, 0)
    row_wait_all(drows, grad_ref, 1)


def back(
    q, ka, va, kb, vb, ba, bb, ot, lse, do, x, h, dx, mod, gain, cosines, sines, misc, vec,
    dup_bias, wqkv, ddown, dup, dout, out_rows, groups, wide_size, ring, lag,
):
    count, width = x.shape
    pieces = wide_size // 2 * ring
    rows = width // pieces
    half = width // 2
    folds = ddown.shape[0] // width
    chunks = 2 * folds + 4
    pairs = width // 128
    total_bits = pieces.bit_length() - 1
    assert width // 256 * 256 == width and chunks > pairs + 2
    srows = -(-(wide_size * groups * 6 + 5 + folds) // (pieces * 8)) * 8
    sizes = [pieces >> (i + 1) for i in range(total_bits)]
    any_space = pl.BlockSpec(memory_space=pl.ANY)
    vmem = pl.BlockSpec(memory_space=pltpu.VMEM)
    block = jax.ShapeDtypeStruct((groups, count // groups, width), BF)
    return pl.pallas_call(
        functools.partial(back_kernel, groups, wide_size, ring, lag),
        in_specs=[vmem] * 20 + [any_space] * 5,
        out_specs=[any_space] * 4,
        out_shape=[
            jax.ShapeDtypeStruct((chunks, pieces, rows, width), BF),
            jax.ShapeDtypeStruct((pieces, srows, width), BF),
            block,
            block,
        ],
        scratch_shapes=[
            pltpu.VMEM(wqkv.shape, BF),
            pltpu.VMEM((count, 3 * width), BF),
            pltpu.VMEM((count, width), F32),
            pltpu.VMEM((count, width), F32),
            pltpu.VMEM((count, width), BF),
            pltpu.VMEM((count, width), BF),
            pltpu.VMEM((count, width), BF),
            pltpu.VMEM((count, width), BF),
            pltpu.VMEM((3, pieces, rows, width), BF),
            pltpu.VMEM((pieces, srows, width), BF),
            pltpu.VMEM((count, width), BF),
            pltpu.VMEM((chunks, pieces, rows, half), BF),
            pltpu.VMEM((pieces, srows, half), BF),
            pltpu.VMEM((chunks, pieces, rows, half), BF),
            pltpu.VMEM((pieces, srows, half), BF),
            [pltpu.VMEM((chunks, n, rows, half), BF) for n in sizes],
            [pltpu.VMEM((n, srows, half), BF) for n in sizes],
            DMA,
            DMA((chunks + 1,)),
            DMA((2 + 2 * total_bits, chunks + 1)),
            DMA((2 + 2 * total_bits, chunks + 1)),
            DMA((2, pairs)),
            DMA((2, pairs)),
            DMA((2,)),
            DMA((2, groups)),
            DMA((2, groups)),
        ],
        compiler_params=pltpu.CompilerParams(
            collective_id=0, has_side_effects=True, vmem_limit_bytes=62 << 20
        ),
        name="back",
    )(
        q, ka, va, kb, vb, ba, bb, ot, lse, do, x, h, dx, mod, gain, cosines, sines, misc, vec,
        dup_bias, wqkv,
        ddown.reshape(folds, pieces, rows, width),
        dup.reshape(folds, pieces, rows, width),
        dout.reshape(1, pieces, rows, width),
        out_rows,
    )


def local(
    tokens, step_ids, prefix, keep_bits, ada_weight, ada_bias, norm1_gain, qkv_weight, out_weight,
    norm2_gain, up_weight, up_bias, down_weight, down_bias, cotangent,
):
    wide_size = lax.axis_size("wide")
    ring = lax.axis_size("narrow")
    groups, span, width = tokens.shape
    assert ring == 2 * groups and wide_size % 2 == 0
    length = ring * span
    hidden = up_weight.shape[1]
    folds = hidden // width
    seqs = wide_size * groups

    allowed = (jnp.arange(length, dtype=jnp.int32)[None, :] < prefix[:, None]) | (keep_bits == 1)
    lanes = jnp.arange(TEMB, dtype=jnp.int32)[None, :]
    steps = step_ids[:, None]
    info = jnp.concatenate(
        [
            jax.nn.silu(time_embed(step_ids)),
            jnp.where(allowed, 0.0, masked_score),
            jnp.where(lanes == 0, steps // 32, jnp.where(lanes == 1, steps % 32, 0)).astype(F32),
        ],
        axis=1,
    )[:, None, :]
    cosines, sines = rope_tables(length)
    x, dy, h, q, ka, va, kb, vb, o, ot, lse, mod, ba, bb, misc = front(
        tokens, cotangent, qkv_weight, ada_weight, info, ada_bias[None], norm1_gain[None],
        cosines, sines, ring,
    )
    out_rows, do, dx, vec, dup_bias, ddown, dup, dout = ffn(
        x, o, ot, dy, mod, norm2_gain[None], out_weight, up_weight, up_bias[None], down_weight,
        down_bias[None],
    )
    summed, small, outputs, input_grad = back(
        q, ka, va, kb, vb, ba, bb, ot, lse, do, x, h, dx, mod, norm1_gain[None], cosines, sines,
        misc, vec, dup_bias.reshape(folds, width), qkv_weight, ddown, dup, dout, out_rows,
        groups, wide_size, ring, LAG,
    )
    summed = summed.reshape(-1, width, width)
    small = small.reshape(-1, width).astype(F32)
    at = seqs * 6
    mod_all = small[:at].reshape(seqs, 6 * width)
    steps_all = small[at + 3, :seqs] * 32 + small[at + 4, :seqs]
    ada_grad = jnp.dot(
        mod_all.T, jax.nn.silu(time_embed(steps_all)), precision=lax.Precision.HIGHEST,
        preferred_element_type=F32,
    )

    def untile(array):
        return jnp.concatenate([array[i] for i in range(array.shape[0])], axis=1).astype(F32)

    return (
        outputs,
        input_grad,
        ada_grad,
        jnp.sum(mod_all, axis=0),
        small[at],
        untile(summed[2 * folds + 1 :]),
        summed[2 * folds].astype(F32),
        small[at + 1],
        untile(summed[folds : 2 * folds]),
        small[at + 5 : at + 5 + folds].reshape(-1),
        summed[:folds].reshape(hidden, width).astype(F32),
        small[at + 2],
    )


def solution(mesh):
    split = P("wide", "narrow", None)
    in_specs = (
        (split, P("wide"), P("wide"), P("wide", None)) + (P(),) * 10 + (split,)
    )
    out_specs = (split, split) + (P(),) * 10
    return jax.shard_map(local, mesh=mesh, in_specs=in_specs, out_specs=out_specs, check_vma=False)
```

```python
import functools
import math

import jax
import jax.numpy as jnp
import numpy as np
from jax import lax
from jax.experimental import pallas as pl
from jax.experimental.pallas import tpu as pltpu
from jax.sharding import PartitionSpec as P

HEAD = 64
TEMB = 128
MESH = pl.DeviceIdType.MESH
BF = jnp.bfloat16
F32 = jnp.float32
DMA = pltpu.SemaphoreType.DMA

norm_epsilon = 1e-05
gelu_coeff = 0.7978845608028654
masked_score = -1e30


def time_embed(step_ids):
    halfway = TEMB // 2
    frequency = jnp.exp(jnp.arange(halfway, dtype=F32) * (-math.log(10000.0) / halfway))
    angles = step_ids.astype(F32)[:, None] * frequency[None, :]
    return jnp.concatenate([jnp.cos(angles), jnp.sin(angles)], axis=-1)


def rope_tables(length):
    halfway = HEAD // 2
    inverse = 10000.0 ** (-2.0 * np.arange(halfway) / HEAD)
    angles = np.arange(length)[:, None] * inverse[None, :]
    sines = np.sin(angles)
    return (
        np.tile(np.cos(angles), (1, 4)).astype(np.float32),
        np.concatenate([-sines, sines, -sines, sines], axis=1).astype(np.float32),
    )


def dot(former, latter, dims):
    return lax.dot_general(former, latter, (dims, ((), ())), preferred_element_type=F32)


def rotate(values, cosines, sines, sign):
    lane = lax.broadcasted_iota(jnp.int32, (1, 128), 1)
    first = (lane % HEAD) < HEAD // 2
    parts = []
    for n in range(values.shape[1] // 128):
        part = values[:, n * 128 : (n + 1) * 128]
        partner = jnp.where(first, pltpu.roll(part, 128 - HEAD // 2, 1), pltpu.roll(part, HEAD // 2, 1))
        turned = partner * sines
        parts.append(part * cosines + (turned if sign > 0 else -turned))
    return parts[0] if len(parts) == 1 else jnp.concatenate(parts, axis=1)


def normed_rows(values):
    center = values - jnp.mean(values, axis=-1, keepdims=True)
    spread = jnp.mean(center * center, axis=-1, keepdims=True)
    scale = lax.rsqrt(spread + norm_epsilon)
    return center * scale, scale


def part_of(mod_ref, index, width):
    return mod_ref[:, index * width : (index + 1) * width]


def wide_of(block, copies):
    return jnp.concatenate([block] * copies, axis=1)


def front_kernel(
    groups, ring,
    tok_ref, cot_ref, wqkv_ref, ada_ref, info_ref, par_ref, cos_ref, sin_ref,
    x_ref, dy_ref, h_ref, q_ref, ka_ref, va_ref, kb_ref, vb_ref, o_ref, ot_ref, lse_ref,
    mod_ref, ba_ref, bb_ref, cond_ref,
    wqkv, ada, table,
    load_sem, self_sem, info_send, info_recv, send_sem, recv_sem, kv_send, kv_recv,
):
    span, width = tok_ref.shape[1:]
    count = groups * span
    wide = lax.axis_index("wide")
    chip = lax.axis_index("narrow")
    core = lax.rem(wide, 2)
    base = wide - core
    peer = (base + 1 - core, chip)

    load_w = pltpu.make_async_copy(wqkv_ref, wqkv, load_sem.at[0])
    load_a = pltpu.make_async_copy(ada_ref, ada, load_sem.at[1])
    load_a.start()
    load_w.start()

    barrier = pltpu.get_barrier_semaphore()
    for c in range(2):
        for d in range(ring):
            if c or d:
                other = (base + lax.rem(core + c, 2), lax.rem(chip + d, ring))
                pl.semaphore_signal(barrier, inc=1, device_id=other, device_id_type=MESH)
    pl.semaphore_wait(barrier, 2 * ring - 1)

    slot = lax.rem(chip, groups)
    to_core = chip // groups
    rows_out = pl.ds(pl.multiple_of(slot * span, span), span)

    def move(src, dst, kind, g):
        remote = pltpu.make_async_remote_copy(
            src_ref=src.at[g],
            dst_ref=dst.at[rows_out],
            send_sem=send_sem.at[kind, g],
            recv_sem=recv_sem.at[kind, slot],
            device_id=(base + to_core, core * groups + g),
            device_id_type=MESH,
        )
        here = pltpu.make_async_copy(src.at[g], dst.at[rows_out], self_sem.at[kind])
        own = (to_core == core) & (slot == g)
        return remote, here, own

    def send(src, dst, kind):
        for g in range(groups):
            remote, here, own = move(src, dst, kind, g)

            @pl.when(own)
            def _():
                here.start()

            @pl.when(jnp.logical_not(own))
            def _():
                remote.start()

    def sent(src, dst, kind):
        for g in range(groups):
            remote, here, own = move(src, dst, kind, g)

            @pl.when(jnp.logical_not(own))
            def _():
                remote.wait_send()

    def arrive(src, dst, kind, j):
        rows = pl.ds(j * span, span)
        own = (to_core == core) & (slot == j)

        @pl.when(own)
        def _():
            pltpu.make_async_copy(src.at[0], dst.at[rows], self_sem.at[kind]).wait()

        @pl.when(jnp.logical_not(own))
        def _():
            pltpu.make_async_remote_copy(
                src_ref=src.at[0],
                dst_ref=dst.at[rows],
                send_sem=send_sem.at[kind, 0],
                recv_sem=recv_sem.at[kind, j],
                device_id=peer,
                device_id_type=MESH,
            ).wait_recv()

    send(tok_ref, x_ref, 0)
    table[core] = info_ref[...]
    swap_info = pltpu.make_async_remote_copy(
        src_ref=info_ref,
        dst_ref=table.at[core],
        send_sem=info_send,
        recv_sem=info_recv,
        device_id=peer,
        device_id_type=MESH,
    )
    swap_info.start()
    swap_info.wait()
    row = table[chip // groups, lax.rem(chip, groups)]
    length = row.shape[1] - TEMB
    cond_ref[...] = row[:, :TEMB]
    bias = jnp.where(core == 0, row[:, TEMB : TEMB + count], row[:, TEMB + count : TEMB + length])
    ba_ref[...] = jnp.broadcast_to(bias, (128, count)).T
    bias = jnp.where(core == 1, row[:, TEMB : TEMB + count], row[:, TEMB + count : TEMB + length])
    bb_ref[...] = jnp.broadcast_to(bias, (128, count)).T

    cond = jnp.broadcast_to(row[:, :TEMB], (16, TEMB))
    high = cond.astype(BF).astype(F32)
    middle = (cond - high).astype(BF).astype(F32)
    low = cond - high - middle
    line = lax.broadcasted_iota(jnp.int32, (16, TEMB), 0)
    three = jnp.where(
        line == 0, high, jnp.where(line == 1, middle, jnp.where(line == 2, low, 0.0))
    ).astype(BF)
    load_a.wait()
    for i in range(6):
        cols = slice(i * width, (i + 1) * width)
        mod_ref[:, cols] = (
            jnp.sum(dot(three, ada[cols, :], ((1,), (1,))), axis=0, keepdims=True)
            + par_ref[3 + i : 4 + i, :]
        )
    shift = part_of(mod_ref, 0, width)
    scale = par_ref[0:1, :] * (1.0 + part_of(mod_ref, 1, width))

    load_w.wait()
    swaps = []
    for j in range(groups):
        rows = pl.ds(j * span, span)
        arrive(tok_ref, x_ref, 0, j)
        if j == groups - 1:
            send(cot_ref, dy_ref, 1)
        normed, _ = normed_rows(x_ref[rows, :].astype(F32))
        h_ref[rows, :] = (normed * scale + shift).astype(BF)
        place = pl.ds(pl.multiple_of(core * count + j * span, span), span)
        cosines = cos_ref[place, :]
        sines = sin_ref[place, :]
        step = 256
        for n in (2, 1, 0):
            target = (q_ref, ka_ref, va_ref)[n]
            for m in range(width // step):
                cols = pl.ds(n * width + m * step, step)
                block = dot(h_ref[rows, :], wqkv[:, cols], ((1,), (0,)))
                if n < 2:
                    block = rotate(block, cosines, sines, 1)
                if n == 0:
                    block = block * HEAD**-0.5
                target[rows, m * step : (m + 1) * step] = block.astype(BF)
            if n > 0:
                swap = pltpu.make_async_remote_copy(
                    src_ref=target.at[rows],
                    dst_ref=(kb_ref, vb_ref)[n - 1].at[rows],
                    send_sem=kv_send.at[n - 1, j],
                    recv_sem=kv_recv.at[n - 1, j],
                    device_id=peer,
                    device_id_type=MESH,
                )
                swap.start()
                swaps.append(swap)
    for swap in swaps:
        swap.wait()

    copies = count // 128
    lane = lax.broadcasted_iota(jnp.int32, (1, 128), 1)

    @pl.loop(0, width // 128)
    def _(p):
        cols = pl.ds(pl.multiple_of(p * 128, 128), 128)
        q = q_ref[:, cols]
        ka = ka_ref[:, cols]
        kb = kb_ref[:, cols]
        va_t = va_ref[:, cols].T
        vb_t = vb_ref[:, cols].T
        outs = []
        for h in range(2):
            qm = jnp.where((lane // HEAD) == h, q, jnp.zeros_like(q))
            sa = dot(ka, qm, ((1,), (1,))) + wide_of(ba_ref[...], copies)
            sb = dot(kb, qm, ((1,), (1,))) + wide_of(bb_ref[...], copies)
            top = jnp.maximum(jnp.max(sa, axis=0, keepdims=True), jnp.max(sb, axis=0, keepdims=True))
            pa = jnp.exp(sa - top)
            pb = jnp.exp(sb - top)
            total = jnp.sum(pa, axis=0, keepdims=True) + jnp.sum(pb, axis=0, keepdims=True)
            part = slice(h * HEAD, (h + 1) * HEAD)
            out = dot(va_t[part], pa.astype(BF), ((1,), (0,))) + dot(
                vb_t[part], pb.astype(BF), ((1,), (0,))
            )
            outs.append(out / total)
            lse_ref[p, h : h + 1, :] = top + jnp.log(total)
        both = jnp.concatenate(outs, axis=0)
        ot_ref[cols, :] = both.astype(BF)
        o_ref[:, cols] = both.T.astype(BF)

    sent(tok_ref, x_ref, 0)
    for j in range(groups):
        arrive(cot_ref, dy_ref, 1, j)
    sent(cot_ref, dy_ref, 1)


def front(tokens, cotangent, wqkv, ada, info, params, cosines, sines, ring):
    groups, span, width = tokens.shape
    count = groups * span
    any_space = pl.BlockSpec(memory_space=pl.ANY)
    vmem = pl.BlockSpec(memory_space=pltpu.VMEM)
    rows = jax.ShapeDtypeStruct((count, width), BF)
    return pl.pallas_call(
        functools.partial(front_kernel, groups, ring),
        in_specs=[any_space] * 4 + [vmem] * 4,
        out_specs=[vmem] * 15,
        out_shape=[rows] * 9
        + [
            jax.ShapeDtypeStruct((width, count), BF),
            jax.ShapeDtypeStruct((width // 128, 8, count), F32),
            jax.ShapeDtypeStruct((1, 6 * width), F32),
            jax.ShapeDtypeStruct((count, 128), F32),
            jax.ShapeDtypeStruct((count, 128), F32),
            jax.ShapeDtypeStruct((1, TEMB), F32),
        ],
        scratch_shapes=[
            pltpu.VMEM(wqkv.shape, BF),
            pltpu.VMEM(ada.shape, BF),
            pltpu.VMEM((2,) + info.shape, F32),
            DMA((2,)),
            DMA((2,)),
            DMA,
            DMA,
            DMA((2, groups)),
            DMA((2, groups)),
            DMA((2, groups)),
            DMA((2, groups)),
        ],
        compiler_params=pltpu.CompilerParams(
            collective_id=1, has_side_effects=True, vmem_limit_bytes=56 << 20
        ),
        name="front",
    )(tokens, cotangent, wqkv, ada, info, params, cosines, sines)


def rest_kernel(
    groups, wide_size, ring, lags,
    x_ref, o_ref, ot_ref, dy_ref, mod_ref, par_ref, cos_ref, sin_ref, cond_ref, lse_ref, wout_ref,
    q_in, ka_in, va_in, kb_in, vb_in, h_in, ba_in, bb_in, up_ref, down_ref, wqkv_ref,
    sum_ref, ssum_ref, tokens_ref, grad_ref,
    q_ref, ka_ref, va_ref, kb_ref, vb_ref, h_ref, ba_ref, bb_ref,
    weights, staging, dsmall, middle, branch, normed_low, normed_t, dm, total_a, total_b, active,
    slope, dq_t, vec, dup_bias, out_rows, drows, dqkv, dk_in, dv_in,
    acc, sacc, core_in, score_in, bit_in, sbit_in,
    load_sem, weight_sem, copy_sem, send_sem, recv_sem, kv_send, kv_recv, self_sem, row_send,
    row_recv,
):
    chunks, pieces, piece_rows = acc.shape[:3]
    slots = core_in.shape[0]
    subs = x_ref.shape[1] // (2 * acc.shape[-1])
    stages = staging.shape[0]
    outer = (wide_size // 2).bit_length() - 1
    inner = ring.bit_length() - 1
    total_bits = outer + inner
    count, width = x_ref.shape
    span = count // groups
    pairs = width // 128
    folds = up_ref.shape[1] // width
    early = (2 * folds + 1) * subs
    gap = 2 * pairs - subs + 2
    wide = lax.axis_index("wide")
    chip = lax.axis_index("narrow")
    core = lax.rem(wide, 2)
    base = wide - core
    core_peer = (base + 1 - core, chip)
    dims = []
    for b in range(outer):
        bit = lax.rem(wide // (2 << b), 2)
        dims.append((bit, wide + (1 - 2 * bit) * (2 << b), chip))
    for b in range(inner):
        bit = lax.rem(chip // (1 << b), 2)
        dims.append((bit, wide, chip + (1 - 2 * bit) * (1 << b)))
    up = list(range(outer))
    rest = list(range(outer, total_bits))
    orders = (up + rest, up[::-1] + rest, rest + up)

    def load_up(i, slot):
        cols = pl.ds(pl.multiple_of(i * width, width), width)
        return pltpu.make_async_copy(up_ref.at[:, cols], weights.at[slot], weight_sem.at[slot])

    def load_down(i, slot):
        rows = pl.ds(pl.multiple_of(i * width, width), width)
        return pltpu.make_async_copy(down_ref.at[rows], weights.at[slot], weight_sem.at[slot])

    def load_qkv(n):
        cols = pl.ds(n * width, width)
        return pltpu.make_async_copy(wqkv_ref.at[:, cols], weights.at[n], weight_sem.at[n])

    for i in range(2):
        load_up(i, 2 * i).start()
        load_down(i, 2 * i + 1).start()
    loads = [
        pltpu.make_async_copy(src, dst, load_sem.at[i])
        for i, (src, dst) in enumerate(
            (
                (q_in, q_ref), (ka_in, ka_ref), (va_in, va_ref), (kb_in, kb_ref), (vb_in, vb_ref),
                (h_in, h_ref), (ba_in, ba_ref), (bb_in, bb_ref),
            )
        )
    ]
    for load in loads:
        load.start()
    barrier = pltpu.get_barrier_semaphore()
    for d in dims[:outer]:
        pl.semaphore_signal(barrier, inc=1, device_id=d[1:], device_id_type=MESH)
    for c in range(2):
        for d in range(ring):
            if c or d:
                other = (base + lax.rem(core + c, 2), lax.rem(chip + d, ring))
                pl.semaphore_signal(barrier, inc=1, device_id=other, device_id_type=MESH)
    pl.semaphore_wait(barrier, outer + 2 * ring - 1)

    slot = lax.rem(chip, groups)
    home = chip // groups

    def row_move(src, dst, kind, j):
        rows = pl.ds(j * span, span)
        remote = pltpu.make_async_remote_copy(
            src_ref=src.at[rows],
            dst_ref=dst.at[slot],
            send_sem=row_send.at[kind, j],
            recv_sem=row_recv.at[kind, slot],
            device_id=(base + home, core * groups + j),
            device_id_type=MESH,
        )
        here = pltpu.make_async_copy(src.at[rows], dst.at[slot], self_sem.at[kind])
        own = (home == core) & (slot == j)
        return remote, here, own

    def row_send_all(src, dst, kind):
        for j in range(groups):
            remote, here, own = row_move(src, dst, kind, j)

            @pl.when(own)
            def _():
                here.start()

            @pl.when(jnp.logical_not(own))
            def _():
                remote.start()

    def row_wait_all(src, dst, kind):
        for j in range(groups):
            remote, here, own = row_move(src, dst, kind, j)

            @pl.when(own)
            def _():
                here.wait()

            @pl.when(jnp.logical_not(own))
            def _():
                remote.wait_send()

        for g in range(groups):
            own = (home == core) & (slot == g)

            @pl.when(jnp.logical_not(own))
            def _():
                pltpu.make_async_remote_copy(
                    src_ref=src.at[pl.ds(0, span)],
                    dst_ref=dst.at[g],
                    send_sem=row_send.at[kind, 0],
                    recv_sem=row_recv.at[kind, g],
                    device_id=core_peer,
                    device_id_type=MESH,
                ).wait_recv()

    def plan(kind):
        late = kind // 4
        odd = lax.rem(kind, 2) * (1 - late)
        low = 0
        size = pieces
        steps = []
        for i in range(total_bits):
            bit, peer_wide, peer_here = (
                a + odd * (b - a) + late * (c - a)
                for a, b, c in zip(*(dims[order[i]] for order in orders))
            )
            size //= 2
            before = low
            low = low + bit * size
            steps.append((before + (1 - bit) * size, low, size, (peer_wide, peer_here)))
        return steps

    def stage(step, kind, sem, lane_base, big, out, total, core_slot, bit_slots):
        cols = total.shape[-1]
        mine = pl.ds(pl.multiple_of(lane_base + core * cols, 128), cols)
        other = pl.ds(pl.multiple_of(lane_base + (1 - core) * cols, 128), cols)
        steps = plan(kind)

        def remote(src, dst, index, peer):
            return pltpu.make_async_remote_copy(
                src_ref=src,
                dst_ref=dst,
                send_sem=send_sem.at[index, sem],
                recv_sem=recv_sem.at[index, sem],
                device_id=peer,
                device_id_type=MESH,
            )

        def core_copy():
            return remote(big.at[:, :, other], core_slot, 0, core_peer)

        def own_copy():
            return pltpu.make_async_copy(big.at[:, :, mine], total, copy_sem.at[sem])

        def bit_copy(i):
            away, _, size, peer = steps[i]
            return remote(total.at[pl.ds(away, size)], bit_slots[i], 1 + i, peer)

        def back_copy(i):
            _, keep, size, peer = steps[i]
            place = out.at[pl.ds(keep, size), :, mine]
            if i == total_bits - 1:
                return remote(total.at[pl.ds(keep, size)], place, 1 + total_bits + i, peer)
            return remote(place, place, 1 + total_bits + i, peer)

        def keep_copy():
            _, keep, size, _ = steps[-1]
            return pltpu.make_async_copy(
                total.at[pl.ds(keep, size)], out.at[pl.ds(keep, size), :, mine], copy_sem.at[sem]
            )

        def core_back():
            place = out.at[:, :, mine]
            return remote(place, place, 1 + 2 * total_bits, core_peer)

        def add(start, size, from_slot):
            @pl.loop(0, size)
            def _(j):
                total[start + j] = (total[start + j].astype(F32) + from_slot[j].astype(F32)).astype(BF)

        if step == 0:
            core_copy().start()
            own_copy().start()
        elif step == 1:
            own_copy().wait()
            core_copy().wait()
            add(0, pieces, core_slot)
            bit_copy(0).start()
        elif step <= total_bits + 1:
            i = step - 2
            bit_copy(i).wait()
            add(steps[i][1], steps[i][2], bit_slots[i])
            if step <= total_bits:
                bit_copy(i + 1).start()
            else:
                keep_copy().start()
                back_copy(i).start()
        elif step <= 2 * total_bits:
            i = 2 * total_bits + 1 - step
            if i == total_bits - 1:
                keep_copy().wait()
            back_copy(i).wait()
            back_copy(i - 1).start()
        elif step == 2 * total_bits + 1:
            back_copy(0).wait()
            core_back().start()
        else:
            core_back().wait()

    last = 2 * total_bits + 2

    offsets = [sum(lags[:step]) for step in range(last + 1)]

    def communicate(tick):
        for step in range(last, -1, -1):
            entry = tick - offsets[step] - 2
            chunk = entry - gap * (entry // (early + gap))

            @pl.when(
                ((entry >= 0) & (entry < early))
                | ((entry >= early + gap) & (entry < chunks + gap))
            )
            def _():
                block = chunk // subs
                stage(
                    step, lax.rem(chunk, 2) + lax.rem(chunk, 12) // 11 * 3, chunk,
                    lax.rem(chunk, subs) * 2 * acc.shape[-1],
                    staging.at[lax.rem(block, stages)], sum_ref.at[block], acc.at[chunk],
                    core_in.at[lax.rem(chunk, slots)], [ref.at[chunk] for ref in bit_in],
                )

            @pl.when(entry == chunks + gap)
            def _():
                stage(step, 0, chunks, 0, dsmall, ssum_ref, sacc, score_in, sbit_in)

    def place_block(block, value, cols):
        for i in range(pieces):
            staging[lax.rem(block, stages), i, :, cols] = value[
                i * piece_rows : (i + 1) * piece_rows
            ]

    tile = min(256, count)
    tiles = [slice(r, r + tile) for r in range(0, count, tile)]
    gain_one = par_ref[0:1, :]
    gain_two = par_ref[1:2, :]
    shift_two, scale_two, gate_one, gate_two = (part_of(mod_ref, i, width) for i in (3, 4, 2, 5))

    def prepare():
        total = 0.0
        for rows in tiles:
            a = dot(o_ref[rows, :], wout_ref[...], ((1,), (0,)))
            branch[rows, :] = a
            x1 = x_ref[rows, :].astype(F32) + gate_one * a
            middle[rows, :] = x1
            normed, _ = normed_rows(x1)
            h2 = (normed * (gain_two * (1.0 + scale_two)) + shift_two).astype(BF)
            normed_low[rows, :] = h2
            normed_t[:, rows] = h2.T
            dm_rows = (dy_ref[rows, :].astype(F32) * gate_two).astype(BF)
            dm[rows, :] = dm_rows
            total = total + jnp.sum(dm_rows.astype(F32), axis=0, keepdims=True)
        vec[5:6, :] = total

    def hidden_units(i, rows):
        slot = 2 * lax.rem(i, 2)
        if rows is tiles[0]:
            load_up(i, slot).wait()
            load_down(i, slot + 1).wait()
        bias = par_ref[pl.ds(9 + i, 1), :]
        u = dot(normed_low[rows, :], weights[slot], ((1,), (0,))) + bias
        square = u * u
        tanh = jnp.tanh(gelu_coeff * (u + 0.044715 * u * square))
        g = (0.5 * u * (1.0 + tanh)).astype(BF)
        active[rows, :] = g
        slope[rows, :] = 0.5 * (1.0 + tanh) + (0.5 * gelu_coeff) * u * (1.0 - tanh * tanh) * (
            1.0 + (3 * 0.044715) * square
        )
        part = dot(g, weights[slot + 1], ((1,), (0,)))

        @pl.when(i == 0)
        def _():
            total_a[rows, :] = part

        @pl.when(i > 0)
        def _():
            total_a[rows, :] += part

    def down_grads(i):
        for m in range(0, width, 256):
            cols = slice(m, m + 256)
            place_block(2 * i, dot(active[...], dm[:, cols], ((0,), (0,))).astype(BF), cols)

    def hidden_units_back(i, rows):
        slot = 2 * lax.rem(i, 2)
        dg = dot(dm[rows, :], weights[slot + 1], ((1,), (1,)))
        du = (dg * slope[rows, :]).astype(BF)
        active[rows, :] = du
        total = jnp.sum(du.astype(F32), axis=0, keepdims=True)
        part = dot(du, weights[slot], ((1,), (1,)))
        line = pl.ds(i, 1)
        if rows is tiles[0]:
            dup_bias[line, :] = total
        else:
            dup_bias[line, :] += total

        @pl.when(i == 0)
        def _():
            total_b[rows, :] = part

        @pl.when(i > 0)
        def _():
            total_b[rows, :] += part

    def up_grads(i):
        slot = 2 * lax.rem(i, 2)

        @pl.when(i + 2 < folds)
        def _():
            load_up(i + 2, slot).start()
            load_down(i + 2, slot + 1).start()

        @pl.when(i == folds - 1)
        def _():
            for n in range(3):
                load_qkv(n).start()

        for m in range(0, width, 256):
            cols = slice(m, m + 256)
            place_block(2 * i + 1, dot(normed_t[...], active[:, cols], ((1,), (0,))).astype(BF), cols)

    def close_hidden(rows):
        m = total_a[rows, :] + par_ref[2:3, :]
        x1 = middle[rows, :]
        out_rows[rows, :] = (x1 + gate_two * m).astype(BF)
        dy = dy_ref[rows, :].astype(F32)
        dh = total_b[rows, :]
        n2, rscale = normed_rows(x1)
        e = dh * ((1.0 + scale_two) * gain_two)
        dx1 = dy + rscale * (
            e
            - jnp.mean(e, axis=-1, keepdims=True)
            - n2 * jnp.mean(e * n2, axis=-1, keepdims=True)
        )
        middle[rows, :] = dx1
        da = (gate_one * dx1).astype(BF)
        normed_low[rows, :] = da
        for i, value in enumerate((dx1 * branch[rows, :], dh, dh * n2, dy * m)):
            total = jnp.sum(value, axis=0, keepdims=True)
            line = slice(i, i + 1)
            vec[line, :] = total if rows is tiles[0] else vec[line, :] + total
        active[rows, :] = dot(da, wout_ref[...], ((1,), (1,))).astype(BF)

    def out_grads():
        vec[4:5, :] = vec[2:3, :] * (1.0 + scale_two)
        vec[2:3, :] = vec[2:3, :] * gain_two
        for load in loads:
            load.wait()
        for m in range(0, width, 256):
            cols = slice(m, m + 256)
            place_block(
                2 * folds, dot(ot_ref[...], normed_low[:, cols], ((1,), (0,))).astype(BF), cols
            )
        row_send_all(out_rows, tokens_ref, 0)

    copies = count // 128
    lane = lax.broadcasted_iota(jnp.int32, (1, 128), 1)
    place = pl.ds(pl.multiple_of(core * count, count), count)

    def kv_copies(p):
        cols = pl.ds(pl.multiple_of(p * 128, 128), 128)
        return [
            pltpu.make_async_remote_copy(
                src_ref=away.at[:, cols],
                dst_ref=landing.at[:, cols],
                send_sem=kv_send.at[i, p],
                recv_sem=kv_recv.at[i, p],
                device_id=core_peer,
                device_id_type=MESH,
            )
            for i, (away, landing) in enumerate(((normed_low, dk_in), (dm, dv_in)))
        ]

    def attention(p, side):
        cols = pl.ds(pl.multiple_of(p * 128, 128), 128)
        q = q_ref[:, cols]
        do = active[:, cols]
        prod = ot_ref[cols, :].astype(F32) * do.astype(F32).T
        k_ref, v_ref, b_ref, dk_ref, dv_ref = (
            (kb_ref, vb_ref, bb_ref, normed_low, dm),
            (ka_ref, va_ref, ba_ref, total_a, total_b),
        )[side]
        k = k_ref[:, cols]
        v = v_ref[:, cols]
        k_t = k.T
        dk = dv = None
        for h in range(2):
            picked = (lane // HEAD) == h
            part = slice(h * HEAD, (h + 1) * HEAD)
            qm = jnp.where(picked, q, jnp.zeros_like(q))
            dom = jnp.where(picked, do, jnp.zeros_like(do))
            delta = jnp.sum(prod[part], axis=0, keepdims=True)
            s = dot(k, qm, ((1,), (1,))) + wide_of(b_ref[...], copies)
            prob = jnp.exp(s - lse_ref[p, h : h + 1, :])
            dv_h = dot(prob.astype(BF), dom, ((1,), (0,)))
            dprob = dot(v, dom, ((1,), (1,)))
            ds = (prob * (dprob - delta)).astype(BF)
            dk_h = dot(ds, qm, ((1,), (0,)))
            dq_h = dot(k_t[part], ds, ((1,), (0,)))
            dq_t[part, :] = dq_h if side == 0 else dq_t[part, :] + dq_h
            dk = dk_h if dk is None else dk + dk_h
            dv = dv_h if dv is None else dv + dv_h
        dk_ref[:, cols] = dk.astype(dk_ref.dtype)
        dv_ref[:, cols] = dv.astype(dv_ref.dtype)
        if side == 0:
            for copy in kv_copies(p):
                copy.start()
        else:
            dq = (dq_t[...] * (HEAD**-0.5)).T
            dqkv[:, cols] = rotate(dq, cos_ref[place, :], sin_ref[place, :], -1).astype(BF)

    def join():
        normed_t[...] = h_ref[...].T

        @pl.loop(0, pairs)
        def _(p):
            for copy in kv_copies(p):
                copy.wait()
            cols = pl.ds(pl.multiple_of(p * 128, 128), 128)
            dk = total_a[:, cols] + dk_in[:, cols].astype(F32)
            dv = total_b[:, cols] + dv_in[:, cols].astype(F32)
            k_cols = pl.ds(pl.multiple_of(width + p * 128, 128), 128)
            v_cols = pl.ds(pl.multiple_of(2 * width + p * 128, 128), 128)
            dqkv[:, k_cols] = rotate(dk, cos_ref[place, :], sin_ref[place, :], -1).astype(BF)
            dqkv[:, v_cols] = dv.astype(BF)

    def project_grads(n):
        for m in range(0, width, 256):
            cols = pl.ds(pl.multiple_of(n * width + m, 256), 256)
            place_block(
                2 * folds + 1 + n,
                dot(normed_t[...], dqkv[:, cols], ((1,), (0,))).astype(BF),
                slice(m, m + 256),
            )

    def finish(rows):
        if rows is tiles[0]:
            for n in range(3):
                load_qkv(n).wait()
        scale = 1.0 + part_of(mod_ref, 1, width)
        dh = sum(
            dot(dqkv[rows, n * width : (n + 1) * width], weights[n], ((1,), (1,)))
            for n in range(3)
        )
        n1, rscale = normed_rows(x_ref[rows, :].astype(F32))
        e = dh * (scale * gain_one)
        drows[rows, :] = (
            middle[rows, :]
            + rscale
            * (
                e
                - jnp.mean(e, axis=-1, keepdims=True)
                - n1 * jnp.mean(e * n1, axis=-1, keepdims=True)
            )
        ).astype(BF)
        for i, value in enumerate((dh, dh * n1)):
            total = jnp.sum(value, axis=0, keepdims=True)
            line = slice(6 + i, 7 + i)
            vec[line, :] = total if rows is tiles[0] else vec[line, :] + total

    def small_grads():
        row_send_all(drows, grad_ref, 1)
        scale = 1.0 + part_of(mod_ref, 1, width)
        srows = dsmall.shape[1]
        seqs = wide_size * groups
        seq = (wide // 2) * ring + chip
        line = lax.broadcasted_iota(jnp.int32, (pieces * srows, width), 0)
        cond = jnp.where(core == 0, cond_ref[...], 0.0)
        high = cond.astype(BF).astype(F32)
        medium = (cond - high).astype(BF).astype(F32)
        filler = jnp.zeros((1, width - 3 * TEMB), F32)
        entries = [
            (seq, vec[6:7, :]),
            (seqs + seq, vec[7:8, :] * gain_one),
            (2 * seqs + seq, vec[0:1, :]),
            (3 * seqs + seq, vec[1:2, :]),
            (4 * seqs + seq, vec[2:3, :]),
            (5 * seqs + seq, vec[3:4, :]),
            (6 * seqs + seq, jnp.concatenate([high, medium, cond - high - medium, filler], axis=1)),
            (7 * seqs, vec[7:8, :] * scale),
            (7 * seqs + 1, vec[4:5, :]),
            (7 * seqs + 2, vec[5:6, :]),
        ] + [(7 * seqs + 3 + i, dup_bias[i : i + 1, :]) for i in range(folds)]
        value = jnp.zeros((pieces * srows, width), F32)
        for at, entry in entries:
            value = jnp.where(line == at, entry, value)
        dsmall[...] = value.reshape(pieces, srows, width).astype(BF)

    prepare()
    join_at = 6 * folds + 3 + 2 * pairs
    units = []
    for n in range(2):
        for t, rows in enumerate(tiles):
            units.append((n * 3 + t, (hidden_units, hidden_units_back)[n], rows))
        units.append((n * 3 + 2, (down_grads, up_grads)[n], None))

    @pl.loop(0, chunks + gap + 3 + offsets[-1])
    def _(tick):
        for at, unit, rows in units:

            @pl.when((tick < 6 * folds) & (lax.rem(tick, 6) == at))
            def _():
                unit(tick // 6, *(() if rows is None else (rows,)))

        for t, rows in enumerate(tiles):

            @pl.when(tick == 6 * folds + t)
            def _():
                close_hidden(rows)

            @pl.when(tick == join_at + 2 + t)
            def _():
                finish(rows)

        @pl.when(tick == 6 * folds + 2)
        def _():
            out_grads()

        for side in range(2):

            @pl.when(
                (tick >= 6 * folds + 3)
                & (tick < 6 * folds + 3 + 2 * pairs)
                & (lax.rem(tick - (6 * folds + 3), 2) == side)
            )
            def _():
                attention((tick - (6 * folds + 3)) // 2, side)

        @pl.when(tick == join_at)
        def _():
            join()

        for n in range(3):

            @pl.when(tick == join_at + 1 + subs * n)
            def _():
                project_grads(n)

        @pl.when(tick == join_at + subs + 2)
        def _():
            small_grads()

        communicate(tick)

    row_wait_all(out_rows, tokens_ref, 0)
    row_wait_all(drows, grad_ref, 1)


def rest_of_block(
    x, o, ot, dy, mod, params, cosines, sines, cond, lse, wout, q, ka, va, kb, vb, h, ba, bb,
    up, down, wqkv, groups, wide_size, ring,
    lags=(3, 6, 5, 3),
):
    count, width = x.shape
    pieces = wide_size // 2 * ring
    rows = width // pieces
    half = width // 2
    sub_half = 128
    folds = up.shape[1] // width
    subs = width // 256
    blocks = 2 * folds + 4
    chunks = blocks * subs
    pairs = width // 128
    total_bits = pieces.bit_length() - 1
    first = list(lags[:3]) + [lags[3]] * (total_bits - 2)
    lags = first + first[::-1]
    assert subs * 256 == width and subs == 3
    seqs = wide_size * groups
    srows = -(-(seqs * 7 + 3 + folds) // (pieces * 8)) * 8
    sizes = [pieces >> (i + 1) for i in range(total_bits)]
    any_space = pl.BlockSpec(memory_space=pl.ANY)
    vmem = pl.BlockSpec(memory_space=pltpu.VMEM)
    block = jax.ShapeDtypeStruct((groups, count // groups, width), BF)
    rows_low = pltpu.VMEM((count, width), BF)
    rows_full = pltpu.VMEM((count, width), F32)
    lanes = pltpu.VMEM((count, 128), F32)
    return pl.pallas_call(
        functools.partial(rest_kernel, groups, wide_size, ring, tuple(lags)),
        in_specs=[vmem] * 11 + [any_space] * 11,
        out_specs=[any_space] * 4,
        out_shape=[
            jax.ShapeDtypeStruct((blocks, pieces, rows, width), BF),
            jax.ShapeDtypeStruct((pieces, srows, width), BF),
            block,
            block,
        ],
        scratch_shapes=[rows_low] * 6
        + [lanes] * 2
        + [
            pltpu.VMEM((4, width, width), BF),
            pltpu.VMEM((4, pieces, rows, width), BF),
            pltpu.VMEM((pieces, srows, width), BF),
            rows_full,
            rows_full,
            rows_low,
            pltpu.VMEM((width, count), BF),
            rows_low,
            rows_full,
            rows_full,
            rows_low,
            rows_full,
            pltpu.VMEM((128, count), F32),
            pltpu.VMEM((8, width), F32),
            pltpu.VMEM((8, width), F32),
            rows_low,
            rows_low,
            pltpu.VMEM((count, 3 * width), BF),
            rows_low,
            rows_low,
            pltpu.VMEM((chunks, pieces, rows, sub_half), BF),
            pltpu.VMEM((pieces, srows, half), BF),
            pltpu.VMEM((2 * lags[0] + 1, pieces, rows, sub_half), BF),
            pltpu.VMEM((pieces, srows, half), BF),
            [pltpu.VMEM((chunks, n, rows, sub_half), BF) for n in sizes],
            [pltpu.VMEM((n, srows, half), BF) for n in sizes],
            DMA((8,)),
            DMA((4,)),
            DMA((chunks + 1,)),
            DMA((2 + 2 * total_bits, chunks + 1)),
            DMA((2 + 2 * total_bits, chunks + 1)),
            DMA((2, pairs)),
            DMA((2, pairs)),
            DMA((2,)),
            DMA((2, groups)),
            DMA((2, groups)),
        ],
        compiler_params=pltpu.CompilerParams(
            collective_id=0, has_side_effects=True, vmem_limit_bytes=63 << 20
        ),
        name="rest_of_block",
    )(
        x, o, ot, dy, mod, params, cosines, sines, cond, lse, wout, q, ka, va, kb, vb, h, ba, bb,
        up, down, wqkv,
    )


def spread_kernel(seqs, folds, sum_ref, small_ref, ada_ref, qkv_ref, out_ref, up_ref, down_ref,
                  ada_bias_ref, gain_one_ref, gain_two_ref, up_bias_ref, down_bias_ref):
    i = pl.program_id(0)
    width = sum_ref.shape[-1]
    value = sum_ref[0].astype(F32)

    @pl.when(i < folds)
    def _():
        down_ref[...] = value

    @pl.when((i >= folds) & (i < 2 * folds))
    def _():
        up_ref[...] = value

    @pl.when(i == 2 * folds)
    def _():
        out_ref[...] = value

    @pl.when(i > 2 * folds)
    def _():
        qkv_ref[...] = value

    @pl.when(i == 0)
    def _():
        cond = small_ref[6 * seqs : 7 * seqs, : 3 * TEMB]
        for n in range(6):
            mod = small_ref[n * seqs : (n + 1) * seqs, :]
            three = dot(mod, cond, ((0,), (0,)))
            ada_ref[n * width : (n + 1) * width, :] = (
                three[:, :TEMB] + three[:, TEMB : 2 * TEMB] + three[:, 2 * TEMB :]
            )
            ada_bias_ref[n * width : (n + 1) * width] = jnp.sum(mod.astype(F32), axis=0)
        rows = small_ref[7 * seqs : 7 * seqs + 8 * (-(-(3 + folds) // 8)), :].astype(F32)
        gain_one_ref[...] = rows[0]
        gain_two_ref[...] = rows[1]
        down_bias_ref[...] = rows[2]
        for n in range(folds):
            up_bias_ref[n * width : (n + 1) * width] = rows[3 + n]


def spread(summed, small, seqs, folds):
    chunks, width = summed.shape[0], summed.shape[-1]

    def fixed(shape):
        return pl.BlockSpec(shape, lambda i: (0,) * len(shape))

    def chunk(i):
        hidden = 2 * (i % folds) + i // folds
        return jnp.where(i < 2 * folds, hidden, i)

    def at(first, size, axis):
        def index(i):
            block = jnp.clip(i - first, 0, size - 1)
            return (block, 0) if axis == 0 else (0, block)

        return pl.BlockSpec((width, width), index)

    vectors = [(6 * width,), (width,), (width,), (folds * width,), (width,)]
    return pl.pallas_call(
        functools.partial(spread_kernel, seqs, folds),
        grid=(chunks,),
        in_specs=[pl.BlockSpec((1, width, width), lambda i: (chunk(i), 0, 0)), fixed(small.shape)],
        out_specs=[
            fixed((6 * width, TEMB)),
            at(2 * folds + 1, 3, 1),
            fixed((width, width)),
            at(folds, folds, 1),
            at(0, folds, 0),
        ]
        + [fixed(shape) for shape in vectors],
        out_shape=[
            jax.ShapeDtypeStruct(shape, F32)
            for shape in [
                (6 * width, TEMB), (width, 3 * width), (width, width), (width, folds * width),
                (folds * width, width),
            ]
            + vectors
        ],
        compiler_params=pltpu.CompilerParams(vmem_limit_bytes=56 << 20),
        name="spread",
    )(summed, small)


def local(
    tokens, step_ids, prefix, keep_bits, ada_weight, ada_bias, norm1_gain, qkv_weight, out_weight,
    norm2_gain, up_weight, up_bias, down_weight, down_bias, cotangent,
):
    wide_size = lax.axis_size("wide")
    ring = lax.axis_size("narrow")
    groups, span, width = tokens.shape
    assert ring == 2 * groups and wide_size % 2 == 0
    length = ring * span
    hidden = up_weight.shape[1]
    folds = hidden // width
    seqs = wide_size * groups

    allowed = (jnp.arange(length, dtype=jnp.int32)[None, :] < prefix[:, None]) | (keep_bits == 1)
    info = jnp.concatenate(
        [jax.nn.silu(time_embed(step_ids)), jnp.where(allowed, 0.0, masked_score)], axis=1
    )[:, None, :]
    params = jnp.concatenate([norm1_gain, norm2_gain, down_bias, ada_bias, up_bias]).reshape(
        -1, width
    )
    cosines, sines = rope_tables(length)
    x, dy, h, q, ka, va, kb, vb, o, ot, lse, mod, ba, bb, cond = front(
        tokens, cotangent, qkv_weight, ada_weight, info, params, cosines, sines, ring
    )
    summed, small, outputs, input_grad = rest_of_block(
        x, o, ot, dy, mod, params, cosines, sines, cond, lse, out_weight, q, ka, va, kb, vb, h,
        ba, bb, up_weight, down_weight, qkv_weight, groups, wide_size, ring,
    )
    ada, qkv, out, up, down, ada_bias_grad, gain_one, gain_two, up_bias_grad, down_bias_grad = (
        spread(summed.reshape(-1, width, width), small.reshape(-1, width), seqs, folds)
    )
    return (
        outputs, input_grad, ada, ada_bias_grad, gain_one, qkv, out, gain_two, up, up_bias_grad,
        down, down_bias_grad,
    )


def solution(mesh):
    split = P("wide", "narrow", None)
    in_specs = (
        (split, P("wide"), P("wide"), P("wide", None)) + (P(),) * 10 + (split,)
    )
    out_specs = (split, split) + (P(),) * 10
    return jax.shard_map(local, mesh=mesh, in_specs=in_specs, out_specs=out_specs, check_vma=False)
```

```python
import functools
import math

import jax
import jax.numpy as jnp
import numpy as np
from jax import lax
from jax.experimental import pallas as pl
from jax.experimental.pallas import tpu as pltpu
from jax.sharding import PartitionSpec as P

HEAD = 64
TEMB = 128
MESH = pl.DeviceIdType.MESH
BF = jnp.bfloat16
F32 = jnp.float32
DMA = pltpu.SemaphoreType.DMA

norm_epsilon = 1e-05
gelu_coeff = 0.7978845608028654
masked_score = -1e30


def time_embed(step_ids):
    halfway = TEMB // 2
    frequency = jnp.exp(jnp.arange(halfway, dtype=F32) * (-math.log(10000.0) / halfway))
    angles = step_ids.astype(F32)[:, None] * frequency[None, :]
    return jnp.concatenate([jnp.cos(angles), jnp.sin(angles)], axis=-1)


def rope_tables(length):
    halfway = HEAD // 2
    inverse = 10000.0 ** (-2.0 * np.arange(halfway) / HEAD)
    angles = np.arange(length)[:, None] * inverse[None, :]
    sines = np.sin(angles)
    return (
        np.tile(np.cos(angles), (1, 4)).astype(np.float32),
        np.concatenate([-sines, sines, -sines, sines], axis=1).astype(np.float32),
    )


def dot(former, latter, dims):
    return lax.dot_general(former, latter, (dims, ((), ())), preferred_element_type=F32)


def rotate(values, cosines, sines, sign):
    lane = lax.broadcasted_iota(jnp.int32, (1, 128), 1)
    first = (lane % HEAD) < HEAD // 2
    parts = []
    for n in range(values.shape[1] // 128):
        part = values[:, n * 128 : (n + 1) * 128]
        partner = jnp.where(first, pltpu.roll(part, 128 - HEAD // 2, 1), pltpu.roll(part, HEAD // 2, 1))
        turned = partner * sines
        parts.append(part * cosines + (turned if sign > 0 else -turned))
    return parts[0] if len(parts) == 1 else jnp.concatenate(parts, axis=1)


def normed_rows(values):
    center = values - jnp.mean(values, axis=-1, keepdims=True)
    spread = jnp.mean(center * center, axis=-1, keepdims=True)
    scale = lax.rsqrt(spread + norm_epsilon)
    return center * scale, scale


def part_of(mod_ref, index, width):
    return mod_ref[:, index * width : (index + 1) * width]


def wide_of(block, copies):
    return jnp.concatenate([block] * copies, axis=1)


def block_kernel(
    groups, wide_size, ring, lags,
    tok_ref, cot_ref, wqkv_ref, ada_ref, wout_ref, up_ref, down_ref,
    info_ref, gain_one_ref, gain_two_ref, down_bias_ref, ada_bias_ref, up_bias_ref, cos_ref,
    sin_ref,
    sum_ref, ssum_ref, tokens_ref, grad_ref,
    x_ref, dy_ref, h_ref, q_ref, ka_ref, va_ref, kb_ref, vb_ref, o_ref, ot_ref, lse_ref, mod_ref,
    ba_ref, bb_ref, cond_ref, table, par_ref, wout,
    weights, staging, dsmall, middle, branch, normed_low, normed_t, dm, total_a, total_b, active,
    slope, dq_t, deltas, vec, dup_bias, out_rows, drows, dqkv, dk_in, dv_in,
    acc, sacc, core_in, score_in, bit_in, sbit_in,
    load_sem, weight_sem, take_self, info_send, info_recv, take_send, take_recv, swap_send,
    swap_recv, copy_sem, send_sem, recv_sem, kv_send, kv_recv, self_sem, row_send, row_recv,
):
    chunks, pieces, piece_rows = acc.shape[:3]
    slots = core_in.shape[0]
    stages = staging.shape[0]
    outer = (wide_size // 2).bit_length() - 1
    inner = ring.bit_length() - 1
    total_bits = outer + inner
    count, width = x_ref.shape
    subs = width // (2 * acc.shape[-1])
    span = count // groups
    pairs = width // 128
    folds = up_ref.shape[1] // width
    early = (2 * folds + 1) * subs
    wide = lax.axis_index("wide")
    chip = lax.axis_index("narrow")
    core = lax.rem(wide, 2)
    base = wide - core
    core_peer = (base + 1 - core, chip)
    dims = []
    for b in range(outer):
        bit = lax.rem(wide // (2 << b), 2)
        dims.append((bit, wide + (1 - 2 * bit) * (2 << b), chip))
    for b in range(inner):
        bit = lax.rem(chip // (1 << b), 2)
        dims.append((bit, wide, chip + (1 - 2 * bit) * (1 << b)))
    up = list(range(outer))
    rest = list(range(outer, total_bits))
    orders = (up + rest, up[::-1] + rest, rest + up)

    def load_up(i, slot):
        cols = pl.ds(pl.multiple_of(i * width, width), width)
        return pltpu.make_async_copy(up_ref.at[:, cols], weights.at[slot], weight_sem.at[slot])

    def load_down(i, slot):
        rows = pl.ds(pl.multiple_of(i * width, width), width)
        return pltpu.make_async_copy(down_ref.at[rows], weights.at[slot], weight_sem.at[slot])

    def load_qkv(n):
        cols = pl.ds(n * width, width)
        return pltpu.make_async_copy(wqkv_ref.at[:, cols], weights.at[n], weight_sem.at[n])

    load_ada = [
        pltpu.make_async_copy(
            ada_ref.at[pl.ds(n * width, width)],
            weights.at[3, :, pl.ds(n * TEMB, TEMB)],
            load_sem.at[1 + n],
        )
        for n in range(6)
    ]
    load_out = pltpu.make_async_copy(wout_ref, wout, load_sem.at[0])

    barrier = pltpu.get_barrier_semaphore()
    for d in dims[:outer]:
        pl.semaphore_signal(barrier, inc=1, device_id=d[1:], device_id_type=MESH)
    for c in range(2):
        for d in range(ring):
            if c or d:
                other = (base + lax.rem(core + c, 2), lax.rem(chip + d, ring))
                pl.semaphore_signal(barrier, inc=1, device_id=other, device_id_type=MESH)
    for load in load_ada:
        load.start()
    for n in range(3):
        load_qkv(n).start()
    load_out.start()
    pl.semaphore_wait(barrier, outer + 2 * ring - 1)

    slot = lax.rem(chip, groups)
    home = chip // groups
    rows_out = pl.ds(pl.multiple_of(slot * span, span), span)

    def move(src, dst, kind, g):
        remote = pltpu.make_async_remote_copy(
            src_ref=src.at[g],
            dst_ref=dst.at[rows_out],
            send_sem=take_send.at[kind, g],
            recv_sem=take_recv.at[kind, slot],
            device_id=(base + home, core * groups + g),
            device_id_type=MESH,
        )
        here = pltpu.make_async_copy(src.at[g], dst.at[rows_out], take_self.at[kind])
        own = (home == core) & (slot == g)
        return remote, here, own

    def send(src, dst, kind):
        for g in range(groups):
            remote, here, own = move(src, dst, kind, g)

            @pl.when(own)
            def _():
                here.start()

            @pl.when(jnp.logical_not(own))
            def _():
                remote.start()

    def sent(src, dst, kind):
        for g in range(groups):
            remote, here, own = move(src, dst, kind, g)

            @pl.when(jnp.logical_not(own))
            def _():
                remote.wait_send()

    def arrive(src, dst, kind, j):
        rows = pl.ds(j * span, span)
        own = (home == core) & (slot == j)

        @pl.when(own)
        def _():
            pltpu.make_async_copy(src.at[0], dst.at[rows], take_self.at[kind]).wait()

        @pl.when(jnp.logical_not(own))
        def _():
            pltpu.make_async_remote_copy(
                src_ref=src.at[0],
                dst_ref=dst.at[rows],
                send_sem=take_send.at[kind, 0],
                recv_sem=take_recv.at[kind, j],
                device_id=core_peer,
                device_id_type=MESH,
            ).wait_recv()

    send(tok_ref, x_ref, 0)
    par_ref[0:1, :] = gain_one_ref[...].reshape(1, width)
    par_ref[1:2, :] = gain_two_ref[...].reshape(1, width)
    par_ref[2:3, :] = down_bias_ref[...].reshape(1, width)
    for i in range(6):
        par_ref[3 + i : 4 + i, :] = ada_bias_ref[i * width : (i + 1) * width].reshape(1, width)
    for i in range(folds):
        par_ref[9 + i : 10 + i, :] = up_bias_ref[i * width : (i + 1) * width].reshape(1, width)
    table[core] = info_ref[...]
    swap_info = pltpu.make_async_remote_copy(
        src_ref=info_ref,
        dst_ref=table.at[core],
        send_sem=info_send,
        recv_sem=info_recv,
        device_id=core_peer,
        device_id_type=MESH,
    )
    swap_info.start()
    swap_info.wait()
    row = table[home, pl.ds(slot, 1), :]
    length = row.shape[1] - TEMB
    cond_ref[...] = row[:, :TEMB]
    bias = jnp.where(core == 0, row[:, TEMB : TEMB + count], row[:, TEMB + count : TEMB + length])
    ba_ref[...] = jnp.broadcast_to(bias, (128, count)).T
    bias = jnp.where(core == 1, row[:, TEMB : TEMB + count], row[:, TEMB + count : TEMB + length])
    bb_ref[...] = jnp.broadcast_to(bias, (128, count)).T

    cond = jnp.broadcast_to(row[:, :TEMB], (16, TEMB))
    high = cond.astype(BF).astype(F32)
    medium = (cond - high).astype(BF).astype(F32)
    low = cond - high - medium
    line = lax.broadcasted_iota(jnp.int32, (16, TEMB), 0)
    three = jnp.where(
        line == 0, high, jnp.where(line == 1, medium, jnp.where(line == 2, low, 0.0))
    ).astype(BF)
    for load in load_ada:
        load.wait()
    for i in range(6):
        cols = slice(i * width, (i + 1) * width)
        mod_ref[:, cols] = (
            jnp.sum(dot(three, weights[3, :, i * TEMB : (i + 1) * TEMB], ((1,), (1,))), axis=0, keepdims=True)
            + par_ref[3 + i : 4 + i, :]
        )
    shift = part_of(mod_ref, 0, width)
    scale = par_ref[0:1, :] * (1.0 + part_of(mod_ref, 1, width))

    for n in range(3):
        load_qkv(n).wait()
    swaps = []
    for j in range(groups):
        rows = pl.ds(j * span, span)
        arrive(tok_ref, x_ref, 0, j)
        if j == groups - 1:
            send(cot_ref, dy_ref, 1)
        normed, _ = normed_rows(x_ref[rows, :].astype(F32))
        h_ref[rows, :] = (normed * scale + shift).astype(BF)
        place = pl.ds(pl.multiple_of(core * count + j * span, span), span)
        cosines = cos_ref[place, :]
        sines = sin_ref[place, :]
        step = 256
        for n in (2, 1, 0):
            target = (q_ref, ka_ref, va_ref)[n]
            for m in range(width // step):
                cols = slice(m * step, (m + 1) * step)
                block = dot(h_ref[rows, :], weights[n, :, cols], ((1,), (0,)))
                if n < 2:
                    block = rotate(block, cosines, sines, 1)
                if n == 0:
                    block = block * HEAD**-0.5
                target[rows, m * step : (m + 1) * step] = block.astype(BF)
            if n > 0:
                swap = pltpu.make_async_remote_copy(
                    src_ref=target.at[rows],
                    dst_ref=(kb_ref, vb_ref)[n - 1].at[rows],
                    send_sem=swap_send.at[n - 1, j],
                    recv_sem=swap_recv.at[n - 1, j],
                    device_id=core_peer,
                    device_id_type=MESH,
                )
                swap.start()
                swaps.append(swap)
    for i in range(2):
        load_up(i, 2 * i).start()
        load_down(i, 2 * i + 1).start()
    for swap in swaps:
        swap.wait()

    copies = count // 128
    lane = lax.broadcasted_iota(jnp.int32, (1, 128), 1)

    @pl.loop(0, width // 128)
    def _(p):
        cols = pl.ds(pl.multiple_of(p * 128, 128), 128)
        q = q_ref[:, cols]
        ka = ka_ref[:, cols]
        kb = kb_ref[:, cols]
        va_t = va_ref[:, cols].T
        vb_t = vb_ref[:, cols].T
        outs = []
        for h in range(2):
            qm = jnp.where((lane // HEAD) == h, q, jnp.zeros_like(q))
            sa = dot(ka, qm, ((1,), (1,))) + wide_of(ba_ref[...], copies)
            sb = dot(kb, qm, ((1,), (1,))) + wide_of(bb_ref[...], copies)
            top = jnp.maximum(jnp.max(sa, axis=0, keepdims=True), jnp.max(sb, axis=0, keepdims=True))
            pa = jnp.exp(sa - top)
            pb = jnp.exp(sb - top)
            total = jnp.sum(pa, axis=0, keepdims=True) + jnp.sum(pb, axis=0, keepdims=True)
            part = slice(h * HEAD, (h + 1) * HEAD)
            out = dot(va_t[part], pa.astype(BF), ((1,), (0,))) + dot(
                vb_t[part], pb.astype(BF), ((1,), (0,))
            )
            outs.append(out / total)
            lse_ref[p, h : h + 1, :] = top + jnp.log(total)
        both = jnp.concatenate(outs, axis=0)
        ot_ref[cols, :] = both.astype(BF)
        o_ref[:, cols] = both.T.astype(BF)

    sent(tok_ref, x_ref, 0)
    for j in range(groups):
        arrive(cot_ref, dy_ref, 1, j)
    load_out.wait()

    parts = 8
    part_rows = span // parts

    def row_move(src, dst, kind, j, q):
        rows = pl.ds(pl.multiple_of(j * span + q * part_rows, part_rows), part_rows)
        place = dst.at[slot, pl.ds(pl.multiple_of(q * part_rows, part_rows), part_rows)]
        remote = pltpu.make_async_remote_copy(
            src_ref=src.at[rows],
            dst_ref=place,
            send_sem=row_send.at[kind, j, q],
            recv_sem=row_recv.at[kind, slot, q],
            device_id=(base + home, core * groups + j),
            device_id_type=MESH,
        )
        here = pltpu.make_async_copy(src.at[rows], place, self_sem.at[kind, q])
        own = (home == core) & (slot == j)
        return remote, here, own

    def row_send_part(src, dst, kind, q):
        for j in range(groups):
            remote, here, own = row_move(src, dst, kind, j, q)

            @pl.when(own)
            def _():
                here.start()

            @pl.when(jnp.logical_not(own))
            def _():
                remote.start()

    def row_wait_part(src, dst, kind, q):
        for j in range(groups):
            remote, here, own = row_move(src, dst, kind, j, q)

            @pl.when(own)
            def _():
                here.wait()

            @pl.when(jnp.logical_not(own))
            def _():
                remote.wait_send()

        rows = pl.ds(pl.multiple_of(q * part_rows, part_rows), part_rows)
        for g in range(groups):
            own = (home == core) & (slot == g)

            @pl.when(jnp.logical_not(own))
            def _():
                pltpu.make_async_remote_copy(
                    src_ref=src.at[rows],
                    dst_ref=dst.at[g, rows],
                    send_sem=row_send.at[kind, 0, q],
                    recv_sem=row_recv.at[kind, g, q],
                    device_id=core_peer,
                    device_id_type=MESH,
                ).wait_recv()

    def plan(kind):
        late = kind // 4
        odd = lax.rem(kind, 2) * (1 - late)
        low = 0
        size = pieces
        steps = []
        for i in range(total_bits):
            bit, peer_wide, peer_here = (
                a + odd * (b - a) + late * (c - a)
                for a, b, c in zip(*(dims[order[i]] for order in orders))
            )
            size //= 2
            before = low
            low = low + bit * size
            steps.append((before + (1 - bit) * size, low, size, (peer_wide, peer_here)))
        return steps

    def stage(step, kind, sem, lane_base, big, out, total, core_slot, bit_slots):
        cols = total.shape[-1]
        mine = pl.ds(pl.multiple_of(lane_base + core * cols, 128), cols)
        other = pl.ds(pl.multiple_of(lane_base + (1 - core) * cols, 128), cols)
        steps = plan(kind)

        def remote(src, dst, index, peer):
            return pltpu.make_async_remote_copy(
                src_ref=src,
                dst_ref=dst,
                send_sem=send_sem.at[index, sem],
                recv_sem=recv_sem.at[index, sem],
                device_id=peer,
                device_id_type=MESH,
            )

        def core_copy():
            return remote(big.at[:, :, other], core_slot, 0, core_peer)

        def own_copy():
            return pltpu.make_async_copy(big.at[:, :, mine], total, copy_sem.at[sem])

        def bit_copy(i):
            away, _, size, peer = steps[i]
            return remote(total.at[pl.ds(away, size)], bit_slots[i], 1 + i, peer)

        def back_copy(i):
            _, keep, size, peer = steps[i]
            place = out.at[pl.ds(keep, size), :, mine]
            if i == total_bits - 1:
                return remote(total.at[pl.ds(keep, size)], place, 1 + total_bits + i, peer)
            return remote(place, place, 1 + total_bits + i, peer)

        def keep_copy():
            _, keep, size, _ = steps[-1]
            return pltpu.make_async_copy(
                total.at[pl.ds(keep, size)], out.at[pl.ds(keep, size), :, mine], copy_sem.at[sem]
            )

        def core_back():
            place = out.at[:, :, mine]
            return remote(place, place, 1 + 2 * total_bits, core_peer)

        def add(start, size, from_slot):
            @pl.loop(0, size)
            def _(j):
                total[start + j] = (total[start + j].astype(F32) + from_slot[j].astype(F32)).astype(BF)

        if step == 0:
            core_copy().start()
            own_copy().start()
        elif step == 1:
            own_copy().wait()
            core_copy().wait()
            add(0, pieces, core_slot)
            bit_copy(0).start()
        elif step <= total_bits + 1:
            i = step - 2
            bit_copy(i).wait()
            add(steps[i][1], steps[i][2], bit_slots[i])
            if step <= total_bits:
                bit_copy(i + 1).start()
            else:
                keep_copy().start()
                back_copy(i).start()
        elif step <= 2 * total_bits:
            i = 2 * total_bits + 1 - step
            if i == total_bits - 1:
                keep_copy().wait()
            back_copy(i).wait()
            back_copy(i - 1).start()
        elif step == 2 * total_bits + 1:
            back_copy(0).wait()
            core_back().start()
        else:
            core_back().wait()

    last = 2 * total_bits + 2
    offsets = [sum(lags[:step]) for step in range(last + 1)]
    turn = 2 * (pairs // subs) + subs
    lead = 6 * folds + 3
    late = lead + turn - 2
    closing = lead + subs * turn + 1

    def communicate(tick):
        for step in range(last, -1, -1):
            at = tick - offsets[step]

            def move_on(chunk, block, sub):
                stage(
                    step, lax.rem(chunk, 2) + lax.rem(chunk, 12) // 11 * 3, chunk,
                    sub * 2 * acc.shape[-1],
                    staging.at[lax.rem(block, stages)], sum_ref.at[block], acc.at[chunk],
                    core_in.at[lax.rem(chunk, slots)], [ref.at[chunk] for ref in bit_in],
                )

            @pl.when((at >= 2) & (at < 2 + early))
            def _():
                move_on(at - 2, (at - 2) // subs, lax.rem(at - 2, subs))

            since = at - late
            part = lax.rem(since, turn)

            @pl.when((since >= 0) & (since < subs * turn) & (part < 3))
            def _():
                group = since // turn
                move_on(early + group * 3 + part, 2 * folds + 1 + part, group)

            @pl.when(at == closing + 2)
            def _():
                stage(step, 0, chunks, 0, dsmall, ssum_ref, sacc, score_in, sbit_in)

    def place_block(block, value, cols):
        for i in range(pieces):
            staging[lax.rem(block, stages), i, :, cols] = value[
                i * piece_rows : (i + 1) * piece_rows
            ]

    tile = min(256, count)
    tiles = [slice(r, r + tile) for r in range(0, count, tile)]
    gain_one = par_ref[0:1, :]
    gain_two = par_ref[1:2, :]
    shift_two, scale_two, gate_one, gate_two = (part_of(mod_ref, i, width) for i in (3, 4, 2, 5))

    def prepare():
        total = 0.0
        for rows in tiles:
            a = dot(o_ref[rows, :], wout[...], ((1,), (0,)))
            branch[rows, :] = a
            x1 = x_ref[rows, :].astype(F32) + gate_one * a
            middle[rows, :] = x1
            normed, _ = normed_rows(x1)
            h2 = (normed * (gain_two * (1.0 + scale_two)) + shift_two).astype(BF)
            normed_low[rows, :] = h2
            normed_t[:, rows] = h2.T
            dm_rows = (dy_ref[rows, :].astype(F32) * gate_two).astype(BF)
            dm[rows, :] = dm_rows
            total = total + jnp.sum(dm_rows.astype(F32), axis=0, keepdims=True)
        vec[5:6, :] = total

    def hidden_units(i, rows):
        slot = 2 * lax.rem(i, 2)
        if rows is tiles[0]:
            load_up(i, slot).wait()
            load_down(i, slot + 1).wait()
        bias = par_ref[pl.ds(9 + i, 1), :]
        u = dot(normed_low[rows, :], weights[slot], ((1,), (0,))) + bias
        square = u * u
        tanh = jnp.tanh(gelu_coeff * (u + 0.044715 * u * square))
        g = (0.5 * u * (1.0 + tanh)).astype(BF)
        active[rows, :] = g
        slope[rows, :] = 0.5 * (1.0 + tanh) + (0.5 * gelu_coeff) * u * (1.0 - tanh * tanh) * (
            1.0 + (3 * 0.044715) * square
        )
        part = dot(g, weights[slot + 1], ((1,), (0,)))

        @pl.when(i == 0)
        def _():
            total_a[rows, :] = part

        @pl.when(i > 0)
        def _():
            total_a[rows, :] += part

    def down_grads(i):
        for m in range(0, width, 256):
            cols = slice(m, m + 256)
            place_block(2 * i, dot(active[...], dm[:, cols], ((0,), (0,))).astype(BF), cols)

    def hidden_units_back(i, rows):
        slot = 2 * lax.rem(i, 2)
        dg = dot(dm[rows, :], weights[slot + 1], ((1,), (1,)))
        du = (dg * slope[rows, :]).astype(BF)
        active[rows, :] = du
        total = jnp.sum(du.astype(F32), axis=0, keepdims=True)
        part = dot(du, weights[slot], ((1,), (1,)))
        line = pl.ds(i, 1)
        if rows is tiles[0]:
            dup_bias[line, :] = total
        else:
            dup_bias[line, :] += total

        @pl.when(i == 0)
        def _():
            total_b[rows, :] = part

        @pl.when(i > 0)
        def _():
            total_b[rows, :] += part

    def up_grads(i):
        slot = 2 * lax.rem(i, 2)

        @pl.when(i + 2 < folds)
        def _():
            load_up(i + 2, slot).start()
            load_down(i + 2, slot + 1).start()

        @pl.when(i == folds - 1)
        def _():
            for n in range(3):
                load_qkv(n).start()

        for m in range(0, width, 256):
            cols = slice(m, m + 256)
            place_block(2 * i + 1, dot(normed_t[...], active[:, cols], ((1,), (0,))).astype(BF), cols)

    def close_hidden(rows):
        m = total_a[rows, :] + par_ref[2:3, :]
        x1 = middle[rows, :]
        out_rows[rows, :] = (x1 + gate_two * m).astype(BF)
        dy = dy_ref[rows, :].astype(F32)
        dh = total_b[rows, :]
        n2, rscale = normed_rows(x1)
        e = dh * ((1.0 + scale_two) * gain_two)
        dx1 = dy + rscale * (
            e
            - jnp.mean(e, axis=-1, keepdims=True)
            - n2 * jnp.mean(e * n2, axis=-1, keepdims=True)
        )
        middle[rows, :] = dx1
        da = (gate_one * dx1).astype(BF)
        normed_low[rows, :] = da
        for i, value in enumerate((dx1 * branch[rows, :], dh, dh * n2, dy * m)):
            total = jnp.sum(value, axis=0, keepdims=True)
            line = slice(i, i + 1)
            vec[line, :] = total if rows is tiles[0] else vec[line, :] + total
        active[rows, :] = dot(da, wout[...], ((1,), (1,))).astype(BF)

    def out_grads():
        vec[4:5, :] = vec[2:3, :] * (1.0 + scale_two)
        vec[2:3, :] = vec[2:3, :] * gain_two
        for m in range(0, width, 256):
            cols = slice(m, m + 256)
            place_block(
                2 * folds, dot(ot_ref[...], normed_low[:, cols], ((1,), (0,))).astype(BF), cols
            )

    place = pl.ds(pl.multiple_of(core * count, count), count)

    def kv_copies(p):
        cols = pl.ds(pl.multiple_of(p * 128, 128), 128)
        return [
            pltpu.make_async_remote_copy(
                src_ref=away.at[:, cols],
                dst_ref=landing.at[:, cols],
                send_sem=kv_send.at[i, p],
                recv_sem=kv_recv.at[i, p],
                device_id=core_peer,
                device_id_type=MESH,
            )
            for i, (away, landing) in enumerate(((normed_low, dk_in), (dm, dv_in)))
        ]

    def attention(p, side):
        cols = pl.ds(pl.multiple_of(p * 128, 128), 128)
        q = q_ref[:, cols]
        do = active[:, cols]
        if side == 0:
            prod = ot_ref[cols, :].astype(F32) * do.astype(F32).T
        k_ref, v_ref, b_ref, dk_ref, dv_ref = (
            (kb_ref, vb_ref, bb_ref, normed_low, dm),
            (ka_ref, va_ref, ba_ref, total_a, total_b),
        )[side]
        k = k_ref[:, cols]
        v = v_ref[:, cols]
        k_t = k.T
        dk = dv = None
        for h in range(2):
            picked = (lane // HEAD) == h
            part = slice(h * HEAD, (h + 1) * HEAD)
            qm = jnp.where(picked, q, jnp.zeros_like(q))
            dom = jnp.where(picked, do, jnp.zeros_like(do))
            if side == 0:
                deltas[h : h + 1, :] = jnp.sum(prod[part], axis=0, keepdims=True)
            delta = deltas[h : h + 1, :]
            s = dot(k, qm, ((1,), (1,))) + wide_of(b_ref[...], copies)
            prob = jnp.exp(s - lse_ref[p, h : h + 1, :])
            dv_h = dot(prob.astype(BF), dom, ((1,), (0,)))
            dprob = dot(v, dom, ((1,), (1,)))
            ds = (prob * (dprob - delta)).astype(BF)
            dk_h = dot(ds, qm, ((1,), (0,)))
            dq_h = dot(k_t[part], ds, ((1,), (0,)))
            dq_t[part, :] = dq_h if side == 0 else dq_t[part, :] + dq_h
            dk = dk_h if dk is None else dk + dk_h
            dv = dv_h if dv is None else dv + dv_h
        dk_ref[:, cols] = dk.astype(dk_ref.dtype)
        dv_ref[:, cols] = dv.astype(dv_ref.dtype)
        if side == 0:
            for copy in kv_copies(p):
                copy.start()
        else:
            dq = (dq_t[...] * (HEAD**-0.5)).T
            dqkv[:, cols] = rotate(dq, cos_ref[place, :], sin_ref[place, :], -1).astype(BF)

    def join(group):
        for i in range(pairs // subs):
            p = group * (pairs // subs) + i
            for copy in kv_copies(p):
                copy.wait()
            cols = pl.ds(pl.multiple_of(p * 128, 128), 128)
            dk = total_a[:, cols] + dk_in[:, cols].astype(F32)
            dv = total_b[:, cols] + dv_in[:, cols].astype(F32)
            k_cols = pl.ds(pl.multiple_of(width + p * 128, 128), 128)
            v_cols = pl.ds(pl.multiple_of(2 * width + p * 128, 128), 128)
            dqkv[:, k_cols] = rotate(dk, cos_ref[place, :], sin_ref[place, :], -1).astype(BF)
            dqkv[:, v_cols] = dv.astype(BF)

    def project_grads(group, n):
        cols = pl.ds(pl.multiple_of(n * width + group * 256, 256), 256)
        value = dot(normed_t[...], dqkv[:, cols], ((1,), (0,))).astype(BF)
        place_block(
            2 * folds + 1 + n, value, pl.ds(pl.multiple_of(group * 256, 256), 256)
        )

    def finish(rows):
        if rows is tiles[0]:
            for n in range(3):
                load_qkv(n).wait()
        scale = 1.0 + part_of(mod_ref, 1, width)
        dh = sum(
            dot(dqkv[rows, n * width : (n + 1) * width], weights[n], ((1,), (1,)))
            for n in range(3)
        )
        n1, rscale = normed_rows(x_ref[rows, :].astype(F32))
        e = dh * (scale * gain_one)
        drows[rows, :] = (
            middle[rows, :]
            + rscale
            * (
                e
                - jnp.mean(e, axis=-1, keepdims=True)
                - n1 * jnp.mean(e * n1, axis=-1, keepdims=True)
            )
        ).astype(BF)
        for i, value in enumerate((dh, dh * n1)):
            total = jnp.sum(value, axis=0, keepdims=True)
            line = slice(6 + i, 7 + i)
            vec[line, :] = total if rows is tiles[0] else vec[line, :] + total

    def small_grads():
        scale = 1.0 + part_of(mod_ref, 1, width)
        srows = dsmall.shape[1]
        seqs = wide_size * groups
        seq = (wide // 2) * ring + chip
        line = lax.broadcasted_iota(jnp.int32, (pieces * srows, width), 0)
        cond = jnp.where(core == 0, cond_ref[...], 0.0)
        high = cond.astype(BF).astype(F32)
        medium = (cond - high).astype(BF).astype(F32)
        filler = jnp.zeros((1, width - 3 * TEMB), F32)
        entries = [
            (seq, vec[6:7, :]),
            (seqs + seq, vec[7:8, :] * gain_one),
            (2 * seqs + seq, vec[0:1, :]),
            (3 * seqs + seq, vec[1:2, :]),
            (4 * seqs + seq, vec[2:3, :]),
            (5 * seqs + seq, vec[3:4, :]),
            (6 * seqs + seq, jnp.concatenate([high, medium, cond - high - medium, filler], axis=1)),
            (7 * seqs, vec[7:8, :] * scale),
            (7 * seqs + 1, vec[4:5, :]),
            (7 * seqs + 2, vec[5:6, :]),
        ] + [(7 * seqs + 3 + i, dup_bias[i : i + 1, :]) for i in range(folds)]
        value = jnp.zeros((pieces * srows, width), F32)
        for at, entry in entries:
            value = jnp.where(line == at, entry, value)
        dsmall[...] = value.reshape(pieces, srows, width).astype(BF)

    prepare()
    units = []
    for n in range(2):
        for t, rows in enumerate(tiles):
            units.append((n * 3 + t, (hidden_units, hidden_units_back)[n], rows))
        units.append((n * 3 + 2, (down_grads, up_grads)[n], None))

    @pl.loop(0, closing + 3 + offsets[-1])
    def _(tick):
        for at, unit, rows in units:

            @pl.when((tick < 6 * folds) & (lax.rem(tick, 6) == at))
            def _():
                unit(tick // 6, *(() if rows is None else (rows,)))

        for t, rows in enumerate(tiles):

            @pl.when(tick == 6 * folds + t)
            def _():
                close_hidden(rows)

            @pl.when(tick == closing + t)
            def _():
                finish(rows)

        @pl.when(tick == 6 * folds + 2)
        def _():
            out_grads()
            normed_t[...] = h_ref[...].T

        since = tick - lead
        part = lax.rem(since, turn)
        for at in range(2 * (pairs // subs)):

            @pl.when((since >= 0) & (since < subs * turn) & (part == at))
            def _():
                attention(since // turn * (pairs // subs) + at // 2, at % 2)

        back = tick - late + 1
        back_part = lax.rem(back, turn)

        @pl.when((back >= 0) & (back < subs * turn) & (back_part == 0))
        def _():
            join(back // turn)

        for n in range(3):

            @pl.when((back >= 0) & (back < subs * turn) & (back_part == 1 + n))
            def _():
                project_grads(back // turn, n)

        @pl.when(tick == closing + 2)
        def _():
            small_grads()

        for kind, (src, dst, first) in enumerate(
            ((out_rows, tokens_ref, 6 * folds + 2), (drows, grad_ref, closing + 2))
        ):

            @pl.when(
                (tick >= first) & (tick < first + 2 * parts) & (lax.rem(tick - first, 2) == 0)
            )
            def _():
                row_send_part(src, dst, kind, (tick - first) // 2)

        communicate(tick)

    sent(cot_ref, dy_ref, 1)

    @pl.loop(0, parts)
    def _(q):
        row_wait_part(out_rows, tokens_ref, 0, q)
        row_wait_part(drows, grad_ref, 1, q)


def whole_block(
    tokens, cotangent, wqkv, ada, wout, up, down, info, gain_one, gain_two, down_bias, ada_bias,
    up_bias, cosines, sines, wide_size, ring,
    lags=(2, 4, 3, 2),
):
    groups, span, width = tokens.shape
    count = groups * span
    pieces = wide_size // 2 * ring
    rows = width // pieces
    half = width // 2
    folds = up.shape[1] // width
    subs = width // 256
    blocks = 2 * folds + 4
    chunks = blocks * subs
    pairs = width // 128
    total_bits = pieces.bit_length() - 1
    first = list(lags[:3]) + [lags[3]] * (total_bits - 2)
    lags = tuple(first + first[::-1])
    assert subs * 256 == width and subs == 3 and sum(lags) > 16
    seqs = wide_size * groups
    srows = -(-(seqs * 7 + 3 + folds) // (pieces * 8)) * 8
    sizes = [pieces >> (i + 1) for i in range(total_bits)]
    any_space = pl.BlockSpec(memory_space=pl.ANY)
    vmem = pl.BlockSpec(memory_space=pltpu.VMEM)
    block = jax.ShapeDtypeStruct((groups, span, width), BF)
    rows_low = pltpu.VMEM((count, width), BF)
    rows_full = pltpu.VMEM((count, width), F32)
    lanes = pltpu.VMEM((count, 128), F32)
    turned = pltpu.VMEM((width, count), BF)
    vectors = pltpu.VMEM((8, width), F32)
    return pl.pallas_call(
        functools.partial(block_kernel, groups, wide_size, ring, lags),
        in_specs=[any_space] * 7 + [vmem] * 8,
        out_specs=[any_space] * 4,
        out_shape=[
            jax.ShapeDtypeStruct((blocks, pieces, rows, width), BF),
            jax.ShapeDtypeStruct((pieces, srows, width), BF),
            block,
            block,
        ],
        scratch_shapes=[rows_low] * 9
        + [
            turned,
            pltpu.VMEM((pairs, 8, count), F32),
            pltpu.VMEM((1, 6 * width), F32),
            lanes,
            lanes,
            pltpu.VMEM((1, TEMB), F32),
            pltpu.VMEM((2,) + info.shape, F32),
            pltpu.VMEM((-(-(9 + folds) // 8) * 8, width), F32),
            pltpu.VMEM((width, width), BF),
            pltpu.VMEM((4, width, width), BF),
            pltpu.VMEM((4, pieces, rows, width), BF),
            pltpu.VMEM((pieces, srows, width), BF),
            rows_full,
            rows_full,
            rows_low,
            turned,
            rows_low,
            rows_full,
            rows_full,
            rows_low,
            rows_full,
            pltpu.VMEM((128, count), F32),
            pltpu.VMEM((8, count), F32),
            vectors,
            vectors,
            rows_low,
            rows_low,
            pltpu.VMEM((count, 3 * width), BF),
            rows_low,
            rows_low,
            pltpu.VMEM((chunks, pieces, rows, 128), BF),
            pltpu.VMEM((pieces, srows, half), BF),
            pltpu.VMEM((2 * lags[0] + 1, pieces, rows, 128), BF),
            pltpu.VMEM((pieces, srows, half), BF),
            [pltpu.VMEM((chunks, n, rows, 128), BF) for n in sizes],
            [pltpu.VMEM((n, srows, half), BF) for n in sizes],
            DMA((7,)),
            DMA((4,)),
            DMA((2,)),
            DMA,
            DMA,
            DMA((2, groups)),
            DMA((2, groups)),
            DMA((2, groups)),
            DMA((2, groups)),
            DMA((chunks + 1,)),
            DMA((2 + 2 * total_bits, chunks + 1)),
            DMA((2 + 2 * total_bits, chunks + 1)),
            DMA((2, pairs)),
            DMA((2, pairs)),
            DMA((2, 8)),
            DMA((2, groups, 8)),
            DMA((2, groups, 8)),
        ],
        compiler_params=pltpu.CompilerParams(
            collective_id=0, has_side_effects=True, vmem_limit_bytes=63 << 20
        ),
        name="whole_block",
    )(
        tokens, cotangent, wqkv, ada, wout, up, down, info, gain_one, gain_two, down_bias, ada_bias,
        up_bias, cosines, sines,
    )


def spread_kernel(
    seqs, folds,
    sum_ref, small_ref,
    ada_ref, qkv_ref, out_ref, up_ref, down_ref,
    ada_bias_ref, gain_one_ref, gain_two_ref, up_bias_ref, down_bias_ref,
    taken, wide, take_sem, give_sem,
):
    blocks, width = sum_ref.shape[0], sum_ref.shape[-1]
    order = list(range(blocks))
    takes = [pltpu.make_async_copy(sum_ref.at[n], taken.at[n], take_sem.at[n]) for n in order]
    for take in takes:
        take.start()
    cond = small_ref[6 * seqs : 7 * seqs, : 3 * TEMB]
    for n in range(6):
        mod = small_ref[n * seqs : (n + 1) * seqs, :]
        three = dot(mod, cond, ((0,), (0,)))
        ada_ref[n * width : (n + 1) * width, :] = (
            three[:, :TEMB] + three[:, TEMB : 2 * TEMB] + three[:, 2 * TEMB :]
        )
        ada_bias_ref[n * width : (n + 1) * width] = jnp.sum(mod.astype(F32), axis=0)
    rows = small_ref[7 * seqs : 7 * seqs + 8 * (-(-(3 + folds) // 8)), :].astype(F32)
    gain_one_ref[...] = rows[0]
    gain_two_ref[...] = rows[1]
    down_bias_ref[...] = rows[2]
    for n in range(folds):
        up_bias_ref[n * width : (n + 1) * width] = rows[3 + n]

    gives = []
    for n in order:
        if n < 2 * folds:
            whole = pl.ds(n // 2 * width, width)
            place = up_ref.at[:, whole] if n % 2 else down_ref.at[whole]
        elif n == 2 * folds:
            place = out_ref
        else:
            place = qkv_ref.at[:, pl.ds((n - 2 * folds - 1) * width, width)]
        gives.append(pltpu.make_async_copy(wide.at[n], place, give_sem.at[n]))
        takes[n].wait()

        @pl.loop(0, width // 32)
        def _(r):
            lines = pl.ds(pl.multiple_of(r * 32, 32), 32)
            wide[n, lines, :] = taken[n, lines, :].astype(F32)

        gives[n].start()
    for give in gives:
        give.wait()


def spread(summed, small, seqs, folds):
    blocks, width = summed.shape[0], summed.shape[-1]
    any_space = pl.BlockSpec(memory_space=pl.ANY)
    vmem = pl.BlockSpec(memory_space=pltpu.VMEM)
    shapes = [
        (6 * width, TEMB), (width, 3 * width), (width, width), (width, folds * width),
        (folds * width, width), (6 * width,), (width,), (width,), (folds * width,), (width,),
    ]
    return pl.pallas_call(
        functools.partial(spread_kernel, seqs, folds),
        in_specs=[any_space, vmem],
        out_specs=[vmem] + [any_space] * 4 + [vmem] * 5,
        out_shape=[jax.ShapeDtypeStruct(shape, F32) for shape in shapes],
        scratch_shapes=[
            pltpu.VMEM((blocks, width, width), BF),
            pltpu.VMEM((blocks, width, width), F32),
            DMA((blocks,)),
            DMA((blocks,)),
        ],
        compiler_params=pltpu.CompilerParams(vmem_limit_bytes=60 << 20),
        name="spread",
    )(summed, small)


def local(
    tokens, step_ids, prefix, keep_bits, ada_weight, ada_bias, norm1_gain, qkv_weight, out_weight,
    norm2_gain, up_weight, up_bias, down_weight, down_bias, cotangent,
):
    wide_size = lax.axis_size("wide")
    ring = lax.axis_size("narrow")
    groups, span, width = tokens.shape
    assert ring == 2 * groups and wide_size % 2 == 0
    length = ring * span
    hidden = up_weight.shape[1]
    folds = hidden // width
    seqs = wide_size * groups

    allowed = (jnp.arange(length, dtype=jnp.int32)[None, :] < prefix[:, None]) | (keep_bits == 1)
    info = jnp.concatenate(
        [jax.nn.silu(time_embed(step_ids)), jnp.where(allowed, 0.0, masked_score)], axis=1
    )
    cosines, sines = rope_tables(length)
    summed, small, outputs, input_grad = whole_block(
        tokens, cotangent, qkv_weight, ada_weight, out_weight, up_weight, down_weight, info,
        norm1_gain, norm2_gain, down_bias, ada_bias, up_bias, cosines, sines, wide_size, ring,
    )
    ada, qkv, out, up, down, ada_bias_grad, gain_one, gain_two, up_bias_grad, down_bias_grad = (
        spread(summed.reshape(-1, width, width), small.reshape(-1, width), seqs, folds)
    )
    return (
        outputs, input_grad, ada, ada_bias_grad, gain_one, qkv, out, gain_two, up, up_bias_grad,
        down, down_bias_grad,
    )


def solution(mesh):
    split = P("wide", "narrow", None)
    in_specs = (
        (split, P("wide"), P("wide"), P("wide", None)) + (P(),) * 10 + (split,)
    )
    out_specs = (split, split) + (P(),) * 10
    return jax.shard_map(local, mesh=mesh, in_specs=in_specs, out_specs=out_specs, check_vma=False)
```

```python
import functools
import math

import jax
import jax.numpy as jnp
import numpy as np
from jax import lax
from jax.experimental import pallas as pl
from jax.experimental.pallas import tpu as pltpu
from jax.sharding import PartitionSpec as P

HEAD = 64
TEMB = 128
MESH = pl.DeviceIdType.MESH
BF = jnp.bfloat16
F32 = jnp.float32
DMA = pltpu.SemaphoreType.DMA

norm_epsilon = 1e-05
gelu_coeff = 0.7978845608028654
masked_score = -1e30
EARLY = (2, 6, 5, 5, 3)
LATE = (2, 4, 3)


def time_embed(step_ids):
    halfway = TEMB // 2
    frequency = jnp.exp(jnp.arange(halfway, dtype=F32) * (-math.log(10000.0) / halfway))
    angles = step_ids.astype(F32)[:, None] * frequency[None, :]
    return jnp.concatenate([jnp.cos(angles), jnp.sin(angles)], axis=-1)


def rope_tables(length):
    halfway = HEAD // 2
    inverse = 10000.0 ** (-2.0 * np.arange(halfway) / HEAD)
    angles = np.arange(length)[:, None] * inverse[None, :]
    sines = np.sin(angles)
    return (
        np.tile(np.cos(angles), (1, 4)).astype(np.float32),
        np.concatenate([-sines, sines, -sines, sines], axis=1).astype(np.float32),
    )


def dot(former, latter, dims):
    return lax.dot_general(former, latter, (dims, ((), ())), preferred_element_type=F32)


def rotate(values, cosines, sines, sign):
    lane = lax.broadcasted_iota(jnp.int32, (1, 128), 1)
    first = (lane % HEAD) < HEAD // 2
    parts = []
    for n in range(values.shape[1] // 128):
        part = values[:, n * 128 : (n + 1) * 128]
        partner = jnp.where(first, pltpu.roll(part, 128 - HEAD // 2, 1), pltpu.roll(part, HEAD // 2, 1))
        turned = partner * sines
        parts.append(part * cosines + (turned if sign > 0 else -turned))
    return parts[0] if len(parts) == 1 else jnp.concatenate(parts, axis=1)


def normed_rows(values):
    center = values - jnp.mean(values, axis=-1, keepdims=True)
    spread = jnp.mean(center * center, axis=-1, keepdims=True)
    scale = lax.rsqrt(spread + norm_epsilon)
    return center * scale, scale


def part_of(mod_ref, index, width):
    return mod_ref[:, index * width : (index + 1) * width]


def wide_of(block, copies):
    return jnp.concatenate([block] * copies, axis=1)


def block_kernel(
    groups, wide_size, ring, early_lags, late_lags,
    tok_ref, cot_ref, wqkv_ref, ada_ref, wout_ref, up_ref, down_ref,
    info_ref, gain_one_ref, gain_two_ref, down_bias_ref, ada_bias_ref, up_bias_ref, cos_ref,
    sin_ref,
    sum_ref, ssum_ref, tokens_ref, grad_ref,
    x_ref, dy_ref, h_ref, q_ref, ka_ref, va_ref, kb_ref, vb_ref, o_ref, ot_ref, lse_ref, mod_ref,
    ba_ref, bb_ref, cond_ref, table, par_ref, wout,
    weights, staging, dsmall, middle, branch, normed_low, normed_t, dm, total_a, total_b, active,
    slope, dq_t, deltas, vec, dup_bias, out_rows, drows, dqkv, dk_in, dv_in,
    early_buffers, late_buffers, small_buffers,
    load_sem, weight_sem, take_self, info_send, info_recv, take_send, take_recv, swap_send,
    swap_recv, copy_sem, send_sem, recv_sem, ring_send, ring_recv, gather_send, gather_recv, kv_send, kv_recv, self_sem, row_send, row_recv,
):
    early, subs, pieces, piece_rows = early_buffers[0].shape[:4]
    late_count = late_buffers[0].shape[0]
    stages = staging.shape[0]
    outer = (wide_size // 2).bit_length() - 1
    count, width = x_ref.shape
    span = count // groups
    pairs = width // 128
    folds = up_ref.shape[1] // width
    wide = lax.axis_index("wide")
    chip = lax.axis_index("narrow")
    core = lax.rem(wide, 2)
    base = wide - core
    core_peer = (base + 1 - core, chip)
    dims = []
    for b in range(outer):
        bit = lax.rem(wide // (2 << b), 2)
        dims.append((bit, wide + (1 - 2 * bit) * (2 << b), chip))

    def load_up(i, slot):
        cols = pl.ds(pl.multiple_of(i * width, width), width)
        return pltpu.make_async_copy(up_ref.at[:, cols], weights.at[slot], weight_sem.at[slot])

    def load_down(i, slot):
        rows = pl.ds(pl.multiple_of(i * width, width), width)
        return pltpu.make_async_copy(down_ref.at[rows], weights.at[slot], weight_sem.at[slot])

    def load_qkv(n):
        cols = pl.ds(n * width, width)
        return pltpu.make_async_copy(wqkv_ref.at[:, cols], weights.at[n], weight_sem.at[n])

    load_ada = [
        pltpu.make_async_copy(
            ada_ref.at[pl.ds(n * width, width)],
            weights.at[3, :, pl.ds(n * TEMB, TEMB)],
            load_sem.at[1 + n],
        )
        for n in range(6)
    ]
    load_out = pltpu.make_async_copy(wout_ref, wout, load_sem.at[0])

    barrier = pltpu.get_barrier_semaphore()
    for d in dims[:outer]:
        pl.semaphore_signal(barrier, inc=1, device_id=d[1:], device_id_type=MESH)
    for c in range(2):
        for d in range(ring):
            if c or d:
                other = (base + lax.rem(core + c, 2), lax.rem(chip + d, ring))
                pl.semaphore_signal(barrier, inc=1, device_id=other, device_id_type=MESH)
    for load in load_ada:
        load.start()
    for n in range(3):
        load_qkv(n).start()
    load_out.start()
    pl.semaphore_wait(barrier, outer + 2 * ring - 1)

    slot = lax.rem(chip, groups)
    home = chip // groups
    rows_out = pl.ds(pl.multiple_of(slot * span, span), span)

    def move(src, dst, kind, g):
        remote = pltpu.make_async_remote_copy(
            src_ref=src.at[g],
            dst_ref=dst.at[rows_out],
            send_sem=take_send.at[kind, g],
            recv_sem=take_recv.at[kind, slot],
            device_id=(base + home, core * groups + g),
            device_id_type=MESH,
        )
        here = pltpu.make_async_copy(src.at[g], dst.at[rows_out], take_self.at[kind])
        own = (home == core) & (slot == g)
        return remote, here, own

    def send(src, dst, kind):
        for g in range(groups):
            remote, here, own = move(src, dst, kind, g)

            @pl.when(own)
            def _():
                here.start()

            @pl.when(jnp.logical_not(own))
            def _():
                remote.start()

    def sent(src, dst, kind):
        for g in range(groups):
            remote, here, own = move(src, dst, kind, g)

            @pl.when(jnp.logical_not(own))
            def _():
                remote.wait_send()

    def arrive(src, dst, kind, j):
        rows = pl.ds(j * span, span)
        own = (home == core) & (slot == j)

        @pl.when(own)
        def _():
            pltpu.make_async_copy(src.at[0], dst.at[rows], take_self.at[kind]).wait()

        @pl.when(jnp.logical_not(own))
        def _():
            pltpu.make_async_remote_copy(
                src_ref=src.at[0],
                dst_ref=dst.at[rows],
                send_sem=take_send.at[kind, 0],
                recv_sem=take_recv.at[kind, j],
                device_id=core_peer,
                device_id_type=MESH,
            ).wait_recv()

    send(tok_ref, x_ref, 0)
    par_ref[0:1, :] = gain_one_ref[...].reshape(1, width)
    par_ref[1:2, :] = gain_two_ref[...].reshape(1, width)
    par_ref[2:3, :] = down_bias_ref[...].reshape(1, width)
    for i in range(6):
        par_ref[3 + i : 4 + i, :] = ada_bias_ref[i * width : (i + 1) * width].reshape(1, width)
    for i in range(folds):
        par_ref[9 + i : 10 + i, :] = up_bias_ref[i * width : (i + 1) * width].reshape(1, width)
    table[core] = info_ref[...]
    swap_info = pltpu.make_async_remote_copy(
        src_ref=info_ref,
        dst_ref=table.at[core],
        send_sem=info_send,
        recv_sem=info_recv,
        device_id=core_peer,
        device_id_type=MESH,
    )
    swap_info.start()
    swap_info.wait()
    row = table[home, pl.ds(slot, 1), :]
    length = row.shape[1] - TEMB
    cond_ref[...] = row[:, :TEMB]
    bias = jnp.where(core == 0, row[:, TEMB : TEMB + count], row[:, TEMB + count : TEMB + length])
    ba_ref[...] = jnp.broadcast_to(bias, (128, count)).T
    bias = jnp.where(core == 1, row[:, TEMB : TEMB + count], row[:, TEMB + count : TEMB + length])
    bb_ref[...] = jnp.broadcast_to(bias, (128, count)).T

    cond = jnp.broadcast_to(row[:, :TEMB], (16, TEMB))
    high = cond.astype(BF).astype(F32)
    medium = (cond - high).astype(BF).astype(F32)
    low = cond - high - medium
    line = lax.broadcasted_iota(jnp.int32, (16, TEMB), 0)
    three = jnp.where(
        line == 0, high, jnp.where(line == 1, medium, jnp.where(line == 2, low, 0.0))
    ).astype(BF)
    for load in load_ada:
        load.wait()
    for i in range(6):
        cols = slice(i * width, (i + 1) * width)
        mod_ref[:, cols] = (
            jnp.sum(dot(three, weights[3, :, i * TEMB : (i + 1) * TEMB], ((1,), (1,))), axis=0, keepdims=True)
            + par_ref[3 + i : 4 + i, :]
        )
    shift = part_of(mod_ref, 0, width)
    scale = par_ref[0:1, :] * (1.0 + part_of(mod_ref, 1, width))

    for n in range(3):
        load_qkv(n).wait()
    swaps = []
    for j in range(groups):
        rows = pl.ds(j * span, span)
        arrive(tok_ref, x_ref, 0, j)
        if j == groups - 1:
            send(cot_ref, dy_ref, 1)
        normed, _ = normed_rows(x_ref[rows, :].astype(F32))
        h_ref[rows, :] = (normed * scale + shift).astype(BF)
        place = pl.ds(pl.multiple_of(core * count + j * span, span), span)
        cosines = cos_ref[place, :]
        sines = sin_ref[place, :]
        step = 256
        for n in (2, 1, 0):
            target = (q_ref, ka_ref, va_ref)[n]
            for m in range(width // step):
                cols = slice(m * step, (m + 1) * step)
                block = dot(h_ref[rows, :], weights[n, :, cols], ((1,), (0,)))
                if n < 2:
                    block = rotate(block, cosines, sines, 1)
                if n == 0:
                    block = block * HEAD**-0.5
                target[rows, m * step : (m + 1) * step] = block.astype(BF)
            if n > 0:
                swap = pltpu.make_async_remote_copy(
                    src_ref=target.at[rows],
                    dst_ref=(kb_ref, vb_ref)[n - 1].at[rows],
                    send_sem=swap_send.at[n - 1, j],
                    recv_sem=swap_recv.at[n - 1, j],
                    device_id=core_peer,
                    device_id_type=MESH,
                )
                swap.start()
                swaps.append(swap)
    for i in range(2):
        load_up(i, 2 * i).start()
        load_down(i, 2 * i + 1).start()
    for swap in swaps:
        swap.wait()

    copies = count // 128
    lane = lax.broadcasted_iota(jnp.int32, (1, 128), 1)

    @pl.loop(0, width // 128)
    def _(p):
        cols = pl.ds(pl.multiple_of(p * 128, 128), 128)
        q = q_ref[:, cols]
        ka = ka_ref[:, cols]
        kb = kb_ref[:, cols]
        va_t = va_ref[:, cols].T
        vb_t = vb_ref[:, cols].T
        outs = []
        for h in range(2):
            qm = jnp.where((lane // HEAD) == h, q, jnp.zeros_like(q))
            sa = dot(ka, qm, ((1,), (1,))) + wide_of(ba_ref[...], copies)
            sb = dot(kb, qm, ((1,), (1,))) + wide_of(bb_ref[...], copies)
            top = jnp.maximum(jnp.max(sa, axis=0, keepdims=True), jnp.max(sb, axis=0, keepdims=True))
            pa = jnp.exp(sa - top)
            pb = jnp.exp(sb - top)
            total = jnp.sum(pa, axis=0, keepdims=True) + jnp.sum(pb, axis=0, keepdims=True)
            part = slice(h * HEAD, (h + 1) * HEAD)
            out = dot(va_t[part], pa.astype(BF), ((1,), (0,))) + dot(
                vb_t[part], pb.astype(BF), ((1,), (0,))
            )
            outs.append(out / total)
            lse_ref[p, h : h + 1, :] = top + jnp.log(total)
        both = jnp.concatenate(outs, axis=0)
        ot_ref[cols, :] = both.astype(BF)
        o_ref[:, cols] = both.T.astype(BF)

    sent(tok_ref, x_ref, 0)
    for j in range(groups):
        arrive(cot_ref, dy_ref, 1, j)
    load_out.wait()

    parts = 8
    part_rows = span // parts

    def row_move(src, dst, kind, j, q):
        rows = pl.ds(pl.multiple_of(j * span + q * part_rows, part_rows), part_rows)
        place = dst.at[slot, pl.ds(pl.multiple_of(q * part_rows, part_rows), part_rows)]
        remote = pltpu.make_async_remote_copy(
            src_ref=src.at[rows],
            dst_ref=place,
            send_sem=row_send.at[kind, j, q],
            recv_sem=row_recv.at[kind, slot, q],
            device_id=(base + home, core * groups + j),
            device_id_type=MESH,
        )
        here = pltpu.make_async_copy(src.at[rows], place, self_sem.at[kind, q])
        own = (home == core) & (slot == j)
        return remote, here, own

    def row_send_part(src, dst, kind, q):
        for j in range(groups):
            remote, here, own = row_move(src, dst, kind, j, q)

            @pl.when(own)
            def _():
                here.start()

            @pl.when(jnp.logical_not(own))
            def _():
                remote.start()

    def row_wait_part(src, dst, kind, q):
        for j in range(groups):
            remote, here, own = row_move(src, dst, kind, j, q)

            @pl.when(own)
            def _():
                here.wait()

            @pl.when(jnp.logical_not(own))
            def _():
                remote.wait_send()

        rows = pl.ds(pl.multiple_of(q * part_rows, part_rows), part_rows)
        for g in range(groups):
            own = (home == core) & (slot == g)

            @pl.when(jnp.logical_not(own))
            def _():
                pltpu.make_async_remote_copy(
                    src_ref=src.at[rows],
                    dst_ref=dst.at[g, rows],
                    send_sem=row_send.at[kind, 0, q],
                    recv_sem=row_recv.at[kind, g, q],
                    device_id=core_peer,
                    device_id_type=MESH,
                ).wait_recv()

    last = 2 * outer + 4

    def stage(step, odd, sem, pick, source, out, total, core_slot, ring_slot, bit_slots):
        low = 0
        size = pieces
        steps = []
        for i in range(outer):
            (bit, peer_wide, _), (other_bit, other_wide, _) = dims[i], dims[outer - 1 - i]
            bit = bit + odd * (other_bit - bit)
            peer_wide = peer_wide + odd * (other_wide - peer_wide)
            size //= 2
            before = low
            low = low + bit * size
            steps.append((before + (1 - bit) * size, low, size, (peer_wide, chip)))
        final = low + chip

        def remote(src, dst, index, peer):
            return pltpu.make_async_remote_copy(
                src_ref=src,
                dst_ref=dst,
                send_sem=send_sem.at[index, sem],
                recv_sem=recv_sem.at[index, sem],
                device_id=peer,
                device_id_type=MESH,
            )

        def core_copy():
            return remote(source(1 - core), core_slot, 0, core_peer)

        def own_copy():
            return pltpu.make_async_copy(source(core), total, copy_sem.at[sem])

        def bit_copy(i):
            away, _, size, peer = steps[i]
            return remote(pick(total, away, size), bit_slots[i], 1 + i, peer)

        def ring_copies():
            copies = []
            for d in range(1, ring):
                target = lax.rem(chip + d, ring)
                copies.append(
                    pltpu.make_async_remote_copy(
                        src_ref=pick(total, low + target, 1),
                        dst_ref=ring_slot.at[d - 1],
                        send_sem=ring_send.at[d - 1, sem],
                        recv_sem=ring_recv.at[d - 1, sem],
                        device_id=(wide, target),
                        device_id_type=MESH,
                    )
                )
            return copies

        def gather_copies():
            return [
                pltpu.make_async_remote_copy(
                    src_ref=pick(total, final, 1),
                    dst_ref=pick(out(core), final, 1),
                    send_sem=gather_send.at[d - 1, sem],
                    recv_sem=gather_recv.at[d - 1, sem],
                    device_id=(wide, lax.rem(chip + d, ring)),
                    device_id_type=MESH,
                )
                for d in range(1, ring)
            ]

        def keep_copy():
            return pltpu.make_async_copy(
                pick(total, final, 1), pick(out(core), final, 1), copy_sem.at[sem]
            )

        def back_copy(i):
            _, keep, size, peer = steps[i]
            place = pick(out(core), keep, size)
            return remote(place, place, 1 + outer + i, peer)

        def core_back():
            return remote(out(core), out(core), 1 + 2 * outer, core_peer)

        def add(start, size, slot):
            place = pick(total, start, size)
            place[...] = place[...] + slot[...]

        if step == 0:
            core_copy().start()
            own_copy().start()
        elif step == 1:
            own_copy().wait()
            core_copy().wait()
            total[...] = total[...] + core_slot[...]
            bit_copy(0).start()
        elif step <= outer + 1:
            i = step - 2
            bit_copy(i).wait()
            add(steps[i][1], steps[i][2], bit_slots[i])
            if step <= outer:
                bit_copy(i + 1).start()
            else:
                for copy in ring_copies():
                    copy.start()
        elif step == outer + 2:
            for copy in ring_copies():
                copy.wait()
            place = pick(total, final, 1)
            value = place[...].astype(F32)
            for d in range(1, ring):
                value = value + ring_slot[d - 1].astype(F32)
            place[...] = value.astype(BF)
            keep_copy().start()
            for copy in gather_copies():
                copy.start()
        elif step == outer + 3:
            keep_copy().wait()
            for copy in gather_copies():
                copy.wait()
            back_copy(outer - 1).start()
        elif step <= 2 * outer + 2:
            i = 2 * outer + 2 - step
            back_copy(i + 1).wait()
            back_copy(i).start()
        elif step == 2 * outer + 3:
            back_copy(0).wait()
            core_back().start()
        else:
            core_back().wait()

    early_at = [2 + sum(early_lags[:step]) for step in range(last + 1)]
    late_at = [sum(late_lags[:step]) for step in range(last + 1)]
    turn = 2 * (pairs // subs) + subs
    lead = 6 * folds + 3
    late = lead + turn - 2
    closing = lead + subs * turn + 1

    def pick_early(ref, start, size):
        return ref.at[:, pl.ds(start, size)]

    def pick_late(ref, start, size):
        return ref.at[pl.ds(start, size)]

    early_end = 3 * early + early_at[-1]

    def move_early(tick):
        turn_now = lax.rem(tick, 3)
        for step in range(last, -1, -1):
            since = tick - early_at[step]

            @pl.when(
                (since >= 0) & (since < 3 * early) & (turn_now == early_at[step] % 3)
            )
            def _():
                chunk = lax.div(since, 3)
                total, core_slots, ring_slots, bit_slots = early_buffers
                stage(
                    step, lax.rem(chunk, 2), chunk, pick_early,
                    lambda half: staging.at[lax.rem(chunk, stages), :, half],
                    lambda half: sum_ref.at[chunk, :, half],
                    total.at[chunk], core_slots.at[lax.rem(chunk, 2)], ring_slots.at[chunk],
                    [ref.at[chunk] for ref in bit_slots],
                )

    def move_late(tick):
        turn_now = lax.rem(tick, turn)
        for step in range(last, -1, -1):
            at = tick - late_at[step] - late
            zero = (late_at[step] + late) % turn
            on = [turn_now == (zero + n) % turn for n in range(3)]

            @pl.when((at >= 0) & (at < subs * turn) & (on[0] | on[1] | on[2]))
            def _():
                group = lax.div(at, turn)
                part = at - group * turn
                chunk = group * 3 + part
                block = early + part
                total, core_slots, ring_slots, bit_slots = late_buffers
                stage(
                    step, lax.rem(chunk, 2), early + chunk, pick_late,
                    lambda half: staging.at[lax.rem(block, stages), group, half],
                    lambda half: sum_ref.at[block, group, half],
                    total.at[chunk], core_slots.at[lax.rem(chunk, core_slots.shape[0])],
                    ring_slots.at[chunk], [ref.at[chunk] for ref in bit_slots],
                )

            @pl.when(tick == closing + 2 + late_at[step])
            def _():
                stage(
                    step, 0, early + late_count, pick_late,
                    lambda half: dsmall.at[half], lambda half: ssum_ref.at[half], *small_buffers
                )

    def place_block(block, part, value):
        for half in range(2):
            lanes = slice(half * 128, (half + 1) * 128)
            for i in range(pieces):
                staging[lax.rem(block, stages), part, half, i] = value[
                    i * piece_rows : (i + 1) * piece_rows, lanes
                ]

    tile = min(256, count)
    tiles = [slice(r, r + tile) for r in range(0, count, tile)]
    gain_one = par_ref[0:1, :]
    gain_two = par_ref[1:2, :]
    shift_two, scale_two, gate_one, gate_two = (part_of(mod_ref, i, width) for i in (3, 4, 2, 5))

    def prepare():
        total = 0.0
        for rows in tiles:
            a = dot(o_ref[rows, :], wout[...], ((1,), (0,)))
            branch[rows, :] = a.astype(BF)
            x1 = x_ref[rows, :].astype(F32) + gate_one * a
            middle[rows, :] = x1
            normed, _ = normed_rows(x1)
            h2 = (normed * (gain_two * (1.0 + scale_two)) + shift_two).astype(BF)
            normed_low[rows, :] = h2
            normed_t[:, rows] = h2.T
            dm_rows = (dy_ref[rows, :].astype(F32) * gate_two).astype(BF)
            dm[rows, :] = dm_rows
            total = total + jnp.sum(dm_rows.astype(F32), axis=0, keepdims=True)
        vec[5:6, :] = total

    def hidden_units(i, rows):
        slot = 2 * lax.rem(i, 2)
        if rows is tiles[0]:
            load_up(i, slot).wait()
            load_down(i, slot + 1).wait()
        bias = par_ref[pl.ds(9 + i, 1), :]
        u = dot(normed_low[rows, :], weights[slot], ((1,), (0,))) + bias
        square = u * u
        tanh = jnp.tanh(gelu_coeff * (u + 0.044715 * u * square))
        g = (0.5 * u * (1.0 + tanh)).astype(BF)
        active[rows, :] = g
        slope[rows, :] = 0.5 * (1.0 + tanh) + (0.5 * gelu_coeff) * u * (1.0 - tanh * tanh) * (
            1.0 + (3 * 0.044715) * square
        )
        part = dot(g, weights[slot + 1], ((1,), (0,)))

        @pl.when(i == 0)
        def _():
            total_a[rows, :] = part

        @pl.when(i > 0)
        def _():
            total_a[rows, :] += part

    def down_grads(i):
        for m in range(0, width, 256):
            cols = slice(m, m + 256)
            place_block(
                2 * i, m // 256, dot(active[...], dm[:, cols], ((0,), (0,))).astype(BF)
            )

    def hidden_units_back(i, rows):
        slot = 2 * lax.rem(i, 2)
        dg = dot(dm[rows, :], weights[slot + 1], ((1,), (1,)))
        du = (dg * slope[rows, :]).astype(BF)
        active[rows, :] = du
        total = jnp.sum(du.astype(F32), axis=0, keepdims=True)
        part = dot(du, weights[slot], ((1,), (1,)))
        line = pl.ds(i, 1)
        if rows is tiles[0]:
            dup_bias[line, :] = total
        else:
            dup_bias[line, :] += total

        @pl.when(i == 0)
        def _():
            total_b[rows, :] = part

        @pl.when(i > 0)
        def _():
            total_b[rows, :] += part

    def up_grads(i):
        slot = 2 * lax.rem(i, 2)

        @pl.when(i + 2 < folds)
        def _():
            load_up(i + 2, slot).start()
            load_down(i + 2, slot + 1).start()

        @pl.when(i == folds - 1)
        def _():
            for n in range(3):
                load_qkv(n).start()

        for m in range(0, width, 256):
            cols = slice(m, m + 256)
            place_block(
                2 * i + 1, m // 256, dot(normed_t[...], active[:, cols], ((1,), (0,))).astype(BF)
            )

    def close_hidden(rows):
        m = total_a[rows, :] + par_ref[2:3, :]
        x1 = middle[rows, :]
        out_rows[rows, :] = (x1 + gate_two * m).astype(BF)
        dy = dy_ref[rows, :].astype(F32)
        dh = total_b[rows, :]
        n2, rscale = normed_rows(x1)
        e = dh * ((1.0 + scale_two) * gain_two)
        dx1 = dy + rscale * (
            e
            - jnp.mean(e, axis=-1, keepdims=True)
            - n2 * jnp.mean(e * n2, axis=-1, keepdims=True)
        )
        middle[rows, :] = dx1
        da = (gate_one * dx1).astype(BF)
        normed_low[rows, :] = da
        for i, value in enumerate((dx1 * branch[rows, :].astype(F32), dh, dh * n2, dy * m)):
            total = jnp.sum(value, axis=0, keepdims=True)
            line = slice(i, i + 1)
            vec[line, :] = total if rows is tiles[0] else vec[line, :] + total
        active[rows, :] = dot(da, wout[...], ((1,), (1,))).astype(BF)

    def out_grads():
        vec[4:5, :] = vec[2:3, :] * (1.0 + scale_two)
        vec[2:3, :] = vec[2:3, :] * gain_two
        for m in range(0, width, 256):
            cols = slice(m, m + 256)
            place_block(
                2 * folds, m // 256, dot(ot_ref[...], normed_low[:, cols], ((1,), (0,))).astype(BF)
            )

    place = pl.ds(pl.multiple_of(core * count, count), count)

    def kv_copies(p):
        cols = pl.ds(pl.multiple_of(p * 128, 128), 128)
        return [
            pltpu.make_async_remote_copy(
                src_ref=away.at[:, cols],
                dst_ref=landing.at[:, cols],
                send_sem=kv_send.at[i, p],
                recv_sem=kv_recv.at[i, p],
                device_id=core_peer,
                device_id_type=MESH,
            )
            for i, (away, landing) in enumerate(((normed_low, dk_in), (dm, dv_in)))
        ]

    def attention(p, side):
        cols = pl.ds(pl.multiple_of(p * 128, 128), 128)
        q = q_ref[:, cols]
        do = active[:, cols]
        if side == 0:
            prod = ot_ref[cols, :].astype(F32) * do.astype(F32).T
        k_ref, v_ref, b_ref, dk_ref, dv_ref = (
            (kb_ref, vb_ref, bb_ref, normed_low, dm),
            (ka_ref, va_ref, ba_ref, total_a, total_b),
        )[side]
        k = k_ref[:, cols]
        v = v_ref[:, cols]
        k_t = k.T
        dk = dv = None
        for h in range(2):
            picked = (lane // HEAD) == h
            part = slice(h * HEAD, (h + 1) * HEAD)
            qm = jnp.where(picked, q, jnp.zeros_like(q))
            dom = jnp.where(picked, do, jnp.zeros_like(do))
            if side == 0:
                deltas[h : h + 1, :] = jnp.sum(prod[part], axis=0, keepdims=True)
            delta = deltas[h : h + 1, :]
            s = dot(k, qm, ((1,), (1,))) + wide_of(b_ref[...], copies)
            prob = jnp.exp(s - lse_ref[p, h : h + 1, :])
            dv_h = dot(prob.astype(BF), dom, ((1,), (0,)))
            dprob = dot(v, dom, ((1,), (1,)))
            ds = (prob * (dprob - delta)).astype(BF)
            dk_h = dot(ds, qm, ((1,), (0,)))
            dq_h = dot(k_t[part], ds, ((1,), (0,)))
            dq_t[part, :] = dq_h if side == 0 else dq_t[part, :] + dq_h
            dk = dk_h if dk is None else dk + dk_h
            dv = dv_h if dv is None else dv + dv_h
        dk_ref[:, cols] = dk.astype(dk_ref.dtype)
        dv_ref[:, cols] = dv.astype(dv_ref.dtype)
        if side == 0:
            for copy in kv_copies(p):
                copy.start()
        else:
            dq = (dq_t[...] * (HEAD**-0.5)).T
            dqkv[:, cols] = rotate(dq, cos_ref[place, :], sin_ref[place, :], -1).astype(BF)

    def join(group):
        for i in range(pairs // subs):
            p = group * (pairs // subs) + i
            for copy in kv_copies(p):
                copy.wait()
            cols = pl.ds(pl.multiple_of(p * 128, 128), 128)
            dk = total_a[:, cols] + dk_in[:, cols].astype(F32)
            dv = total_b[:, cols] + dv_in[:, cols].astype(F32)
            k_cols = pl.ds(pl.multiple_of(width + p * 128, 128), 128)
            v_cols = pl.ds(pl.multiple_of(2 * width + p * 128, 128), 128)
            dqkv[:, k_cols] = rotate(dk, cos_ref[place, :], sin_ref[place, :], -1).astype(BF)
            dqkv[:, v_cols] = dv.astype(BF)

    def project_grads(group, n):
        cols = pl.ds(pl.multiple_of(n * width + group * 256, 256), 256)
        value = dot(normed_t[...], dqkv[:, cols], ((1,), (0,))).astype(BF)
        place_block(early + n, group, value)

    def finish(rows):
        if rows is tiles[0]:
            for n in range(3):
                load_qkv(n).wait()
        scale = 1.0 + part_of(mod_ref, 1, width)
        dh = sum(
            dot(dqkv[rows, n * width : (n + 1) * width], weights[n], ((1,), (1,)))
            for n in range(3)
        )
        n1, rscale = normed_rows(x_ref[rows, :].astype(F32))
        e = dh * (scale * gain_one)
        drows[rows, :] = (
            middle[rows, :]
            + rscale
            * (
                e
                - jnp.mean(e, axis=-1, keepdims=True)
                - n1 * jnp.mean(e * n1, axis=-1, keepdims=True)
            )
        ).astype(BF)
        for i, value in enumerate((dh, dh * n1)):
            total = jnp.sum(value, axis=0, keepdims=True)
            line = slice(6 + i, 7 + i)
            vec[line, :] = total if rows is tiles[0] else vec[line, :] + total

    def small_grads():
        scale = 1.0 + part_of(mod_ref, 1, width)
        srows = dsmall.shape[2]
        seqs = wide_size * groups
        seq = (wide // 2) * ring + chip
        line = lax.broadcasted_iota(jnp.int32, (pieces * srows, width), 0)
        cond = jnp.where(core == 0, cond_ref[...], 0.0)
        high = cond.astype(BF).astype(F32)
        medium = (cond - high).astype(BF).astype(F32)
        filler = jnp.zeros((1, width - 3 * TEMB), F32)
        entries = [
            (seq, vec[6:7, :]),
            (seqs + seq, vec[7:8, :] * gain_one),
            (2 * seqs + seq, vec[0:1, :]),
            (3 * seqs + seq, vec[1:2, :]),
            (4 * seqs + seq, vec[2:3, :]),
            (5 * seqs + seq, vec[3:4, :]),
            (6 * seqs + seq, jnp.concatenate([high, medium, cond - high - medium, filler], axis=1)),
            (7 * seqs, vec[7:8, :] * scale),
            (7 * seqs + 1, vec[4:5, :]),
            (7 * seqs + 2, vec[5:6, :]),
        ] + [(7 * seqs + 3 + i, dup_bias[i : i + 1, :]) for i in range(folds)]
        value = jnp.zeros((pieces * srows, width), F32)
        for at, entry in entries:
            value = jnp.where(line == at, entry, value)
        for half in range(2):
            lanes = slice(half * (width // 2), (half + 1) * (width // 2))
            dsmall[half] = value[:, lanes].reshape(pieces, srows, width // 2).astype(BF)

    prepare()
    units = []
    for n in range(2):
        for t, rows in enumerate(tiles):
            units.append((n * 3 + t, (hidden_units, hidden_units_back)[n], rows))
        units.append((n * 3 + 2, (down_grads, up_grads)[n], None))

    @pl.loop(0, closing + 3 + late_at[-1])
    def _(tick):
        @pl.when(tick < 6 * folds)
        def _():
            i = lax.div(tick, 6)
            turn_now = tick - 6 * i
            for at, unit, rows in units:

                @pl.when(turn_now == at)
                def _():
                    unit(i, *(() if rows is None else (rows,)))

        @pl.when((tick >= 6 * folds) & (tick < lead))
        def _():
            for t, rows in enumerate(tiles):

                @pl.when(tick == 6 * folds + t)
                def _():
                    close_hidden(rows)

            @pl.when(tick == 6 * folds + 2)
            def _():
                out_grads()
                normed_t[...] = h_ref[...].T

        @pl.when((tick >= lead) & (tick < lead + subs * turn))
        def _():
            since = tick - lead
            group = lax.div(since, turn)
            part = since - group * turn
            for at in range(2 * (pairs // subs)):

                @pl.when(part == at)
                def _():
                    attention(group * (pairs // subs) + at // 2, at % 2)

        @pl.when((tick >= late - 1) & (tick < late - 1 + subs * turn))
        def _():
            since = tick - late + 1
            group = lax.div(since, turn)
            part = since - group * turn

            @pl.when(part == 0)
            def _():
                join(group)

            for n in range(3):

                @pl.when(part == 1 + n)
                def _():
                    project_grads(group, n)

        @pl.when((tick >= closing) & (tick < closing + 3))
        def _():
            for t, rows in enumerate(tiles):

                @pl.when(tick == closing + t)
                def _():
                    finish(rows)

            @pl.when(tick == closing + 2)
            def _():
                small_grads()

        for kind, (src, dst, first) in enumerate(
            ((out_rows, tokens_ref, 6 * folds + 2), (drows, grad_ref, closing + 2))
        ):

            @pl.when(
                (tick >= first) & (tick < first + 2 * parts) & (lax.rem(tick - first, 2) == 0)
            )
            def _():
                row_send_part(src, dst, kind, (tick - first) // 2)

        @pl.when(tick < early_end)
        def _():
            move_early(tick)

        @pl.when(tick >= late)
        def _():
            move_late(tick)

    sent(cot_ref, dy_ref, 1)

    @pl.loop(0, parts)
    def _(q):
        row_wait_part(out_rows, tokens_ref, 0, q)
        row_wait_part(drows, grad_ref, 1, q)


def whole_block(
    tokens, cotangent, wqkv, ada, wout, up, down, info, gain_one, gain_two, down_bias, ada_bias,
    up_bias, cosines, sines, wide_size, ring,
):
    groups, span, width = tokens.shape
    count = groups * span
    pieces = wide_size // 2 * ring
    rows = width // pieces
    half = width // 2
    folds = up.shape[1] // width
    subs = width // 256
    early = 2 * folds + 1
    blocks = early + 3
    late = 3 * subs
    pairs = width // 128
    outer = (wide_size // 2).bit_length() - 1
    bits = EARLY[1:2] + EARLY[2:3] * (outer - 1)
    early_lags = EARLY[:1] + bits + EARLY[3:4] * 2 + bits[::-1] + EARLY[4:]
    late_lags = LATE[:1] + LATE[1:2] * (2 * outer + 2) + LATE[2:]
    assert subs * 256 == width and subs == 3 and sum(late_lags) > 16
    assert 26 + sum(early_lags) < 50 + sum(late_lags)
    seqs = wide_size * groups
    srows = -(-(seqs * 7 + 3 + folds) // (pieces * 8)) * 8
    sizes = [pieces >> (i + 1) for i in range(outer)]
    tail = (rows, 128)
    small = (srows, half)
    any_space = pl.BlockSpec(memory_space=pl.ANY)
    vmem = pl.BlockSpec(memory_space=pltpu.VMEM)
    block = jax.ShapeDtypeStruct((groups, span, width), BF)
    rows_low = pltpu.VMEM((count, width), BF)
    rows_full = pltpu.VMEM((count, width), F32)
    lanes = pltpu.VMEM((count, 128), F32)
    turned = pltpu.VMEM((width, count), BF)
    vectors = pltpu.VMEM((8, width), F32)
    return pl.pallas_call(
        functools.partial(block_kernel, groups, wide_size, ring, early_lags, late_lags),
        in_specs=[any_space] * 7 + [vmem] * 8,
        out_specs=[any_space] * 4,
        out_shape=[
            jax.ShapeDtypeStruct((blocks, subs, 2, pieces, rows, 128), BF),
            jax.ShapeDtypeStruct((2, pieces, srows, half), BF),
            block,
            block,
        ],
        scratch_shapes=[rows_low] * 9
        + [
            turned,
            pltpu.VMEM((pairs, 8, count), F32),
            pltpu.VMEM((1, 6 * width), F32),
            lanes,
            lanes,
            pltpu.VMEM((1, TEMB), F32),
            pltpu.VMEM((2,) + info.shape, F32),
            pltpu.VMEM((-(-(9 + folds) // 8) * 8, width), F32),
            pltpu.VMEM((width, width), BF),
            pltpu.VMEM((4, width, width), BF),
            pltpu.VMEM((4, subs, 2, pieces, rows, 128), BF),
            pltpu.VMEM((2, pieces, srows, half), BF),
            rows_full,
            rows_low,
            rows_low,
            turned,
            rows_low,
            rows_full,
            rows_full,
            rows_low,
            rows_full,
            pltpu.VMEM((128, count), F32),
            pltpu.VMEM((8, count), F32),
            vectors,
            vectors,
            rows_low,
            rows_low,
            pltpu.VMEM((count, 3 * width), BF),
            rows_low,
            rows_low,
            [
                pltpu.VMEM((early, subs, pieces) + tail, BF),
                pltpu.VMEM((2, subs, pieces) + tail, BF),
                pltpu.VMEM((early, ring - 1, subs, 1) + tail, BF),
                [pltpu.VMEM((early, subs, n) + tail, BF) for n in sizes],
            ],
            [
                pltpu.VMEM((late, pieces) + tail, BF),
                pltpu.VMEM((2 * LATE[0] + 1, pieces) + tail, BF),
                pltpu.VMEM((late, ring - 1, 1) + tail, BF),
                [pltpu.VMEM((late, n) + tail, BF) for n in sizes],
            ],
            [
                pltpu.VMEM((pieces,) + small, BF),
                pltpu.VMEM((pieces,) + small, BF),
                pltpu.VMEM((ring - 1, 1) + small, BF),
                [pltpu.VMEM((n,) + small, BF) for n in sizes],
            ],
            DMA((7,)),
            DMA((4,)),
            DMA((2,)),
            DMA,
            DMA,
            DMA((2, groups)),
            DMA((2, groups)),
            DMA((2, groups)),
            DMA((2, groups)),
            DMA((early + late + 1,)),
            DMA((2 + 2 * outer, early + late + 1)),
            DMA((2 + 2 * outer, early + late + 1)),
            DMA((ring - 1, early + late + 1)),
            DMA((ring - 1, early + late + 1)),
            DMA((ring - 1, early + late + 1)),
            DMA((ring - 1, early + late + 1)),
            DMA((2, pairs)),
            DMA((2, pairs)),
            DMA((2, 8)),
            DMA((2, groups, 8)),
            DMA((2, groups, 8)),
        ],
        compiler_params=pltpu.CompilerParams(
            collective_id=0, has_side_effects=True, vmem_limit_bytes=63 << 20
        ),
        name="whole_block",
    )(
        tokens, cotangent, wqkv, ada, wout, up, down, info, gain_one, gain_two, down_bias, ada_bias,
        up_bias, cosines, sines,
    )


def spread_kernel(
    seqs, folds,
    sum_ref, small_ref,
    ada_ref, qkv_ref, out_ref, up_ref, down_ref,
    ada_bias_ref, gain_one_ref, gain_two_ref, up_bias_ref, down_bias_ref,
    taken, wide, take_sem, give_sem,
):
    blocks, subs, _, width, _ = sum_ref.shape
    small = jnp.concatenate([small_ref[0], small_ref[1]], axis=1)
    order = list(range(blocks))
    takes = [pltpu.make_async_copy(sum_ref.at[n], taken.at[n], take_sem.at[n]) for n in order]
    for take in takes:
        take.start()
    cond = small[6 * seqs : 7 * seqs, : 3 * TEMB]
    for n in range(6):
        mod = small[n * seqs : (n + 1) * seqs, :]
        three = dot(mod, cond, ((0,), (0,)))
        ada_ref[n * width : (n + 1) * width, :] = (
            three[:, :TEMB] + three[:, TEMB : 2 * TEMB] + three[:, 2 * TEMB :]
        )
        ada_bias_ref[n * width : (n + 1) * width] = jnp.sum(mod.astype(F32), axis=0)
    rows = small[7 * seqs : 7 * seqs + 8 * (-(-(3 + folds) // 8)), :].astype(F32)
    gain_one_ref[...] = rows[0]
    gain_two_ref[...] = rows[1]
    down_bias_ref[...] = rows[2]
    for n in range(folds):
        up_bias_ref[n * width : (n + 1) * width] = rows[3 + n]

    gives = []
    for n in order:
        if n < 2 * folds:
            whole = pl.ds(n // 2 * width, width)
            place = up_ref.at[:, whole] if n % 2 else down_ref.at[whole]
        elif n == 2 * folds:
            place = out_ref
        else:
            place = qkv_ref.at[:, pl.ds((n - 2 * folds - 1) * width, width)]
        gives.append(pltpu.make_async_copy(wide.at[n], place, give_sem.at[n]))
        takes[n].wait()

        @pl.loop(0, width // 32)
        def _(r):
            lines = pl.ds(pl.multiple_of(r * 32, 32), 32)
            for m in range(subs):
                for half in range(2):
                    lanes = slice((2 * m + half) * 128, (2 * m + half + 1) * 128)
                    wide[n, lines, lanes] = taken[n, m, half, lines].astype(F32)

        gives[n].start()
    for give in gives:
        give.wait()


def spread(summed, small, seqs, folds):
    blocks, _, _, width, _ = summed.shape
    any_space = pl.BlockSpec(memory_space=pl.ANY)
    vmem = pl.BlockSpec(memory_space=pltpu.VMEM)
    shapes = [
        (6 * width, TEMB), (width, 3 * width), (width, width), (width, folds * width),
        (folds * width, width), (6 * width,), (width,), (width,), (folds * width,), (width,),
    ]
    return pl.pallas_call(
        functools.partial(spread_kernel, seqs, folds),
        in_specs=[any_space, vmem],
        out_specs=[vmem] + [any_space] * 4 + [vmem] * 5,
        out_shape=[jax.ShapeDtypeStruct(shape, F32) for shape in shapes],
        scratch_shapes=[
            pltpu.VMEM(summed.shape, BF),
            pltpu.VMEM((blocks, width, width), F32),
            DMA((blocks,)),
            DMA((blocks,)),
        ],
        compiler_params=pltpu.CompilerParams(vmem_limit_bytes=60 << 20),
        name="spread",
    )(summed, small)


def local(
    tokens, step_ids, prefix, keep_bits, ada_weight, ada_bias, norm1_gain, qkv_weight, out_weight,
    norm2_gain, up_weight, up_bias, down_weight, down_bias, cotangent,
):
    wide_size = lax.axis_size("wide")
    ring = lax.axis_size("narrow")
    groups, span, width = tokens.shape
    assert ring == 2 * groups and wide_size % 2 == 0
    length = ring * span
    hidden = up_weight.shape[1]
    folds = hidden // width
    seqs = wide_size * groups

    allowed = (jnp.arange(length, dtype=jnp.int32)[None, :] < prefix[:, None]) | (keep_bits == 1)
    info = jnp.concatenate(
        [jax.nn.silu(time_embed(step_ids)), jnp.where(allowed, 0.0, masked_score)], axis=1
    )
    cosines, sines = rope_tables(length)
    summed, small, outputs, input_grad = whole_block(
        tokens, cotangent, qkv_weight, ada_weight, out_weight, up_weight, down_weight, info,
        norm1_gain, norm2_gain, down_bias, ada_bias, up_bias, cosines, sines, wide_size, ring,
    )
    ada, qkv, out, up, down, ada_bias_grad, gain_one, gain_two, up_bias_grad, down_bias_grad = (
        spread(
            summed.reshape(-1, width // 256, 2, width, 128), small.reshape(2, -1, width // 2), seqs,
            folds,
        )
    )
    return (
        outputs, input_grad, ada, ada_bias_grad, gain_one, qkv, out, gain_two, up, up_bias_grad,
        down, down_bias_grad,
    )


def solution(mesh):
    split = P("wide", "narrow", None)
    in_specs = (
        (split, P("wide"), P("wide"), P("wide", None)) + (P(),) * 10 + (split,)
    )
    out_specs = (split, split) + (P(),) * 10
    return jax.shard_map(local, mesh=mesh, in_specs=in_specs, out_specs=out_specs, check_vma=False)
```

```python
import functools
import math

import jax
import jax.numpy as jnp
import numpy as np
from jax import lax
from jax.experimental import pallas as pl
from jax.experimental.pallas import tpu as pltpu
from jax.sharding import PartitionSpec as P

HEAD = 64
TEMB = 128
MESH = pl.DeviceIdType.MESH
BF = jnp.bfloat16
F32 = jnp.float32
DMA = pltpu.SemaphoreType.DMA

norm_epsilon = 1e-05
gelu_coeff = 0.7978845608028654
masked_score = -1e30
EARLY = (2, 6, 5, 5, 3)
LATE = (2, 4, 3)


def time_embed(step_ids):
    halfway = TEMB // 2
    frequency = jnp.exp(jnp.arange(halfway, dtype=F32) * (-math.log(10000.0) / halfway))
    angles = step_ids.astype(F32)[:, None] * frequency[None, :]
    return jnp.concatenate([jnp.cos(angles), jnp.sin(angles)], axis=-1)


def rope_tables(length):
    halfway = HEAD // 2
    inverse = 10000.0 ** (-2.0 * np.arange(halfway) / HEAD)
    angles = np.arange(length)[:, None] * inverse[None, :]
    sines = np.sin(angles)
    return (
        np.tile(np.cos(angles), (1, 4)).astype(np.float32),
        np.concatenate([-sines, sines, -sines, sines], axis=1).astype(np.float32),
    )


def dot(former, latter, dims):
    return lax.dot_general(former, latter, (dims, ((), ())), preferred_element_type=F32)


def rotate(values, cosines, sines, sign):
    lane = lax.broadcasted_iota(jnp.int32, (1, 128), 1)
    first = (lane % HEAD) < HEAD // 2
    parts = []
    for n in range(values.shape[1] // 128):
        part = values[:, n * 128 : (n + 1) * 128]
        partner = jnp.where(first, pltpu.roll(part, 128 - HEAD // 2, 1), pltpu.roll(part, HEAD // 2, 1))
        turned = partner * sines
        parts.append(part * cosines + (turned if sign > 0 else -turned))
    return parts[0] if len(parts) == 1 else jnp.concatenate(parts, axis=1)


def normed_rows(values):
    center = values - jnp.mean(values, axis=-1, keepdims=True)
    spread = jnp.mean(center * center, axis=-1, keepdims=True)
    scale = lax.rsqrt(spread + norm_epsilon)
    return center * scale, scale


def part_of(mod_ref, index, width):
    return mod_ref[:, index * width : (index + 1) * width]


def wide_of(block, copies):
    return jnp.concatenate([block] * copies, axis=1)


def block_kernel(
    groups, wide_size, ring, early_lags, late_lags,
    tok_ref, cot_ref, wqkv_ref, ada_ref, wout_ref, up_ref, down_ref,
    info_ref, gain_one_ref, gain_two_ref, down_bias_ref, ada_bias_ref, up_bias_ref, cos_ref,
    sin_ref,
    sum_ref, ssum_ref, tokens_ref, grad_ref,
    x_ref, dy_ref, h_ref, q_ref, ka_ref, va_ref, kb_ref, vb_ref, o_ref, ot_ref, lse_ref, mod_ref,
    ba_ref, bb_ref, cond_ref, table, par_ref, wout,
    weights, staging, dsmall, middle, branch, normed_low, normed_t, dm, total_a, total_b, active,
    slope, dq_t, deltas, vec, dup_bias, out_rows, dqkv, dk_in, dv_in,
    early_buffers, late_buffers, small_buffers,
    load_sem, weight_sem, take_self, info_send, info_recv, take_send, take_recv, swap_send,
    swap_recv, copy_sem, send_sem, recv_sem, ring_send, ring_recv, gather_send, gather_recv, kv_send, kv_recv, self_sem, row_send, row_recv,
):
    early, subs, pieces, piece_rows = early_buffers[0].shape[:4]
    late_count = late_buffers[0].shape[0]
    stages = staging.shape[0]
    outer = (wide_size // 2).bit_length() - 1
    count, width = x_ref.shape
    span = count // groups
    pairs = width // 128
    folds = up_ref.shape[1] // width
    wide = lax.axis_index("wide")
    chip = lax.axis_index("narrow")
    core = lax.rem(wide, 2)
    base = wide - core
    core_peer = (base + 1 - core, chip)
    dims = []
    for b in range(outer):
        bit = lax.rem(wide // (2 << b), 2)
        dims.append((bit, wide + (1 - 2 * bit) * (2 << b), chip))

    def load_up(i, slot):
        cols = pl.ds(pl.multiple_of(i * width, width), width)
        return pltpu.make_async_copy(up_ref.at[:, cols], weights.at[slot], weight_sem.at[slot])

    def load_down(i, slot):
        rows = pl.ds(pl.multiple_of(i * width, width), width)
        return pltpu.make_async_copy(down_ref.at[rows], weights.at[slot], weight_sem.at[slot])

    def load_qkv(n):
        cols = pl.ds(n * width, width)
        return pltpu.make_async_copy(wqkv_ref.at[:, cols], weights.at[n], weight_sem.at[n])

    load_ada = [
        pltpu.make_async_copy(
            ada_ref.at[pl.ds(n * width, width)],
            weights.at[3, :, pl.ds(n * TEMB, TEMB)],
            load_sem.at[1 + n],
        )
        for n in range(6)
    ]
    load_out = pltpu.make_async_copy(wout_ref, wout, load_sem.at[0])

    barrier = pltpu.get_barrier_semaphore()
    for d in dims[:outer]:
        pl.semaphore_signal(barrier, inc=1, device_id=d[1:], device_id_type=MESH)
    for c in range(2):
        for d in range(ring):
            if c or d:
                other = (base + lax.rem(core + c, 2), lax.rem(chip + d, ring))
                pl.semaphore_signal(barrier, inc=1, device_id=other, device_id_type=MESH)
    for load in load_ada:
        load.start()
    for n in range(3):
        load_qkv(n).start()
    load_out.start()
    pl.semaphore_wait(barrier, outer + 2 * ring - 1)

    slot = lax.rem(chip, groups)
    home = chip // groups
    rows_out = pl.ds(pl.multiple_of(slot * span, span), span)

    def move(src, dst, kind, g):
        remote = pltpu.make_async_remote_copy(
            src_ref=src.at[g],
            dst_ref=dst.at[rows_out],
            send_sem=take_send.at[kind, g],
            recv_sem=take_recv.at[kind, slot],
            device_id=(base + home, core * groups + g),
            device_id_type=MESH,
        )
        here = pltpu.make_async_copy(src.at[g], dst.at[rows_out], take_self.at[kind])
        own = (home == core) & (slot == g)
        return remote, here, own

    def send(src, dst, kind):
        for g in range(groups):
            remote, here, own = move(src, dst, kind, g)

            @pl.when(own)
            def _():
                here.start()

            @pl.when(jnp.logical_not(own))
            def _():
                remote.start()

    def sent(src, dst, kind):
        for g in range(groups):
            remote, here, own = move(src, dst, kind, g)

            @pl.when(jnp.logical_not(own))
            def _():
                remote.wait_send()

    def arrive(src, dst, kind, j):
        rows = pl.ds(j * span, span)
        own = (home == core) & (slot == j)

        @pl.when(own)
        def _():
            pltpu.make_async_copy(src.at[0], dst.at[rows], take_self.at[kind]).wait()

        @pl.when(jnp.logical_not(own))
        def _():
            pltpu.make_async_remote_copy(
                src_ref=src.at[0],
                dst_ref=dst.at[rows],
                send_sem=take_send.at[kind, 0],
                recv_sem=take_recv.at[kind, j],
                device_id=core_peer,
                device_id_type=MESH,
            ).wait_recv()

    send(tok_ref, x_ref, 0)
    par_ref[0:1, :] = gain_one_ref[...].reshape(1, width)
    par_ref[1:2, :] = gain_two_ref[...].reshape(1, width)
    par_ref[2:3, :] = down_bias_ref[...].reshape(1, width)
    for i in range(6):
        par_ref[3 + i : 4 + i, :] = ada_bias_ref[i * width : (i + 1) * width].reshape(1, width)
    for i in range(folds):
        par_ref[9 + i : 10 + i, :] = up_bias_ref[i * width : (i + 1) * width].reshape(1, width)
    table[core] = info_ref[...]
    swap_info = pltpu.make_async_remote_copy(
        src_ref=info_ref,
        dst_ref=table.at[core],
        send_sem=info_send,
        recv_sem=info_recv,
        device_id=core_peer,
        device_id_type=MESH,
    )
    swap_info.start()
    swap_info.wait()
    row = table[home, pl.ds(slot, 1), :]
    length = row.shape[1] - TEMB
    cond_ref[...] = row[:, :TEMB]
    bias = jnp.where(core == 0, row[:, TEMB : TEMB + count], row[:, TEMB + count : TEMB + length])
    ba_ref[...] = jnp.broadcast_to(bias, (128, count)).T
    bias = jnp.where(core == 1, row[:, TEMB : TEMB + count], row[:, TEMB + count : TEMB + length])
    bb_ref[...] = jnp.broadcast_to(bias, (128, count)).T

    cond = jnp.broadcast_to(row[:, :TEMB], (16, TEMB))
    high = cond.astype(BF).astype(F32)
    medium = (cond - high).astype(BF).astype(F32)
    low = cond - high - medium
    line = lax.broadcasted_iota(jnp.int32, (16, TEMB), 0)
    three = jnp.where(
        line == 0, high, jnp.where(line == 1, medium, jnp.where(line == 2, low, 0.0))
    ).astype(BF)
    for load in load_ada:
        load.wait()
    for i in range(6):
        cols = slice(i * width, (i + 1) * width)
        mod_ref[:, cols] = (
            jnp.sum(dot(three, weights[3, :, i * TEMB : (i + 1) * TEMB], ((1,), (1,))), axis=0, keepdims=True)
            + par_ref[3 + i : 4 + i, :]
        )
    shift = part_of(mod_ref, 0, width)
    scale = par_ref[0:1, :] * (1.0 + part_of(mod_ref, 1, width))

    for n in range(3):
        load_qkv(n).wait()
    swaps = []
    for j in range(groups):
        rows = pl.ds(j * span, span)
        arrive(tok_ref, x_ref, 0, j)
        if j == groups - 1:
            send(cot_ref, dy_ref, 1)
        normed, _ = normed_rows(x_ref[rows, :].astype(F32))
        h_ref[rows, :] = (normed * scale + shift).astype(BF)
        place = pl.ds(pl.multiple_of(core * count + j * span, span), span)
        cosines = cos_ref[place, :]
        sines = sin_ref[place, :]
        step = 256
        for n in (2, 1, 0):
            target = (q_ref, ka_ref, va_ref)[n]
            for m in range(width // step):
                cols = slice(m * step, (m + 1) * step)
                block = dot(h_ref[rows, :], weights[n, :, cols], ((1,), (0,)))
                if n < 2:
                    block = rotate(block, cosines, sines, 1)
                if n == 0:
                    block = block * HEAD**-0.5
                target[rows, m * step : (m + 1) * step] = block.astype(BF)
            if n > 0:
                swap = pltpu.make_async_remote_copy(
                    src_ref=target.at[rows],
                    dst_ref=(kb_ref, vb_ref)[n - 1].at[rows],
                    send_sem=swap_send.at[n - 1, j],
                    recv_sem=swap_recv.at[n - 1, j],
                    device_id=core_peer,
                    device_id_type=MESH,
                )
                swap.start()
                swaps.append(swap)
    for i in range(2):
        load_up(i, 2 * i).start()
        load_down(i, 2 * i + 1).start()
    for swap in swaps:
        swap.wait()

    copies = count // 128
    lane = lax.broadcasted_iota(jnp.int32, (1, 128), 1)

    @pl.loop(0, width // 128)
    def _(p):
        cols = pl.ds(pl.multiple_of(p * 128, 128), 128)
        q = q_ref[:, cols]
        ka = ka_ref[:, cols]
        kb = kb_ref[:, cols]
        va_t = va_ref[:, cols].T
        vb_t = vb_ref[:, cols].T
        outs = []
        for h in range(2):
            qm = jnp.where((lane // HEAD) == h, q, jnp.zeros_like(q))
            sa = dot(ka, qm, ((1,), (1,))) + wide_of(ba_ref[...], copies)
            sb = dot(kb, qm, ((1,), (1,))) + wide_of(bb_ref[...], copies)
            top = jnp.maximum(jnp.max(sa, axis=0, keepdims=True), jnp.max(sb, axis=0, keepdims=True))
            pa = jnp.exp(sa - top)
            pb = jnp.exp(sb - top)
            total = jnp.sum(pa, axis=0, keepdims=True) + jnp.sum(pb, axis=0, keepdims=True)
            part = slice(h * HEAD, (h + 1) * HEAD)
            out = dot(va_t[part], pa.astype(BF), ((1,), (0,))) + dot(
                vb_t[part], pb.astype(BF), ((1,), (0,))
            )
            outs.append(out / total)
            lse_ref[p, h : h + 1, :] = top + jnp.log(total)
        both = jnp.concatenate(outs, axis=0)
        ot_ref[cols, :] = both.astype(BF)
        o_ref[:, cols] = both.T.astype(BF)

    sent(tok_ref, x_ref, 0)
    for j in range(groups):
        arrive(cot_ref, dy_ref, 1, j)
    load_out.wait()

    parts = 8
    part_rows = span // parts

    def row_move(src, dst, kind, j, q):
        rows = pl.ds(pl.multiple_of(j * span + q * part_rows, part_rows), part_rows)
        place = dst.at[slot, pl.ds(pl.multiple_of(q * part_rows, part_rows), part_rows)]
        remote = pltpu.make_async_remote_copy(
            src_ref=src.at[rows],
            dst_ref=place,
            send_sem=row_send.at[kind, j, q],
            recv_sem=row_recv.at[kind, slot, q],
            device_id=(base + home, core * groups + j),
            device_id_type=MESH,
        )
        here = pltpu.make_async_copy(src.at[rows], place, self_sem.at[kind, q])
        own = (home == core) & (slot == j)
        return remote, here, own

    def row_send_part(src, dst, kind, q):
        for j in range(groups):
            remote, here, own = row_move(src, dst, kind, j, q)

            @pl.when(own)
            def _():
                here.start()

            @pl.when(jnp.logical_not(own))
            def _():
                remote.start()

    def row_wait_part(src, dst, kind, q):
        for j in range(groups):
            remote, here, own = row_move(src, dst, kind, j, q)

            @pl.when(own)
            def _():
                here.wait()

            @pl.when(jnp.logical_not(own))
            def _():
                remote.wait_send()

        rows = pl.ds(pl.multiple_of(q * part_rows, part_rows), part_rows)
        for g in range(groups):
            own = (home == core) & (slot == g)

            @pl.when(jnp.logical_not(own))
            def _():
                pltpu.make_async_remote_copy(
                    src_ref=src.at[rows],
                    dst_ref=dst.at[g, rows],
                    send_sem=row_send.at[kind, 0, q],
                    recv_sem=row_recv.at[kind, g, q],
                    device_id=core_peer,
                    device_id_type=MESH,
                ).wait_recv()

    last = 2 * outer + 4

    def stage(step, odd, sem, pick, source, out, total, core_slot, ring_slot, bit_slots):
        low = 0
        size = pieces
        steps = []
        for i in range(outer):
            (bit, peer_wide, _), (other_bit, other_wide, _) = dims[i], dims[outer - 1 - i]
            bit = bit + odd * (other_bit - bit)
            peer_wide = peer_wide + odd * (other_wide - peer_wide)
            size //= 2
            before = low
            low = low + bit * size
            steps.append((before + (1 - bit) * size, low, size, (peer_wide, chip)))
        final = low + chip

        def remote(src, dst, index, peer):
            return pltpu.make_async_remote_copy(
                src_ref=src,
                dst_ref=dst,
                send_sem=send_sem.at[index, sem],
                recv_sem=recv_sem.at[index, sem],
                device_id=peer,
                device_id_type=MESH,
            )

        def core_copy():
            return remote(source(1 - core), core_slot, 0, core_peer)

        def own_copy():
            return pltpu.make_async_copy(source(core), total, copy_sem.at[sem])

        def bit_copy(i):
            away, _, size, peer = steps[i]
            return remote(pick(total, away, size), bit_slots[i], 1 + i, peer)

        def ring_copies():
            copies = []
            for d in range(1, ring):
                target = lax.rem(chip + d, ring)
                copies.append(
                    pltpu.make_async_remote_copy(
                        src_ref=pick(total, low + target, 1),
                        dst_ref=ring_slot.at[d - 1],
                        send_sem=ring_send.at[d - 1, sem],
                        recv_sem=ring_recv.at[d - 1, sem],
                        device_id=(wide, target),
                        device_id_type=MESH,
                    )
                )
            return copies

        def gather_copies():
            return [
                pltpu.make_async_remote_copy(
                    src_ref=pick(total, final, 1),
                    dst_ref=pick(out(core), final, 1),
                    send_sem=gather_send.at[d - 1, sem],
                    recv_sem=gather_recv.at[d - 1, sem],
                    device_id=(wide, lax.rem(chip + d, ring)),
                    device_id_type=MESH,
                )
                for d in range(1, ring)
            ]

        def keep_copy():
            return pltpu.make_async_copy(
                pick(total, final, 1), pick(out(core), final, 1), copy_sem.at[sem]
            )

        def back_copy(i):
            _, keep, size, peer = steps[i]
            place = pick(out(core), keep, size)
            return remote(place, place, 1 + outer + i, peer)

        def core_back():
            return remote(out(core), out(core), 1 + 2 * outer, core_peer)

        def add(start, size, slot):
            place = pick(total, start, size)
            place[...] = place[...] + slot[...]

        if step == 0:
            core_copy().start()
            own_copy().start()
        elif step == 1:
            own_copy().wait()
            core_copy().wait()
            total[...] = total[...] + core_slot[...]
            bit_copy(0).start()
        elif step <= outer + 1:
            i = step - 2
            bit_copy(i).wait()
            add(steps[i][1], steps[i][2], bit_slots[i])
            if step <= outer:
                bit_copy(i + 1).start()
            else:
                for copy in ring_copies():
                    copy.start()
        elif step == outer + 2:
            for copy in ring_copies():
                copy.wait()
            place = pick(total, final, 1)
            value = place[...].astype(F32)
            for d in range(1, ring):
                value = value + ring_slot[d - 1].astype(F32)
            place[...] = value.astype(BF)
            keep_copy().start()
            for copy in gather_copies():
                copy.start()
        elif step == outer + 3:
            keep_copy().wait()
            for copy in gather_copies():
                copy.wait()
            back_copy(outer - 1).start()
        elif step <= 2 * outer + 2:
            i = 2 * outer + 2 - step
            back_copy(i + 1).wait()
            back_copy(i).start()
        elif step == 2 * outer + 3:
            back_copy(0).wait()
            core_back().start()
        else:
            core_back().wait()

    early_at = [2 + sum(early_lags[:step]) for step in range(last + 1)]
    late_at = [sum(late_lags[:step]) for step in range(last + 1)]
    per_group = pairs // subs
    turn = 2 * per_group + 2
    lead = 6 * folds + 3
    closing = lead + subs * turn

    def pick_early(ref, start, size):
        return ref.at[:, pl.ds(start, size)]

    def pick_late(ref, start, size):
        return ref.at[pl.ds(start, size)]

    def early_stage(step, chunk, odd):
        total, core_slots, ring_slots, bit_slots = early_buffers
        stage(
            step, odd, chunk, pick_early,
            lambda half: staging.at[chunk % stages, :, half],
            lambda half: sum_ref.at[chunk, :, half],
            total.at[chunk], core_slots.at[odd], ring_slots.at[chunk],
            [ref.at[chunk] for ref in bit_slots],
        )

    def late_stage(step, group, part):
        chunk = group * 3 + part
        total, core_slots, ring_slots, bit_slots = late_buffers
        stage(
            step, (group + part) % 2, early + chunk, pick_late,
            lambda half: staging.at[(early + part) % stages, group, half],
            lambda half: sum_ref.at[early + part, group, half],
            total.at[chunk], core_slots.at[chunk % core_slots.shape[0]],
            ring_slots.at[chunk], [ref.at[chunk] for ref in bit_slots],
        )

    def small_stage(step):
        stage(
            step, 0, early + late_count, pick_late,
            lambda half: dsmall.at[half], lambda half: ssum_ref.at[half], *small_buffers
        )

    def move_on(tick, turns, repeat, period):
        for step in range(last, -1, -1):
            since = tick - early_at[step]
            first = since // 3
            if since % 3 == 0 and first + (turns - 1) * period // 3 >= 0 and first < early:
                chunk = first + repeat * (period // 3)
                one = functools.partial(early_stage, step, chunk, first % 2)
                if first >= 0 and first + (turns - 1) * period // 3 < early:
                    one()
                else:
                    pl.when((chunk >= 0) & (chunk < early))(one)
        for step in range(last, -1, -1):
            for part in range(3):
                since = tick - (lead + 2 * per_group + part) - late_at[step]
                first = since // turn
                if since % turn == 0 and first + (turns - 1) * period // turn >= 0 and first < subs:
                    group = first + repeat * (period // turn)
                    one = functools.partial(late_stage, step, group, part)
                    if first >= 0 and first + (turns - 1) * period // turn < subs:
                        one()
                    else:
                        pl.when((group >= 0) & (group < subs))(one)
            if turns == 1 and tick == closing + 2 + late_at[step]:
                small_stage(step)

    def place_block(block, part, value):
        for half in range(2):
            lanes = slice(half * 128, (half + 1) * 128)
            for i in range(pieces):
                staging[lax.rem(block, stages), part, half, i] = value[
                    i * piece_rows : (i + 1) * piece_rows, lanes
                ]

    tile = min(256, count)
    tiles = [slice(r, r + tile) for r in range(0, count, tile)]
    gain_one = par_ref[0:1, :]
    gain_two = par_ref[1:2, :]
    shift_two, scale_two, gate_one, gate_two = (part_of(mod_ref, i, width) for i in (3, 4, 2, 5))

    def prepare():
        total = 0.0
        for rows in tiles:
            a = dot(o_ref[rows, :], wout[...], ((1,), (0,)))
            branch[rows, :] = a.astype(BF)
            x1 = x_ref[rows, :].astype(F32) + gate_one * a
            middle[rows, :] = x1
            normed, _ = normed_rows(x1)
            h2 = (normed * (gain_two * (1.0 + scale_two)) + shift_two).astype(BF)
            normed_low[rows, :] = h2
            normed_t[:, rows] = h2.T
            dm_rows = (dy_ref[rows, :].astype(F32) * gate_two).astype(BF)
            dm[rows, :] = dm_rows
            total = total + jnp.sum(dm_rows.astype(F32), axis=0, keepdims=True)
        vec[5:6, :] = total

    def hidden_units(i, rows):
        slot = 2 * lax.rem(i, 2)
        if rows is tiles[0]:
            load_up(i, slot).wait()
            load_down(i, slot + 1).wait()
        bias = par_ref[pl.ds(9 + i, 1), :]
        u = dot(normed_low[rows, :], weights[slot], ((1,), (0,))) + bias
        square = u * u
        tanh = jnp.tanh(gelu_coeff * (u + 0.044715 * u * square))
        g = (0.5 * u * (1.0 + tanh)).astype(BF)
        active[rows, :] = g
        slope[rows, :] = (
            0.5 * (1.0 + tanh)
            + (0.5 * gelu_coeff) * u * (1.0 - tanh * tanh) * (1.0 + (3 * 0.044715) * square)
        ).astype(BF)
        part = dot(g, weights[slot + 1], ((1,), (0,)))

        @pl.when(i == 0)
        def _():
            total_a[rows, :] = part

        @pl.when(i > 0)
        def _():
            total_a[rows, :] += part

    def down_grads(i):
        for m in range(0, width, 256):
            cols = slice(m, m + 256)
            place_block(
                2 * i, m // 256, dot(active[...], dm[:, cols], ((0,), (0,))).astype(BF)
            )

    def hidden_units_back(i, rows):
        slot = 2 * lax.rem(i, 2)
        dg = dot(dm[rows, :], weights[slot + 1], ((1,), (1,)))
        du = (dg * slope[rows, :].astype(F32)).astype(BF)
        active[rows, :] = du
        total = jnp.sum(du.astype(F32), axis=0, keepdims=True)
        part = dot(du, weights[slot], ((1,), (1,)))
        line = pl.ds(i, 1)
        if rows is tiles[0]:
            dup_bias[line, :] = total
        else:
            dup_bias[line, :] += total

        @pl.when(i == 0)
        def _():
            total_b[rows, :] = part

        @pl.when(i > 0)
        def _():
            total_b[rows, :] += part

    def up_grads(i):
        slot = 2 * lax.rem(i, 2)

        @pl.when(i + 2 < folds)
        def _():
            load_up(i + 2, slot).start()
            load_down(i + 2, slot + 1).start()

        @pl.when(i == folds - 1)
        def _():
            for n in range(3):
                load_qkv(n).start()

        for m in range(0, width, 256):
            cols = slice(m, m + 256)
            place_block(
                2 * i + 1, m // 256, dot(normed_t[...], active[:, cols], ((1,), (0,))).astype(BF)
            )

    def close_hidden_rows(rows):
        m = total_a[rows, :] + par_ref[2:3, :]
        x1 = middle[rows, :]
        out_rows[rows, :] = (x1 + gate_two * m).astype(BF)
        dy = dy_ref[rows, :].astype(F32)
        dh = total_b[rows, :]
        n2, rscale = normed_rows(x1)
        e = dh * ((1.0 + scale_two) * gain_two)
        dx1 = dy + rscale * (
            e
            - jnp.mean(e, axis=-1, keepdims=True)
            - n2 * jnp.mean(e * n2, axis=-1, keepdims=True)
        )
        middle[rows, :] = dx1
        da = (gate_one * dx1).astype(BF)
        normed_low[rows, :] = da
        for i, value in enumerate((dx1 * branch[rows, :].astype(F32), dh, dh * n2, dy * m)):
            total = jnp.sum(value, axis=0, keepdims=True)
            line = slice(i, i + 1)
            vec[line, :] = total if rows is tiles[0] else vec[line, :] + total
        active[rows, :] = dot(da, wout[...], ((1,), (1,))).astype(BF)

    def close_hidden(all_tiles):
        for rows in all_tiles:
            close_hidden_rows(rows)

    def out_grads():
        vec[4:5, :] = vec[2:3, :] * (1.0 + scale_two)
        vec[2:3, :] = vec[2:3, :] * gain_two
        for m in range(0, width, 256):
            cols = slice(m, m + 256)
            place_block(
                2 * folds, m // 256, dot(ot_ref[...], normed_low[:, cols], ((1,), (0,))).astype(BF)
            )

    place = pl.ds(pl.multiple_of(core * count, count), count)

    def kv_copies(p):
        cols = pl.ds(pl.multiple_of(p * 128, 128), 128)
        return [
            pltpu.make_async_remote_copy(
                src_ref=away.at[:, cols],
                dst_ref=landing.at[:, cols],
                send_sem=kv_send.at[i, p],
                recv_sem=kv_recv.at[i, p],
                device_id=core_peer,
                device_id_type=MESH,
            )
            for i, (away, landing) in enumerate(((normed_low, dk_in), (dm, dv_in)))
        ]

    def attention(p, side):
        cols = pl.ds(pl.multiple_of(p * 128, 128), 128)
        q = q_ref[:, cols]
        do = active[:, cols]
        if side == 0:
            prod = ot_ref[cols, :].astype(F32) * do.astype(F32).T
        k_ref, v_ref, b_ref, dk_ref, dv_ref = (
            (kb_ref, vb_ref, bb_ref, normed_low, dm),
            (ka_ref, va_ref, ba_ref, total_a, total_b),
        )[side]
        k = k_ref[:, cols]
        v = v_ref[:, cols]
        k_t = k.T
        dk = dv = None
        for h in range(2):
            picked = (lane // HEAD) == h
            part = slice(h * HEAD, (h + 1) * HEAD)
            qm = jnp.where(picked, q, jnp.zeros_like(q))
            dom = jnp.where(picked, do, jnp.zeros_like(do))
            if side == 0:
                deltas[h : h + 1, :] = jnp.sum(prod[part], axis=0, keepdims=True)
            delta = deltas[h : h + 1, :]
            s = dot(k, qm, ((1,), (1,))) + wide_of(b_ref[...], copies)
            prob = jnp.exp(s - lse_ref[p, h : h + 1, :])
            dv_h = dot(prob.astype(BF), dom, ((1,), (0,)))
            dprob = dot(v, dom, ((1,), (1,)))
            ds = (prob * (dprob - delta)).astype(BF)
            dk_h = dot(ds, qm, ((1,), (0,)))
            dq_h = dot(k_t[part], ds, ((1,), (0,)))
            dq_t[part, :] = dq_h if side == 0 else dq_t[part, :] + dq_h
            dk = dk_h if dk is None else dk + dk_h
            dv = dv_h if dv is None else dv + dv_h
        dk_ref[:, cols] = dk.astype(dk_ref.dtype)
        dv_ref[:, cols] = dv.astype(dv_ref.dtype)
        if side == 0:
            for copy in kv_copies(p):
                copy.start()
        else:
            dq = (dq_t[...] * (HEAD**-0.5)).T
            dqkv[:, cols] = rotate(dq, cos_ref[place, :], sin_ref[place, :], -1).astype(BF)

    def join(group):
        for i in range(pairs // subs):
            p = group * (pairs // subs) + i
            for copy in kv_copies(p):
                copy.wait()
            cols = pl.ds(pl.multiple_of(p * 128, 128), 128)
            dk = total_a[:, cols] + dk_in[:, cols].astype(F32)
            dv = total_b[:, cols] + dv_in[:, cols].astype(F32)
            k_cols = pl.ds(pl.multiple_of(width + p * 128, 128), 128)
            v_cols = pl.ds(pl.multiple_of(2 * width + p * 128, 128), 128)
            dqkv[:, k_cols] = rotate(dk, cos_ref[place, :], sin_ref[place, :], -1).astype(BF)
            dqkv[:, v_cols] = dv.astype(BF)

    def project_grads(group, n):
        cols = pl.ds(pl.multiple_of(n * width + group * 256, 256), 256)
        value = dot(normed_t[...], dqkv[:, cols], ((1,), (0,))).astype(BF)
        place_block(early + n, group, value)

    def finish(rows):
        if rows is tiles[0]:
            for n in range(3):
                load_qkv(n).wait()
        scale = 1.0 + part_of(mod_ref, 1, width)
        dh = sum(
            dot(dqkv[rows, n * width : (n + 1) * width], weights[n], ((1,), (1,)))
            for n in range(3)
        )
        n1, rscale = normed_rows(x_ref[rows, :].astype(F32))
        e = dh * (scale * gain_one)
        active[rows, :] = (
            middle[rows, :]
            + rscale
            * (
                e
                - jnp.mean(e, axis=-1, keepdims=True)
                - n1 * jnp.mean(e * n1, axis=-1, keepdims=True)
            )
        ).astype(BF)
        for i, value in enumerate((dh, dh * n1)):
            total = jnp.sum(value, axis=0, keepdims=True)
            line = slice(6 + i, 7 + i)
            vec[line, :] = total if rows is tiles[0] else vec[line, :] + total

    def small_grads():
        scale = 1.0 + part_of(mod_ref, 1, width)
        srows = dsmall.shape[2]
        seqs = wide_size * groups
        seq = (wide // 2) * ring + chip
        line = lax.broadcasted_iota(jnp.int32, (pieces * srows, width), 0)
        cond = jnp.where(core == 0, cond_ref[...], 0.0)
        high = cond.astype(BF).astype(F32)
        medium = (cond - high).astype(BF).astype(F32)
        filler = jnp.zeros((1, width - 3 * TEMB), F32)
        entries = [
            (seq, vec[6:7, :]),
            (seqs + seq, vec[7:8, :] * gain_one),
            (2 * seqs + seq, vec[0:1, :]),
            (3 * seqs + seq, vec[1:2, :]),
            (4 * seqs + seq, vec[2:3, :]),
            (5 * seqs + seq, vec[3:4, :]),
            (6 * seqs + seq, jnp.concatenate([high, medium, cond - high - medium, filler], axis=1)),
            (7 * seqs, vec[7:8, :] * scale),
            (7 * seqs + 1, vec[4:5, :]),
            (7 * seqs + 2, vec[5:6, :]),
        ] + [(7 * seqs + 3 + i, dup_bias[i : i + 1, :]) for i in range(folds)]
        value = jnp.zeros((pieces * srows, width), F32)
        for at, entry in entries:
            value = jnp.where(line == at, entry, value)
        for half in range(2):
            lanes = slice(half * (width // 2), (half + 1) * (width // 2))
            dsmall[half] = value[:, lanes].reshape(pieces, srows, width // 2).astype(BF)

    prepare()

    @pl.loop(0, folds)
    def _(i):
        for u in range(6):
            unit = (hidden_units, hidden_units_back)[u // 3]
            if u % 3 == 2:
                (down_grads, up_grads)[u // 3](i)
            else:
                for rows in tiles[u % 3 :: 2]:
                    unit(i, rows)
            move_on(u, folds, i, 6)

    close_hidden(tiles)
    move_on(lead - 3, 1, 0, 0)
    move_on(lead - 2, 1, 0, 0)
    out_grads()
    normed_t[...] = h_ref[...].T
    move_on(lead - 1, 1, 0, 0)

    @pl.loop(0, subs)
    def _(group):
        for u in range(turn):
            if u < 2 * per_group:
                attention(group * per_group + u // 2, u % 2)
            elif u == 2 * per_group:
                join(group)
                project_grads(group, 0)
            else:
                project_grads(group, 1)
                project_grads(group, 2)
            if u % 2 == 0:
                part = group * (turn // 2) + u // 2

                @pl.when(part < parts)
                def _():
                    row_send_part(out_rows, tokens_ref, 0, part)

            move_on(lead + u, subs, group, turn)

    for tick in range(closing, closing + 3 + late_at[-1]):
        if tick < closing + 2:
            for rows in tiles[tick - closing :: 2]:
                finish(rows)
        elif tick == closing + 2:
            small_grads()
        part = tick - closing - 2
        if part >= 0 and part % 2 == 0 and part // 2 < parts:
            row_send_part(active, grad_ref, 1, part // 2)
        move_on(tick, 1, 0, 0)

    sent(cot_ref, dy_ref, 1)

    @pl.loop(0, parts)
    def _(q):
        row_wait_part(out_rows, tokens_ref, 0, q)
        row_wait_part(active, grad_ref, 1, q)


def whole_block(
    tokens, cotangent, wqkv, ada, wout, up, down, info, gain_one, gain_two, down_bias, ada_bias,
    up_bias, cosines, sines, wide_size, ring,
):
    groups, span, width = tokens.shape
    count = groups * span
    pieces = wide_size // 2 * ring
    rows = width // pieces
    half = width // 2
    folds = up.shape[1] // width
    subs = width // 256
    early = 2 * folds + 1
    blocks = early + 3
    late = 3 * subs
    pairs = width // 128
    outer = (wide_size // 2).bit_length() - 1
    bits = EARLY[1:2] + EARLY[2:3] * (outer - 1)
    early_lags = EARLY[:1] + bits + EARLY[3:4] * 2 + bits[::-1] + EARLY[4:]
    late_lags = LATE[:1] + LATE[1:2] * (2 * outer + 2) + LATE[2:]
    assert subs * 256 == width and subs == 3 and sum(late_lags) > 16
    assert 26 + sum(early_lags) < 48 + sum(late_lags) and folds % 2 == 0
    seqs = wide_size * groups
    srows = -(-(seqs * 7 + 3 + folds) // (pieces * 8)) * 8
    sizes = [pieces >> (i + 1) for i in range(outer)]
    tail = (rows, 128)
    small = (srows, half)
    any_space = pl.BlockSpec(memory_space=pl.ANY)
    vmem = pl.BlockSpec(memory_space=pltpu.VMEM)
    block = jax.ShapeDtypeStruct((groups, span, width), BF)
    rows_low = pltpu.VMEM((count, width), BF)
    rows_full = pltpu.VMEM((count, width), F32)
    lanes = pltpu.VMEM((count, 128), F32)
    turned = pltpu.VMEM((width, count), BF)
    vectors = pltpu.VMEM((8, width), F32)
    return pl.pallas_call(
        functools.partial(block_kernel, groups, wide_size, ring, early_lags, late_lags),
        in_specs=[any_space] * 7 + [vmem] * 8,
        out_specs=[any_space] * 4,
        out_shape=[
            jax.ShapeDtypeStruct((blocks, subs, 2, pieces, rows, 128), BF),
            jax.ShapeDtypeStruct((2, pieces, srows, half), BF),
            block,
            block,
        ],
        scratch_shapes=[rows_low] * 9
        + [
            turned,
            pltpu.VMEM((pairs, 8, count), F32),
            pltpu.VMEM((1, 6 * width), F32),
            lanes,
            lanes,
            pltpu.VMEM((1, TEMB), F32),
            pltpu.VMEM((2,) + info.shape, F32),
            pltpu.VMEM((-(-(9 + folds) // 8) * 8, width), F32),
            pltpu.VMEM((width, width), BF),
            pltpu.VMEM((4, width, width), BF),
            pltpu.VMEM((4, subs, 2, pieces, rows, 128), BF),
            pltpu.VMEM((2, pieces, srows, half), BF),
            rows_full,
            rows_low,
            rows_low,
            turned,
            rows_low,
            rows_full,
            rows_full,
            rows_low,
            rows_low,
            pltpu.VMEM((128, count), F32),
            pltpu.VMEM((8, count), F32),
            vectors,
            vectors,
            rows_low,
            pltpu.VMEM((count, 3 * width), BF),
            rows_low,
            rows_low,
            [
                pltpu.VMEM((early, subs, pieces) + tail, BF),
                pltpu.VMEM((2, subs, pieces) + tail, BF),
                pltpu.VMEM((early, ring - 1, subs, 1) + tail, BF),
                [pltpu.VMEM((early, subs, n) + tail, BF) for n in sizes],
            ],
            [
                pltpu.VMEM((late, pieces) + tail, BF),
                pltpu.VMEM((2 * LATE[0] + 1, pieces) + tail, BF),
                pltpu.VMEM((late, ring - 1, 1) + tail, BF),
                [pltpu.VMEM((late, n) + tail, BF) for n in sizes],
            ],
            [
                pltpu.VMEM((pieces,) + small, BF),
                pltpu.VMEM((pieces,) + small, BF),
                pltpu.VMEM((ring - 1, 1) + small, BF),
                [pltpu.VMEM((n,) + small, BF) for n in sizes],
            ],
            DMA((7,)),
            DMA((4,)),
            DMA((2,)),
            DMA,
            DMA,
            DMA((2, groups)),
            DMA((2, groups)),
            DMA((2, groups)),
            DMA((2, groups)),
            DMA((early + late + 1,)),
            DMA((2 + 2 * outer, early + late + 1)),
            DMA((2 + 2 * outer, early + late + 1)),
            DMA((ring - 1, early + late + 1)),
            DMA((ring - 1, early + late + 1)),
            DMA((ring - 1, early + late + 1)),
            DMA((ring - 1, early + late + 1)),
            DMA((2, pairs)),
            DMA((2, pairs)),
            DMA((2, 8)),
            DMA((2, groups, 8)),
            DMA((2, groups, 8)),
        ],
        compiler_params=pltpu.CompilerParams(
            collective_id=0, has_side_effects=True, vmem_limit_bytes=63 << 20
        ),
        name="whole_block",
    )(
        tokens, cotangent, wqkv, ada, wout, up, down, info, gain_one, gain_two, down_bias, ada_bias,
        up_bias, cosines, sines,
    )


def spread_kernel(
    seqs, folds,
    sum_ref, small_ref,
    ada_ref, qkv_ref, out_ref, up_ref, down_ref,
    ada_bias_ref, gain_one_ref, gain_two_ref, up_bias_ref, down_bias_ref,
    taken, wide, take_sem, give_sem,
):
    blocks, subs, _, width, _ = sum_ref.shape
    small = jnp.concatenate([small_ref[0], small_ref[1]], axis=1)
    order = list(range(blocks))
    takes = [pltpu.make_async_copy(sum_ref.at[n], taken.at[n], take_sem.at[n]) for n in order]
    for take in takes:
        take.start()
    cond = small[6 * seqs : 7 * seqs, : 3 * TEMB]
    for n in range(6):
        mod = small[n * seqs : (n + 1) * seqs, :]
        three = dot(mod, cond, ((0,), (0,)))
        ada_ref[n * width : (n + 1) * width, :] = (
            three[:, :TEMB] + three[:, TEMB : 2 * TEMB] + three[:, 2 * TEMB :]
        )
        ada_bias_ref[n * width : (n + 1) * width] = jnp.sum(mod.astype(F32), axis=0)
    rows = small[7 * seqs : 7 * seqs + 8 * (-(-(3 + folds) // 8)), :].astype(F32)
    gain_one_ref[...] = rows[0]
    gain_two_ref[...] = rows[1]
    down_bias_ref[...] = rows[2]
    for n in range(folds):
        up_bias_ref[n * width : (n + 1) * width] = rows[3 + n]

    gives = []
    for n in order:
        if n < 2 * folds:
            whole = pl.ds(n // 2 * width, width)
            place = up_ref.at[:, whole] if n % 2 else down_ref.at[whole]
        elif n == 2 * folds:
            place = out_ref
        else:
            place = qkv_ref.at[:, pl.ds((n - 2 * folds - 1) * width, width)]
        gives.append(pltpu.make_async_copy(wide.at[n], place, give_sem.at[n]))
        takes[n].wait()

        @pl.loop(0, width // 32)
        def _(r):
            lines = pl.ds(pl.multiple_of(r * 32, 32), 32)
            for m in range(subs):
                for half in range(2):
                    lanes = slice((2 * m + half) * 128, (2 * m + half + 1) * 128)
                    wide[n, lines, lanes] = taken[n, m, half, lines].astype(F32)

        gives[n].start()
    for give in gives:
        give.wait()


def spread(summed, small, seqs, folds):
    blocks, _, _, width, _ = summed.shape
    any_space = pl.BlockSpec(memory_space=pl.ANY)
    vmem = pl.BlockSpec(memory_space=pltpu.VMEM)
    shapes = [
        (6 * width, TEMB), (width, 3 * width), (width, width), (width, folds * width),
        (folds * width, width), (6 * width,), (width,), (width,), (folds * width,), (width,),
    ]
    return pl.pallas_call(
        functools.partial(spread_kernel, seqs, folds),
        in_specs=[any_space, vmem],
        out_specs=[vmem] + [any_space] * 4 + [vmem] * 5,
        out_shape=[jax.ShapeDtypeStruct(shape, F32) for shape in shapes],
        scratch_shapes=[
            pltpu.VMEM(summed.shape, BF),
            pltpu.VMEM((blocks, width, width), F32),
            DMA((blocks,)),
            DMA((blocks,)),
        ],
        compiler_params=pltpu.CompilerParams(vmem_limit_bytes=60 << 20),
        name="spread",
    )(summed, small)


def local(
    tokens, step_ids, prefix, keep_bits, ada_weight, ada_bias, norm1_gain, qkv_weight, out_weight,
    norm2_gain, up_weight, up_bias, down_weight, down_bias, cotangent,
):
    wide_size = lax.axis_size("wide")
    ring = lax.axis_size("narrow")
    groups, span, width = tokens.shape
    assert ring == 2 * groups and wide_size % 2 == 0
    length = ring * span
    hidden = up_weight.shape[1]
    folds = hidden // width
    seqs = wide_size * groups

    allowed = (jnp.arange(length, dtype=jnp.int32)[None, :] < prefix[:, None]) | (keep_bits == 1)
    info = jnp.concatenate(
        [jax.nn.silu(time_embed(step_ids)), jnp.where(allowed, 0.0, masked_score)], axis=1
    )
    cosines, sines = rope_tables(length)
    summed, small, outputs, input_grad = whole_block(
        tokens, cotangent, qkv_weight, ada_weight, out_weight, up_weight, down_weight, info,
        norm1_gain, norm2_gain, down_bias, ada_bias, up_bias, cosines, sines, wide_size, ring,
    )
    ada, qkv, out, up, down, ada_bias_grad, gain_one, gain_two, up_bias_grad, down_bias_grad = (
        spread(
            summed.reshape(-1, width // 256, 2, width, 128), small.reshape(2, -1, width // 2), seqs,
            folds,
        )
    )
    return (
        outputs, input_grad, ada, ada_bias_grad, gain_one, qkv, out, gain_two, up, up_bias_grad,
        down, down_bias_grad,
    )


def solution(mesh):
    split = P("wide", "narrow", None)
    in_specs = (
        (split, P("wide"), P("wide"), P("wide", None)) + (P(),) * 10 + (split,)
    )
    out_specs = (split, split) + (P(),) * 10
    return jax.shard_map(local, mesh=mesh, in_specs=in_specs, out_specs=out_specs, check_vma=False)
```

```python
import functools
import math

import jax
import jax.numpy as jnp
import numpy as np
from jax import lax
from jax.experimental import pallas as pl
from jax.experimental.pallas import tpu as pltpu
from jax.sharding import PartitionSpec as P

HEAD = 64
TEMB = 128
MESH = pl.DeviceIdType.MESH
BF = jnp.bfloat16
F32 = jnp.float32
DMA = pltpu.SemaphoreType.DMA

norm_epsilon = 1e-05
gelu_coeff = 0.7978845608028654
masked_score = -1e30
EARLY = (2, 6, 5, 5, 3)
LATE = (2, 4, 3)


def time_embed(step_ids):
    halfway = TEMB // 2
    frequency = jnp.exp(jnp.arange(halfway, dtype=F32) * (-math.log(10000.0) / halfway))
    angles = step_ids.astype(F32)[:, None] * frequency[None, :]
    return jnp.concatenate([jnp.cos(angles), jnp.sin(angles)], axis=-1)


def rope_tables(length):
    halfway = HEAD // 2
    inverse = 10000.0 ** (-2.0 * np.arange(halfway) / HEAD)
    angles = np.arange(length)[:, None] * inverse[None, :]
    sines = np.sin(angles)
    return (
        np.tile(np.cos(angles), (1, 4)).astype(np.float32),
        np.concatenate([-sines, sines, -sines, sines], axis=1).astype(np.float32),
    )


def dot(former, latter, dims):
    return lax.dot_general(former, latter, (dims, ((), ())), preferred_element_type=F32)


def rotate(values, cosines, sines, sign):
    lane = lax.broadcasted_iota(jnp.int32, (1, 128), 1)
    first = (lane % HEAD) < HEAD // 2
    parts = []
    for n in range(values.shape[1] // 128):
        part = values[:, n * 128 : (n + 1) * 128]
        partner = jnp.where(first, pltpu.roll(part, 128 - HEAD // 2, 1), pltpu.roll(part, HEAD // 2, 1))
        turned = partner * sines
        parts.append(part * cosines + (turned if sign > 0 else -turned))
    return parts[0] if len(parts) == 1 else jnp.concatenate(parts, axis=1)


def normed_rows(values):
    center = values - jnp.mean(values, axis=-1, keepdims=True)
    spread = jnp.mean(center * center, axis=-1, keepdims=True)
    scale = lax.rsqrt(spread + norm_epsilon)
    return center * scale, scale


def part_of(mod_ref, index, width):
    return mod_ref[:, index * width : (index + 1) * width]


def wide_of(block, copies):
    return jnp.concatenate([block] * copies, axis=1)


def block_kernel(
    groups, wide_size, ring, early_lags, late_lags,
    tok_ref, cot_ref, wqkv_ref, ada_ref, wout_ref, up_ref, down_ref,
    info_ref, gain_one_ref, gain_two_ref, down_bias_ref, ada_bias_ref, up_bias_ref, cos_ref,
    sin_ref,
    sum_ref, ssum_ref, tokens_ref, grad_ref,
    x_ref, dy_ref, h_ref, q_ref, ka_ref, va_ref, kb_ref, vb_ref, o_ref, ot_ref, lse_ref, mod_ref,
    ba_ref, bb_ref, cond_ref, table, par_ref, wout,
    weights, staging, dsmall, middle, branch, normed_low, normed_t, dm, total_a, total_b, active,
    slope, dq_t, deltas, vec, dup_bias, out_rows, dqkv, dk_in, dv_in,
    early_buffers, late_buffers, small_buffers,
    load_sem, weight_sem, take_self, info_send, info_recv, take_send, take_recv, swap_send,
    swap_recv, copy_sem, send_sem, recv_sem, ring_send, ring_recv, gather_send, gather_recv, kv_send, kv_recv, self_sem, row_send, row_recv,
):
    early, subs, pieces, piece_rows = early_buffers[0].shape[:4]
    late_count = late_buffers[0].shape[0]
    stages = staging.shape[0]
    outer = (wide_size // 2).bit_length() - 1
    count, width = x_ref.shape
    span = count // groups
    pairs = width // 128
    folds = up_ref.shape[1] // width
    wide = lax.axis_index("wide")
    chip = lax.axis_index("narrow")
    core = lax.rem(wide, 2)
    base = wide - core
    core_peer = (base + 1 - core, chip)
    dims = []
    for b in range(outer):
        bit = lax.rem(wide // (2 << b), 2)
        dims.append((bit, wide + (1 - 2 * bit) * (2 << b), chip))

    def load_up(i, slot):
        cols = pl.ds(pl.multiple_of(i * width, width), width)
        return pltpu.make_async_copy(up_ref.at[:, cols], weights.at[slot], weight_sem.at[slot])

    def load_down(i, slot):
        rows = pl.ds(pl.multiple_of(i * width, width), width)
        return pltpu.make_async_copy(down_ref.at[rows], weights.at[slot], weight_sem.at[slot])

    def load_qkv(n):
        cols = pl.ds(n * width, width)
        return pltpu.make_async_copy(wqkv_ref.at[:, cols], weights.at[n], weight_sem.at[n])

    load_ada = [
        pltpu.make_async_copy(
            ada_ref.at[pl.ds(n * width, width)],
            weights.at[3, :, pl.ds(n * TEMB, TEMB)],
            load_sem.at[1 + n],
        )
        for n in range(6)
    ]
    load_out = pltpu.make_async_copy(wout_ref, wout, load_sem.at[0])

    barrier = pltpu.get_barrier_semaphore()
    for d in dims[:outer]:
        pl.semaphore_signal(barrier, inc=1, device_id=d[1:], device_id_type=MESH)
    for c in range(2):
        for d in range(ring):
            if c or d:
                other = (base + lax.rem(core + c, 2), lax.rem(chip + d, ring))
                pl.semaphore_signal(barrier, inc=1, device_id=other, device_id_type=MESH)
    for load in load_ada:
        load.start()
    for n in range(3):
        load_qkv(n).start()
    load_out.start()
    pl.semaphore_wait(barrier, outer + 2 * ring - 1)

    slot = lax.rem(chip, groups)
    home = chip // groups
    rows_out = pl.ds(pl.multiple_of(slot * span, span), span)

    def move(src, dst, kind, g):
        remote = pltpu.make_async_remote_copy(
            src_ref=src.at[g],
            dst_ref=dst.at[rows_out],
            send_sem=take_send.at[kind, g],
            recv_sem=take_recv.at[kind, slot],
            device_id=(base + home, core * groups + g),
            device_id_type=MESH,
        )
        here = pltpu.make_async_copy(src.at[g], dst.at[rows_out], take_self.at[kind])
        own = (home == core) & (slot == g)
        return remote, here, own

    def send(src, dst, kind):
        for g in range(groups):
            remote, here, own = move(src, dst, kind, g)

            @pl.when(own)
            def _():
                here.start()

            @pl.when(jnp.logical_not(own))
            def _():
                remote.start()

    def sent(src, dst, kind):
        for g in range(groups):
            remote, here, own = move(src, dst, kind, g)

            @pl.when(jnp.logical_not(own))
            def _():
                remote.wait_send()

    def arrive(src, dst, kind, j):
        rows = pl.ds(j * span, span)
        own = (home == core) & (slot == j)

        @pl.when(own)
        def _():
            pltpu.make_async_copy(src.at[0], dst.at[rows], take_self.at[kind]).wait()

        @pl.when(jnp.logical_not(own))
        def _():
            pltpu.make_async_remote_copy(
                src_ref=src.at[0],
                dst_ref=dst.at[rows],
                send_sem=take_send.at[kind, 0],
                recv_sem=take_recv.at[kind, j],
                device_id=core_peer,
                device_id_type=MESH,
            ).wait_recv()

    send(tok_ref, x_ref, 0)
    par_ref[0:1, :] = gain_one_ref[...].reshape(1, width)
    par_ref[1:2, :] = gain_two_ref[...].reshape(1, width)
    par_ref[2:3, :] = down_bias_ref[...].reshape(1, width)
    for i in range(6):
        par_ref[3 + i : 4 + i, :] = ada_bias_ref[i * width : (i + 1) * width].reshape(1, width)
    for i in range(folds):
        par_ref[9 + i : 10 + i, :] = up_bias_ref[i * width : (i + 1) * width].reshape(1, width)
    table[core] = info_ref[...]
    swap_info = pltpu.make_async_remote_copy(
        src_ref=info_ref,
        dst_ref=table.at[core],
        send_sem=info_send,
        recv_sem=info_recv,
        device_id=core_peer,
        device_id_type=MESH,
    )
    swap_info.start()
    swap_info.wait()
    row = table[home, pl.ds(slot, 1), :]
    length = row.shape[1] - TEMB
    cond_ref[...] = row[:, :TEMB]
    bias = jnp.where(core == 0, row[:, TEMB : TEMB + count], row[:, TEMB + count : TEMB + length])
    ba_ref[...] = jnp.broadcast_to(bias, (128, count)).T
    bias = jnp.where(core == 1, row[:, TEMB : TEMB + count], row[:, TEMB + count : TEMB + length])
    bb_ref[...] = jnp.broadcast_to(bias, (128, count)).T

    cond = jnp.broadcast_to(row[:, :TEMB], (16, TEMB))
    high = cond.astype(BF).astype(F32)
    medium = (cond - high).astype(BF).astype(F32)
    low = cond - high - medium
    line = lax.broadcasted_iota(jnp.int32, (16, TEMB), 0)
    three = jnp.where(
        line == 0, high, jnp.where(line == 1, medium, jnp.where(line == 2, low, 0.0))
    ).astype(BF)
    for load in load_ada:
        load.wait()
    for i in range(6):
        cols = slice(i * width, (i + 1) * width)
        mod_ref[:, cols] = (
            jnp.sum(dot(three, weights[3, :, i * TEMB : (i + 1) * TEMB], ((1,), (1,))), axis=0, keepdims=True)
            + par_ref[3 + i : 4 + i, :]
        )
    shift = part_of(mod_ref, 0, width)
    scale = par_ref[0:1, :] * (1.0 + part_of(mod_ref, 1, width))

    for n in range(3):
        load_qkv(n).wait()
    swaps = []
    for j in range(groups):
        rows = pl.ds(j * span, span)
        arrive(tok_ref, x_ref, 0, j)
        if j == groups - 1:
            send(cot_ref, dy_ref, 1)
        normed, _ = normed_rows(x_ref[rows, :].astype(F32))
        h_ref[rows, :] = (normed * scale + shift).astype(BF)
        place = pl.ds(pl.multiple_of(core * count + j * span, span), span)
        cosines = cos_ref[place, :]
        sines = sin_ref[place, :]
        step = 256
        for n in (2, 1, 0):
            target = (q_ref, ka_ref, va_ref)[n]
            for m in range(width // step):
                cols = slice(m * step, (m + 1) * step)
                block = dot(h_ref[rows, :], weights[n, :, cols], ((1,), (0,)))
                if n < 2:
                    block = rotate(block, cosines, sines, 1)
                if n == 0:
                    block = block * HEAD**-0.5
                target[rows, m * step : (m + 1) * step] = block.astype(BF)
            if n > 0:
                swap = pltpu.make_async_remote_copy(
                    src_ref=target.at[rows],
                    dst_ref=(kb_ref, vb_ref)[n - 1].at[rows],
                    send_sem=swap_send.at[n - 1, j],
                    recv_sem=swap_recv.at[n - 1, j],
                    device_id=core_peer,
                    device_id_type=MESH,
                )
                swap.start()
                swaps.append(swap)
    for i in range(2):
        load_up(i, 2 * i).start()
        load_down(i, 2 * i + 1).start()
    for swap in swaps:
        swap.wait()

    copies = count // 128
    lane = lax.broadcasted_iota(jnp.int32, (1, 128), 1)

    @pl.loop(0, width // 128)
    def _(p):
        cols = pl.ds(pl.multiple_of(p * 128, 128), 128)
        q = q_ref[:, cols]
        ka = ka_ref[:, cols]
        kb = kb_ref[:, cols]
        va_t = va_ref[:, cols].T
        vb_t = vb_ref[:, cols].T
        outs = []
        for h in range(2):
            qm = jnp.where((lane // HEAD) == h, q, jnp.zeros_like(q))
            sa = dot(ka, qm, ((1,), (1,))) + wide_of(ba_ref[...], copies)
            sb = dot(kb, qm, ((1,), (1,))) + wide_of(bb_ref[...], copies)
            top = jnp.maximum(jnp.max(sa, axis=0, keepdims=True), jnp.max(sb, axis=0, keepdims=True))
            pa = jnp.exp(sa - top)
            pb = jnp.exp(sb - top)
            total = jnp.sum(pa, axis=0, keepdims=True) + jnp.sum(pb, axis=0, keepdims=True)
            part = slice(h * HEAD, (h + 1) * HEAD)
            out = dot(va_t[part], pa.astype(BF), ((1,), (0,))) + dot(
                vb_t[part], pb.astype(BF), ((1,), (0,))
            )
            outs.append(out / total)
            lse_ref[p, h : h + 1, :] = top + jnp.log(total)
        both = jnp.concatenate(outs, axis=0)
        ot_ref[cols, :] = both.astype(BF)
        o_ref[:, cols] = both.T.astype(BF)

    sent(tok_ref, x_ref, 0)
    for j in range(groups):
        arrive(cot_ref, dy_ref, 1, j)
    load_out.wait()

    parts = 8
    part_rows = span // parts

    def row_move(src, dst, kind, j, q):
        rows = pl.ds(pl.multiple_of(j * span + q * part_rows, part_rows), part_rows)
        place = dst.at[slot, pl.ds(pl.multiple_of(q * part_rows, part_rows), part_rows)]
        remote = pltpu.make_async_remote_copy(
            src_ref=src.at[rows],
            dst_ref=place,
            send_sem=row_send.at[kind, j, q],
            recv_sem=row_recv.at[kind, slot, q],
            device_id=(base + home, core * groups + j),
            device_id_type=MESH,
        )
        here = pltpu.make_async_copy(src.at[rows], place, self_sem.at[kind, q])
        own = (home == core) & (slot == j)
        return remote, here, own

    def row_send_part(src, dst, kind, q):
        for j in range(groups):
            remote, here, own = row_move(src, dst, kind, j, q)

            @pl.when(own)
            def _():
                here.start()

            @pl.when(jnp.logical_not(own))
            def _():
                remote.start()

    def row_wait_part(src, dst, kind, q):
        for j in range(groups):
            remote, here, own = row_move(src, dst, kind, j, q)

            @pl.when(own)
            def _():
                here.wait()

            @pl.when(jnp.logical_not(own))
            def _():
                remote.wait_send()

        rows = pl.ds(pl.multiple_of(q * part_rows, part_rows), part_rows)
        for g in range(groups):
            own = (home == core) & (slot == g)

            @pl.when(jnp.logical_not(own))
            def _():
                pltpu.make_async_remote_copy(
                    src_ref=src.at[rows],
                    dst_ref=dst.at[g, rows],
                    send_sem=row_send.at[kind, 0, q],
                    recv_sem=row_recv.at[kind, g, q],
                    device_id=core_peer,
                    device_id_type=MESH,
                ).wait_recv()

    last = 2 * outer + 4

    def stage(step, odd, sem, pick, source, out, total, core_slot, ring_slot, bit_slots):
        low = 0
        size = pieces
        steps = []
        for i in range(outer):
            (bit, peer_wide, _), (other_bit, other_wide, _) = dims[i], dims[outer - 1 - i]
            bit = bit + odd * (other_bit - bit)
            peer_wide = peer_wide + odd * (other_wide - peer_wide)
            size //= 2
            before = low
            low = low + bit * size
            steps.append((before + (1 - bit) * size, low, size, (peer_wide, chip)))
        final = low + chip

        def remote(src, dst, index, peer):
            return pltpu.make_async_remote_copy(
                src_ref=src,
                dst_ref=dst,
                send_sem=send_sem.at[index, sem],
                recv_sem=recv_sem.at[index, sem],
                device_id=peer,
                device_id_type=MESH,
            )

        def core_copy():
            return remote(source(1 - core), core_slot, 0, core_peer)

        def own_copy():
            return pltpu.make_async_copy(source(core), total, copy_sem.at[sem])

        def bit_copy(i):
            away, _, size, peer = steps[i]
            return remote(pick(total, away, size), bit_slots[i], 1 + i, peer)

        def ring_copies():
            copies = []
            for d in range(1, ring):
                target = lax.rem(chip + d, ring)
                copies.append(
                    pltpu.make_async_remote_copy(
                        src_ref=pick(total, low + target, 1),
                        dst_ref=ring_slot.at[d - 1],
                        send_sem=ring_send.at[d - 1, sem],
                        recv_sem=ring_recv.at[d - 1, sem],
                        device_id=(wide, target),
                        device_id_type=MESH,
                    )
                )
            return copies

        def gather_copies():
            return [
                pltpu.make_async_remote_copy(
                    src_ref=pick(total, final, 1),
                    dst_ref=pick(out(core), final, 1),
                    send_sem=gather_send.at[d - 1, sem],
                    recv_sem=gather_recv.at[d - 1, sem],
                    device_id=(wide, lax.rem(chip + d, ring)),
                    device_id_type=MESH,
                )
                for d in range(1, ring)
            ]

        def keep_copy():
            return pltpu.make_async_copy(
                pick(total, final, 1), pick(out(core), final, 1), copy_sem.at[sem]
            )

        def back_copy(i):
            _, keep, size, peer = steps[i]
            place = pick(out(core), keep, size)
            return remote(place, place, 1 + outer + i, peer)

        def core_back():
            return remote(out(core), out(core), 1 + 2 * outer, core_peer)

        def add(start, size, slot):
            place = pick(total, start, size)
            place[...] = place[...] + slot[...]

        if step == 0:
            core_copy().start()
            own_copy().start()
        elif step == 1:
            own_copy().wait()
            core_copy().wait()
            total[...] = total[...] + core_slot[...]
            bit_copy(0).start()
        elif step <= outer + 1:
            i = step - 2
            bit_copy(i).wait()
            add(steps[i][1], steps[i][2], bit_slots[i])
            if step <= outer:
                bit_copy(i + 1).start()
            else:
                for copy in ring_copies():
                    copy.start()
        elif step == outer + 2:
            for copy in ring_copies():
                copy.wait()
            place = pick(total, final, 1)
            value = place[...].astype(F32)
            for d in range(1, ring):
                value = value + ring_slot[d - 1].astype(F32)
            place[...] = value.astype(BF)
            keep_copy().start()
            for copy in gather_copies():
                copy.start()
        elif step == outer + 3:
            keep_copy().wait()
            for copy in gather_copies():
                copy.wait()
            back_copy(outer - 1).start()
        elif step <= 2 * outer + 2:
            i = 2 * outer + 2 - step
            back_copy(i + 1).wait()
            back_copy(i).start()
        elif step == 2 * outer + 3:
            back_copy(0).wait()
            core_back().start()
        else:
            core_back().wait()

    early_at = [2 + sum(early_lags[:step]) for step in range(last + 1)]
    late_at = [sum(late_lags[:step]) for step in range(last + 1)]
    per_group = pairs // subs
    turn = 2 * per_group + 2
    lead = 6 * folds + 3
    closing = lead + subs * turn

    def pick_early(ref, start, size):
        return ref.at[:, pl.ds(start, size)]

    def pick_late(ref, start, size):
        return ref.at[pl.ds(start, size)]

    def early_stage(step, chunk, odd):
        total, core_slots, ring_slots, bit_slots = early_buffers
        stage(
            step, odd, chunk, pick_early,
            lambda half: staging.at[chunk % stages, :, half],
            lambda half: sum_ref.at[chunk, :, half],
            total.at[chunk], core_slots.at[odd], ring_slots.at[chunk],
            [ref.at[chunk] for ref in bit_slots],
        )

    def late_stage(step, group, part):
        chunk = group * 3 + part
        total, core_slots, ring_slots, bit_slots = late_buffers
        stage(
            step, (group + part) % 2, early + chunk, pick_late,
            lambda half: staging.at[(early + part) % stages, group, half],
            lambda half: sum_ref.at[early + part, group, half],
            total.at[chunk], core_slots.at[chunk % core_slots.shape[0]],
            ring_slots.at[chunk], [ref.at[chunk] for ref in bit_slots],
        )

    def small_stage(step):
        stage(
            step, 0, early + late_count, pick_late,
            lambda half: dsmall.at[half], lambda half: ssum_ref.at[half], *small_buffers
        )

    def move_on(tick, turns, repeat, period):
        for step in range(last, -1, -1):
            since = tick - early_at[step]
            first = since // 3
            if since % 3 == 0 and first + (turns - 1) * period // 3 >= 0 and first < early:
                chunk = first + repeat * (period // 3)
                one = functools.partial(early_stage, step, chunk, first % 2)
                if first >= 0 and first + (turns - 1) * period // 3 < early:
                    one()
                else:
                    pl.when((chunk >= 0) & (chunk < early))(one)
        for step in range(last, -1, -1):
            for part in range(3):
                since = tick - (lead + 2 * per_group + part) - late_at[step]
                first = since // turn
                if since % turn == 0 and first + (turns - 1) * period // turn >= 0 and first < subs:
                    group = first + repeat * (period // turn)
                    one = functools.partial(late_stage, step, group, part)
                    if first >= 0 and first + (turns - 1) * period // turn < subs:
                        one()
                    else:
                        pl.when((group >= 0) & (group < subs))(one)
            if turns == 1 and tick == closing + 2 + late_at[step]:
                small_stage(step)

    def place_block(block, part, value):
        for half in range(2):
            lanes = slice(half * 128, (half + 1) * 128)
            for i in range(pieces):
                staging[lax.rem(block, stages), part, half, i] = value[
                    i * piece_rows : (i + 1) * piece_rows, lanes
                ]

    tile = min(256, count)
    tiles = [slice(r, r + tile) for r in range(0, count, tile)]
    gain_one = par_ref[0:1, :]
    gain_two = par_ref[1:2, :]
    shift_two, scale_two, gate_one, gate_two = (part_of(mod_ref, i, width) for i in (3, 4, 2, 5))

    def prepare():
        total = 0.0
        for rows in tiles:
            a = dot(o_ref[rows, :], wout[...], ((1,), (0,)))
            branch[rows, :] = a.astype(BF)
            x1 = x_ref[rows, :].astype(F32) + gate_one * a
            middle[rows, :] = x1
            normed, _ = normed_rows(x1)
            h2 = (normed * (gain_two * (1.0 + scale_two)) + shift_two).astype(BF)
            normed_low[rows, :] = h2
            normed_t[:, rows] = h2.T
            dm_rows = (dy_ref[rows, :].astype(F32) * gate_two).astype(BF)
            dm[rows, :] = dm_rows
            total = total + jnp.sum(dm_rows.astype(F32), axis=0, keepdims=True)
        vec[5:6, :] = total

    def hidden_units(i, rows):
        slot = 2 * lax.rem(i, 2)
        if rows is tiles[0]:
            load_up(i, slot).wait()
            load_down(i, slot + 1).wait()
        bias = par_ref[pl.ds(9 + i, 1), :]
        u = dot(normed_low[rows, :], weights[slot], ((1,), (0,))) + bias
        square = u * u
        tanh = jnp.tanh(gelu_coeff * (u + 0.044715 * u * square))
        g = (0.5 * u * (1.0 + tanh)).astype(BF)
        active[rows, :] = g
        slope[rows, :] = (
            0.5 * (1.0 + tanh)
            + (0.5 * gelu_coeff) * u * (1.0 - tanh * tanh) * (1.0 + (3 * 0.044715) * square)
        ).astype(BF)
        part = dot(g, weights[slot + 1], ((1,), (0,)))

        @pl.when(i == 0)
        def _():
            total_a[rows, :] = part

        @pl.when(i > 0)
        def _():
            total_a[rows, :] += part

    def down_grads(i):
        for m in range(0, width, 256):
            cols = slice(m, m + 256)
            place_block(
                2 * i, m // 256, dot(active[...], dm[:, cols], ((0,), (0,))).astype(BF)
            )

    def hidden_units_back(i, rows):
        slot = 2 * lax.rem(i, 2)
        dg = dot(dm[rows, :], weights[slot + 1], ((1,), (1,)))
        du = (dg * slope[rows, :].astype(F32)).astype(BF)
        active[rows, :] = du
        total = jnp.sum(du.astype(F32), axis=0, keepdims=True)
        part = dot(du, weights[slot], ((1,), (1,)))
        line = pl.ds(i, 1)
        if rows is tiles[0]:
            dup_bias[line, :] = total
        else:
            dup_bias[line, :] += total

        @pl.when(i == 0)
        def _():
            total_b[rows, :] = part

        @pl.when(i > 0)
        def _():
            total_b[rows, :] += part

    def up_grads(i):
        slot = 2 * lax.rem(i, 2)

        @pl.when(i + 2 < folds)
        def _():
            load_up(i + 2, slot).start()
            load_down(i + 2, slot + 1).start()

        @pl.when(i == folds - 1)
        def _():
            for n in range(3):
                load_qkv(n).start()

        for m in range(0, width, 256):
            cols = slice(m, m + 256)
            place_block(
                2 * i + 1, m // 256, dot(normed_t[...], active[:, cols], ((1,), (0,))).astype(BF)
            )

    def close_hidden_rows(rows):
        m = total_a[rows, :] + par_ref[2:3, :]
        x1 = middle[rows, :]
        out_rows[rows, :] = (x1 + gate_two * m).astype(BF)
        dy = dy_ref[rows, :].astype(F32)
        dh = total_b[rows, :]
        n2, rscale = normed_rows(x1)
        e = dh * ((1.0 + scale_two) * gain_two)
        dx1 = dy + rscale * (
            e
            - jnp.mean(e, axis=-1, keepdims=True)
            - n2 * jnp.mean(e * n2, axis=-1, keepdims=True)
        )
        middle[rows, :] = dx1
        da = (gate_one * dx1).astype(BF)
        normed_low[rows, :] = da
        for i, value in enumerate((dx1 * branch[rows, :].astype(F32), dh, dh * n2, dy * m)):
            total = jnp.sum(value, axis=0, keepdims=True)
            line = slice(i, i + 1)
            vec[line, :] = total if rows is tiles[0] else vec[line, :] + total
        active[rows, :] = dot(da, wout[...], ((1,), (1,))).astype(BF)

    def close_hidden(all_tiles):
        for rows in all_tiles:
            close_hidden_rows(rows)

    def out_grads():
        vec[4:5, :] = vec[2:3, :] * (1.0 + scale_two)
        vec[2:3, :] = vec[2:3, :] * gain_two
        for m in range(0, width, 256):
            cols = slice(m, m + 256)
            place_block(
                2 * folds, m // 256, dot(ot_ref[...], normed_low[:, cols], ((1,), (0,))).astype(BF)
            )

    place = pl.ds(pl.multiple_of(core * count, count), count)

    def kv_copies(p):
        cols = pl.ds(pl.multiple_of(p * 128, 128), 128)
        return [
            pltpu.make_async_remote_copy(
                src_ref=away.at[:, cols],
                dst_ref=landing.at[:, cols],
                send_sem=kv_send.at[i, p],
                recv_sem=kv_recv.at[i, p],
                device_id=core_peer,
                device_id_type=MESH,
            )
            for i, (away, landing) in enumerate(((normed_low, dk_in), (dm, dv_in)))
        ]

    def attention(p, side):
        cols = pl.ds(pl.multiple_of(p * 128, 128), 128)
        q = q_ref[:, cols]
        do = active[:, cols]
        if side == 0:
            prod = ot_ref[cols, :].astype(F32) * do.astype(F32).T
        k_ref, v_ref, b_ref, dk_ref, dv_ref = (
            (kb_ref, vb_ref, bb_ref, normed_low, dm),
            (ka_ref, va_ref, ba_ref, total_a, total_b),
        )[side]
        k = k_ref[:, cols]
        v = v_ref[:, cols]
        k_t = k.T
        dk = dv = None
        for h in range(2):
            picked = (lane // HEAD) == h
            part = slice(h * HEAD, (h + 1) * HEAD)
            qm = jnp.where(picked, q, jnp.zeros_like(q))
            dom = jnp.where(picked, do, jnp.zeros_like(do))
            if side == 0:
                deltas[h : h + 1, :] = jnp.sum(prod[part], axis=0, keepdims=True)
            delta = deltas[h : h + 1, :]
            s = dot(k, qm, ((1,), (1,))) + wide_of(b_ref[...], copies)
            prob = jnp.exp(s - lse_ref[p, h : h + 1, :])
            dv_h = dot(prob.astype(BF), dom, ((1,), (0,)))
            dprob = dot(v, dom, ((1,), (1,)))
            ds = (prob * (dprob - delta)).astype(BF)
            dk_h = dot(ds, qm, ((1,), (0,)))
            dq_h = dot(k_t[part], ds, ((1,), (0,)))
            dq_t[part, :] = dq_h if side == 0 else dq_t[part, :] + dq_h
            dk = dk_h if dk is None else dk + dk_h
            dv = dv_h if dv is None else dv + dv_h
        dk_ref[:, cols] = dk.astype(dk_ref.dtype)
        dv_ref[:, cols] = dv.astype(dv_ref.dtype)
        if side == 0:
            for copy in kv_copies(p):
                copy.start()
        else:
            dq = (dq_t[...] * (HEAD**-0.5)).T
            dqkv[:, cols] = rotate(dq, cos_ref[place, :], sin_ref[place, :], -1).astype(BF)

    def join(group):
        for i in range(pairs // subs):
            p = group * (pairs // subs) + i
            for copy in kv_copies(p):
                copy.wait()
            cols = pl.ds(pl.multiple_of(p * 128, 128), 128)
            dk = total_a[:, cols] + dk_in[:, cols].astype(F32)
            dv = total_b[:, cols] + dv_in[:, cols].astype(F32)
            k_cols = pl.ds(pl.multiple_of(width + p * 128, 128), 128)
            v_cols = pl.ds(pl.multiple_of(2 * width + p * 128, 128), 128)
            dqkv[:, k_cols] = rotate(dk, cos_ref[place, :], sin_ref[place, :], -1).astype(BF)
            dqkv[:, v_cols] = dv.astype(BF)

    def project_grads(group, n):
        cols = pl.ds(pl.multiple_of(n * width + group * 256, 256), 256)
        value = dot(normed_t[...], dqkv[:, cols], ((1,), (0,))).astype(BF)
        place_block(early + n, group, value)

    def finish(rows):
        if rows is tiles[0]:
            for n in range(3):
                load_qkv(n).wait()
        scale = 1.0 + part_of(mod_ref, 1, width)
        dh = sum(
            dot(dqkv[rows, n * width : (n + 1) * width], weights[n], ((1,), (1,)))
            for n in range(3)
        )
        n1, rscale = normed_rows(x_ref[rows, :].astype(F32))
        e = dh * (scale * gain_one)
        active[rows, :] = (
            middle[rows, :]
            + rscale
            * (
                e
                - jnp.mean(e, axis=-1, keepdims=True)
                - n1 * jnp.mean(e * n1, axis=-1, keepdims=True)
            )
        ).astype(BF)
        for i, value in enumerate((dh, dh * n1)):
            total = jnp.sum(value, axis=0, keepdims=True)
            line = slice(6 + i, 7 + i)
            vec[line, :] = total if rows is tiles[0] else vec[line, :] + total

    def small_grads():
        scale = 1.0 + part_of(mod_ref, 1, width)
        srows = dsmall.shape[2]
        seqs = wide_size * groups
        seq = (wide // 2) * ring + chip
        line = lax.broadcasted_iota(jnp.int32, (pieces * srows, width), 0)
        cond = jnp.where(core == 0, cond_ref[...], 0.0)
        high = cond.astype(BF).astype(F32)
        medium = (cond - high).astype(BF).astype(F32)
        filler = jnp.zeros((1, width - 3 * TEMB), F32)
        entries = [
            (seq, vec[6:7, :]),
            (seqs + seq, vec[7:8, :] * gain_one),
            (2 * seqs + seq, vec[0:1, :]),
            (3 * seqs + seq, vec[1:2, :]),
            (4 * seqs + seq, vec[2:3, :]),
            (5 * seqs + seq, vec[3:4, :]),
            (6 * seqs + seq, jnp.concatenate([high, medium, cond - high - medium, filler], axis=1)),
            (7 * seqs, vec[7:8, :] * scale),
            (7 * seqs + 1, vec[4:5, :]),
            (7 * seqs + 2, vec[5:6, :]),
        ] + [(7 * seqs + 3 + i, dup_bias[i : i + 1, :]) for i in range(folds)]
        value = jnp.zeros((pieces * srows, width), F32)
        for at, entry in entries:
            value = jnp.where(line == at, entry, value)
        for half in range(2):
            lanes = slice(half * (width // 2), (half + 1) * (width // 2))
            dsmall[half] = value[:, lanes].reshape(pieces, srows, width // 2).astype(BF)

    prepare()

    @pl.loop(0, folds)
    def _(i):
        for u in range(6):
            unit = (hidden_units, hidden_units_back)[u // 3]
            if u % 3 == 2:
                (down_grads, up_grads)[u // 3](i)
            else:
                for rows in tiles[u % 3 :: 2]:
                    unit(i, rows)
            move_on(u, folds, i, 6)

    close_hidden(tiles)
    move_on(lead - 3, 1, 0, 0)
    move_on(lead - 2, 1, 0, 0)
    out_grads()
    normed_t[...] = h_ref[...].T
    move_on(lead - 1, 1, 0, 0)

    @pl.loop(0, subs)
    def _(group):
        for u in range(turn):
            if u < 2 * per_group:
                attention(group * per_group + u // 2, u % 2)
            elif u == 2 * per_group:
                join(group)
                project_grads(group, 0)
            else:
                project_grads(group, 1)
                project_grads(group, 2)
            if u % 2 == 0:
                part = group * (turn // 2) + u // 2

                @pl.when(part < parts)
                def _():
                    row_send_part(out_rows, tokens_ref, 0, part)

            move_on(lead + u, subs, group, turn)

    for tick in range(closing, closing + 3 + late_at[-1]):
        if tick < closing + 2:
            for rows in tiles[tick - closing :: 2]:
                finish(rows)
        elif tick == closing + 2:
            small_grads()
        part = tick - closing - 2
        if part >= 0 and part % 3 == 0 and part // 3 < parts:
            row_send_part(active, grad_ref, 1, part // 3)
        move_on(tick, 1, 0, 0)

    sent(cot_ref, dy_ref, 1)

    @pl.loop(0, parts)
    def _(q):
        row_wait_part(out_rows, tokens_ref, 0, q)
        row_wait_part(active, grad_ref, 1, q)


def whole_block(
    tokens, cotangent, wqkv, ada, wout, up, down, info, gain_one, gain_two, down_bias, ada_bias,
    up_bias, cosines, sines, wide_size, ring,
):
    groups, span, width = tokens.shape
    count = groups * span
    pieces = wide_size // 2 * ring
    rows = width // pieces
    half = width // 2
    folds = up.shape[1] // width
    subs = width // 256
    early = 2 * folds + 1
    blocks = early + 3
    late = 3 * subs
    pairs = width // 128
    outer = (wide_size // 2).bit_length() - 1
    bits = EARLY[1:2] + EARLY[2:3] * (outer - 1)
    early_lags = EARLY[:1] + bits + EARLY[3:4] * 2 + bits[::-1] + EARLY[4:]
    late_lags = LATE[:1] + LATE[1:2] * (2 * outer + 2) + LATE[2:]
    assert subs * 256 == width and subs == 3 and sum(late_lags) > 16
    assert 26 + sum(early_lags) < 48 + sum(late_lags) and folds % 2 == 0
    seqs = wide_size * groups
    srows = -(-(seqs * 7 + 3 + folds) // (pieces * 8)) * 8
    sizes = [pieces >> (i + 1) for i in range(outer)]
    tail = (rows, 128)
    small = (srows, half)
    any_space = pl.BlockSpec(memory_space=pl.ANY)
    vmem = pl.BlockSpec(memory_space=pltpu.VMEM)
    block = jax.ShapeDtypeStruct((groups, span, width), BF)
    rows_low = pltpu.VMEM((count, width), BF)
    rows_full = pltpu.VMEM((count, width), F32)
    lanes = pltpu.VMEM((count, 128), F32)
    turned = pltpu.VMEM((width, count), BF)
    vectors = pltpu.VMEM((8, width), F32)
    return pl.pallas_call(
        functools.partial(block_kernel, groups, wide_size, ring, early_lags, late_lags),
        in_specs=[any_space] * 7 + [vmem] * 8,
        out_specs=[any_space] * 4,
        out_shape=[
            jax.ShapeDtypeStruct((blocks, subs, 2, pieces, rows, 128), BF),
            jax.ShapeDtypeStruct((2, pieces, srows, half), BF),
            block,
            block,
        ],
        scratch_shapes=[rows_low] * 9
        + [
            turned,
            pltpu.VMEM((pairs, 8, count), F32),
            pltpu.VMEM((1, 6 * width), F32),
            lanes,
            lanes,
            pltpu.VMEM((1, TEMB), F32),
            pltpu.VMEM((2,) + info.shape, F32),
            pltpu.VMEM((-(-(9 + folds) // 8) * 8, width), F32),
            pltpu.VMEM((width, width), BF),
            pltpu.VMEM((4, width, width), BF),
            pltpu.VMEM((4, subs, 2, pieces, rows, 128), BF),
            pltpu.VMEM((2, pieces, srows, half), BF),
            rows_full,
            rows_low,
            rows_low,
            turned,
            rows_low,
            rows_full,
            rows_full,
            rows_low,
            rows_low,
            pltpu.VMEM((128, count), F32),
            pltpu.VMEM((8, count), F32),
            vectors,
            vectors,
            rows_low,
            pltpu.VMEM((count, 3 * width), BF),
            rows_low,
            rows_low,
            [
                pltpu.VMEM((early, subs, pieces) + tail, BF),
                pltpu.VMEM((2, subs, pieces) + tail, BF),
                pltpu.VMEM((early, ring - 1, subs, 1) + tail, BF),
                [pltpu.VMEM((early, subs, n) + tail, BF) for n in sizes],
            ],
            [
                pltpu.VMEM((late, pieces) + tail, BF),
                pltpu.VMEM((2 * LATE[0] + 1, pieces) + tail, BF),
                pltpu.VMEM((late, ring - 1, 1) + tail, BF),
                [pltpu.VMEM((late, n) + tail, BF) for n in sizes],
            ],
            [
                pltpu.VMEM((pieces,) + small, BF),
                pltpu.VMEM((pieces,) + small, BF),
                pltpu.VMEM((ring - 1, 1) + small, BF),
                [pltpu.VMEM((n,) + small, BF) for n in sizes],
            ],
            DMA((7,)),
            DMA((4,)),
            DMA((2,)),
            DMA,
            DMA,
            DMA((2, groups)),
            DMA((2, groups)),
            DMA((2, groups)),
            DMA((2, groups)),
            DMA((early + late + 1,)),
            DMA((2 + 2 * outer, early + late + 1)),
            DMA((2 + 2 * outer, early + late + 1)),
            DMA((ring - 1, early + late + 1)),
            DMA((ring - 1, early + late + 1)),
            DMA((ring - 1, early + late + 1)),
            DMA((ring - 1, early + late + 1)),
            DMA((2, pairs)),
            DMA((2, pairs)),
            DMA((2, 8)),
            DMA((2, groups, 8)),
            DMA((2, groups, 8)),
        ],
        compiler_params=pltpu.CompilerParams(
            collective_id=0, has_side_effects=True, vmem_limit_bytes=63 << 20
        ),
        name="whole_block",
    )(
        tokens, cotangent, wqkv, ada, wout, up, down, info, gain_one, gain_two, down_bias, ada_bias,
        up_bias, cosines, sines,
    )


def spread_kernel(
    seqs, folds,
    sum_ref, small_ref,
    ada_ref, qkv_ref, out_ref, up_ref, down_ref,
    ada_bias_ref, gain_one_ref, gain_two_ref, up_bias_ref, down_bias_ref,
    taken, wide, take_sem, give_sem,
):
    blocks, subs, _, width, _ = sum_ref.shape
    small = jnp.concatenate([small_ref[0], small_ref[1]], axis=1)
    order = list(range(blocks))
    takes = [pltpu.make_async_copy(sum_ref.at[n], taken.at[n], take_sem.at[n]) for n in order]
    for take in takes:
        take.start()
    cond = small[6 * seqs : 7 * seqs, : 3 * TEMB]
    for n in range(6):
        mod = small[n * seqs : (n + 1) * seqs, :]
        three = dot(mod, cond, ((0,), (0,)))
        ada_ref[n * width : (n + 1) * width, :] = (
            three[:, :TEMB] + three[:, TEMB : 2 * TEMB] + three[:, 2 * TEMB :]
        )
        ada_bias_ref[n * width : (n + 1) * width] = jnp.sum(mod.astype(F32), axis=0)
    rows = small[7 * seqs : 7 * seqs + 8 * (-(-(3 + folds) // 8)), :].astype(F32)
    gain_one_ref[...] = rows[0]
    gain_two_ref[...] = rows[1]
    down_bias_ref[...] = rows[2]
    for n in range(folds):
        up_bias_ref[n * width : (n + 1) * width] = rows[3 + n]

    gives = []
    for n in order:
        if n < 2 * folds:
            whole = pl.ds(n // 2 * width, width)
            place = up_ref.at[:, whole] if n % 2 else down_ref.at[whole]
        elif n == 2 * folds:
            place = out_ref
        else:
            place = qkv_ref.at[:, pl.ds((n - 2 * folds - 1) * width, width)]
        gives.append(pltpu.make_async_copy(wide.at[n], place, give_sem.at[n]))
        takes[n].wait()

        @pl.loop(0, width // 32)
        def _(r):
            lines = pl.ds(pl.multiple_of(r * 32, 32), 32)
            for m in range(subs):
                for half in range(2):
                    lanes = slice((2 * m + half) * 128, (2 * m + half + 1) * 128)
                    wide[n, lines, lanes] = taken[n, m, half, lines].astype(F32)

        gives[n].start()
    for give in gives:
        give.wait()


def spread(summed, small, seqs, folds):
    blocks, _, _, width, _ = summed.shape
    any_space = pl.BlockSpec(memory_space=pl.ANY)
    vmem = pl.BlockSpec(memory_space=pltpu.VMEM)
    shapes = [
        (6 * width, TEMB), (width, 3 * width), (width, width), (width, folds * width),
        (folds * width, width), (6 * width,), (width,), (width,), (folds * width,), (width,),
    ]
    return pl.pallas_call(
        functools.partial(spread_kernel, seqs, folds),
        in_specs=[any_space, vmem],
        out_specs=[vmem] + [any_space] * 4 + [vmem] * 5,
        out_shape=[jax.ShapeDtypeStruct(shape, F32) for shape in shapes],
        scratch_shapes=[
            pltpu.VMEM(summed.shape, BF),
            pltpu.VMEM((blocks, width, width), F32),
            DMA((blocks,)),
            DMA((blocks,)),
        ],
        compiler_params=pltpu.CompilerParams(vmem_limit_bytes=60 << 20),
        name="spread",
    )(summed, small)


def local(
    tokens, step_ids, prefix, keep_bits, ada_weight, ada_bias, norm1_gain, qkv_weight, out_weight,
    norm2_gain, up_weight, up_bias, down_weight, down_bias, cotangent,
):
    wide_size = lax.axis_size("wide")
    ring = lax.axis_size("narrow")
    groups, span, width = tokens.shape
    assert ring == 2 * groups and wide_size % 2 == 0
    length = ring * span
    hidden = up_weight.shape[1]
    folds = hidden // width
    seqs = wide_size * groups

    allowed = (jnp.arange(length, dtype=jnp.int32)[None, :] < prefix[:, None]) | (keep_bits == 1)
    info = jnp.concatenate(
        [jax.nn.silu(time_embed(step_ids)), jnp.where(allowed, 0.0, masked_score)], axis=1
    )
    cosines, sines = rope_tables(length)
    summed, small, outputs, input_grad = whole_block(
        tokens, cotangent, qkv_weight, ada_weight, out_weight, up_weight, down_weight, info,
        norm1_gain, norm2_gain, down_bias, ada_bias, up_bias, cosines, sines, wide_size, ring,
    )
    ada, qkv, out, up, down, ada_bias_grad, gain_one, gain_two, up_bias_grad, down_bias_grad = (
        spread(
            summed.reshape(-1, width // 256, 2, width, 128), small.reshape(2, -1, width // 2), seqs,
            folds,
        )
    )
    return (
        outputs, input_grad, ada, ada_bias_grad, gain_one, qkv, out, gain_two, up, up_bias_grad,
        down, down_bias_grad,
    )


def solution(mesh):
    split = P("wide", "narrow", None)
    in_specs = (
        (split, P("wide"), P("wide"), P("wide", None)) + (P(),) * 10 + (split,)
    )
    out_specs = (split, split) + (P(),) * 10
    return jax.shard_map(local, mesh=mesh, in_specs=in_specs, out_specs=out_specs, check_vma=False)
```
